256 devices in a mesh: comp: 2 (over x_lo), face: 128 (over y, z, x_hi, core).
Axes of the slice: x: 4 (x_hi: 2, x_lo: 2; x = x_hi * 2 + x_lo), y: 4, z: 8, core: 2. Of those that a mesh axis runs over, the one named last changes fastest.
Arguments:
- state: bfloat16 [2, 16, 32768], P('comp', None, 'face'), may hold values from -6 to 6
- cotangent: bfloat16 [2, 16, 32768], P('comp', None, 'face'), may hold values from -6 to 6
- land_sea: int32 [32768], P('face'), may hold values 0 or 1
- turn_table: int32 [128, 4], replicated, may hold values from 0 to 3
- first_kernel: bfloat16 [2, 216, 256], P('comp'), may hold values from -0.625 to 0.625
- mid_kernel: bfloat16 [2, 2304, 256], P('comp'), may hold values from -0.1875 to 0.1875
- out_kernel: bfloat16 [2, 2304, 16], P('comp'), may hold values from -0.1875 to 0.1875
- first_gates: int32 [2, 216, 64], P('comp'), may hold values from 0 to 5
- mid_gates: int32 [2, 2304, 64], P('comp'), may hold values from 0 to 5
- out_gates: int32 [2, 2304, 4], P('comp'), may hold values from 0 to 5
Outputs:
- upcoming_climate_estimate: bfloat16 [2, 16, 32768], P('comp', None, 'face')
- condition_adjoint_grid: float32 [2, 16, 32768], P('comp', None, 'face')
- opening_filter_adjoint: float32 [2, 216, 256], P('comp')
- central_filter_adjoint: float32 [2, 589824], P('comp', 'face')
- closing_filter_adjoint: float32 [2, 36864], P('comp', 'face')
The draws below stay inside these ranges and needn't reach their ends.
Inputs may be any that keep to these rules, and one draw needn't show every extreme that they name: `mid_gates`: a gate value picks one of the six ways of keeping 2 of 4 consecutive output channels. `first_gates`: a gate value picks one of the six ways of keeping 2 of 4 consecutive output channels. `out_gates`: a gate value picks one of the six ways of keeping 2 of 4 consecutive output channels.
All inputs are finite; a program needn't handle non-finite values. No bound on the sum of `land_sea` on one device may be relied on, other than what follows from the above.
Results may differ from the reference program's by a relative error of at most 0.0052.
Values may be sent and summed in bfloat16 or wider, within the bound.
No kernel may reach another device: no remote copies, remote signals or barrier semaphores. Data moves between devices by JAX's collectives and lax.ppermute only.
A program may use at most 64 MiB of HBM per device.

```python
from functools import partial
import jax
import jax.numpy as jnp
from jax import lax

FIELDS = 16
COUPLED = 8
HIDDEN_SIZE = 256
ROW_TILES = 4
TS = 16
IN_CH = 24
CELLS = 256
TILES = 128


def touch_ends(result, key, smallest, largest):
    index_at = [jax.random.randint(jax.random.fold_in(key, axis), (), 0, length) for axis, length in enumerate(result.shape)]
    longest = result.shape.index(max(result.shape))
    neighbour = index_at[:longest] + [(index_at[longest] + 1) % result.shape[longest]] + index_at[longest + 1:]
    return result.at[tuple(index_at)].set(smallest).at[tuple(neighbour)].set(largest)


def block_levels(key, dims, pieces, low, high):
    factor_of = 1.0
    for axis_at, blocks in pieces:
        heights = jax.random.uniform(jax.random.fold_in(jax.random.fold_in(key, 6), axis_at), (blocks,), jnp.float32, low / len(pieces), high / len(pieces))
        factor_of = factor_of * jnp.repeat(jnp.exp(heights), dims[axis_at] // blocks).reshape((-1,) + (1,) * (len(dims) - 1 - axis_at))
    return factor_of


def gaussian(key, shape, scale, most, pieces=(), kind=jnp.bfloat16):
    values = jax.random.normal(key, shape, jnp.float32) * scale
    if len(pieces) > 0:
        values = block_levels(key, shape, pieces, -0.22, 0.18) * values
    return jnp.clip(values, min=-most, max=most).astype(kind)


def setup_inputs(seed: int = 0) -> dict:
    streams_of = jax.random.split(jax.random.key(seed), 11)
    return {
        "state": gaussian(streams_of[0], (2, FIELDS, TILES * CELLS), 1.0, 6.0, ((0, 2), (2, 128))),
        "cotangent": gaussian(streams_of[1], (2, FIELDS, TILES * CELLS), 1.0, 6.0, ((0, 2), (2, 128))),
        "land_sea": touch_ends((jax.random.randint(streams_of[2], (TILES * CELLS,), 0, 3) < 2).astype(jnp.int32), jax.random.fold_in(streams_of[2], 1), 0, 1),
        "turn_table": touch_ends(jax.random.randint(streams_of[3], (TILES, 4), 0, 4), jax.random.fold_in(streams_of[3], 1), 0, 3).astype(jnp.int32),
        "first_kernel": gaussian(streams_of[4], (2, 9 * IN_CH, HIDDEN_SIZE), (9 * IN_CH // 2) ** -0.5, 0.625, ((0, 2),)),
        "mid_kernel": gaussian(streams_of[5], (2, 9 * HIDDEN_SIZE, HIDDEN_SIZE), (9 * HIDDEN_SIZE // 2) ** -0.5, 0.1875, ((0, 2),)),
        "out_kernel": gaussian(streams_of[6], (2, 9 * HIDDEN_SIZE, FIELDS), (9 * HIDDEN_SIZE // 2) ** -0.5, 0.1875, ((0, 2),)),
        "first_gates": touch_ends(jax.random.randint(streams_of[7], (2, 9 * IN_CH, HIDDEN_SIZE // 4), 0, 6), jax.random.fold_in(streams_of[7], 1), 0, 5).astype(jnp.int32),
        "mid_gates": touch_ends(jax.random.randint(streams_of[8], (2, 9 * HIDDEN_SIZE, HIDDEN_SIZE // 4), 0, 6), jax.random.fold_in(streams_of[8], 1), 0, 5).astype(jnp.int32),
        "out_gates": touch_ends(jax.random.randint(streams_of[9], (2, 9 * HIDDEN_SIZE, FIELDS // 4), 0, 6), jax.random.fold_in(streams_of[9], 1), 0, 5).astype(jnp.int32),
    }


def gate_pair(gates):
    low = (gates >= 3).astype(jnp.int32) + (gates >= 5).astype(jnp.int32)
    high = jnp.where(gates == 0, 1, jnp.where((gates == 1) | (gates == 3), 2, 3)).astype(jnp.int32)
    return (low, high)

def gate_keep(gates):
    low, high = gate_pair(gates)
    lanes = jnp.arange(4, dtype=jnp.int32)
    keep = (low[..., None] == lanes) | (high[..., None] == lanes)
    return keep.reshape(gates.shape[0], gates.shape[1] * 4)

def edge_of(square, side):
    if side == 0:
        return square[:, :, -1]
    if side == 1:
        return square[:, :, 0]
    if side == 2:
        return square[:, -1, :]
    return square[:, 0, :]

def turned_edge(square, turns, side):
    return edge_of(jnp.rot90(square, turns, axes=(1, 2)), side)

def take_edge(square, turn, side):
    return lax.switch(turn, [partial(turned_edge, turns=j, side=side) for j in range(4)], square)

def pad_all(tiles, turn_table):
    shifts = (1, -1, ROW_TILES, -ROW_TILES)
    strips = [jax.vmap(partial(take_edge, side=side))(jnp.roll(tiles, shifts[side], 0), turn_table[:, side]) for side in range(4)]
    padded = jnp.pad(tiles, ((0, 0), (0, 0), (1, 1), (1, 1)))
    padded = padded.at[:, :, 1:-1, 0].set(strips[0])
    padded = padded.at[:, :, 1:-1, -1].set(strips[1])
    padded = padded.at[:, :, 0, 1:-1].set(strips[2])
    padded = padded.at[:, :, -1, 1:-1].set(strips[3])
    return padded

def unfold(padded, breadth_count):
    feature_depth = padded.shape[0]
    return jnp.concatenate([padded[:, vertical_place:vertical_place + breadth_count, horizontal_place:horizontal_place + breadth_count].reshape(feature_depth, breadth_count * breadth_count) for vertical_place in range(3) for horizontal_place in range(3)], 0)

def fold(columns, feature_depth, breadth_count):
    prognosis_outcome = jnp.zeros((feature_depth, breadth_count + 2, breadth_count + 2), jnp.float32)
    index = 0
    for vertical_place in range(3):
        for horizontal_place in range(3):
            square_piece = columns[index * feature_depth:(index + 1) * feature_depth].reshape(feature_depth, breadth_count, breadth_count)
            prognosis_outcome = prognosis_outcome.at[:, vertical_place:vertical_place + breadth_count, horizontal_place:horizontal_place + breadth_count].add(square_piece)
            index = index + 1
    return prognosis_outcome

def correlate_everything(padded, kernel):

    def one_tile(square):
        return lax.dot_general(kernel, unfold(square, TS), (((0,), (0,)), ((), ())), preferred_element_type=jnp.float32)
    return lax.map(one_tile, padded)

def back_all(padded, grads, kernel):
    feature_depth = padded.shape[1]

    def step(total, pair):
        square, grad = pair
        columns = unfold(square, TS)
        total = total + lax.dot_general(columns, grad, (((1,), (1,)), ((), ())), preferred_element_type=jnp.float32)
        back = jnp.dot(kernel, grad, preferred_element_type=jnp.float32)
        return (total, fold(back, feature_depth, TS))
    start = jnp.zeros((kernel.shape[0], kernel.shape[1]), jnp.float32)
    return lax.scan(step, start, (padded, grads))

def slope(values):
    sig = jax.nn.sigmoid(values)
    return sig * (1.0 + values * (1.0 - sig))

def reference(state, cotangent, land_sea, turn_table, first_kernel, mid_kernel, out_kernel, first_gates, mid_gates, out_gates):
    cells = TS * TS
    sea = land_sea.astype(jnp.float32).reshape(TILES, 1, cells)

    def as_tiles(flat):
        feature_depth = flat.shape[0]
        return flat.reshape(feature_depth, TILES, cells).transpose(1, 0, 2)

    def linear_layout(tiles):
        return tiles.transpose(1, 0, 2).reshape(tiles.shape[1], TILES * cells)

    def squares(tiles):
        return tiles.reshape(TILES, tiles.shape[1], TS, TS)

    def unpad(dpad):
        zero_tiles = jnp.zeros((TILES, dpad.shape[1], TS, TS), jnp.float32)
        _, pull = jax.vjp(lambda tiles: pad_all(tiles, turn_table), zero_tiles)
        return pull(dpad)[0].reshape(TILES, dpad.shape[1], cells)

    def component(comp):
        local_region_quantity = state[comp]
        partner = state[1 - comp][:COUPLED]
        inputs = jnp.concatenate([local_region_quantity, partner], 0)
        opening_keep = gate_keep(first_gates[comp])
        central_keep = gate_keep(mid_gates[comp])
        closing_keep = gate_keep(out_gates[comp])
        kernel_first = jnp.where(opening_keep, first_kernel[comp], jnp.zeros((), jnp.bfloat16))
        kernel_mid = jnp.where(central_keep, mid_kernel[comp], jnp.zeros((), jnp.bfloat16))
        stencil_produced = jnp.where(closing_keep, out_kernel[comp], jnp.zeros((), jnp.bfloat16))
        pad_zero = pad_all(squares(as_tiles(inputs)), turn_table)
        act_one = correlate_everything(pad_zero, kernel_first)
        hid_one = jax.nn.silu(act_one).astype(jnp.bfloat16)
        pad_one = pad_all(squares(hid_one), turn_table)
        act_two = correlate_everything(pad_one, kernel_mid)
        hid_two = jax.nn.silu(act_two).astype(jnp.bfloat16)
        border_fill_two = pad_all(squares(hid_two), turn_table)
        prognosis_outcome = correlate_everything(border_fill_two, stencil_produced)
        if comp == 1:
            scaling_ratio = sea
        else:
            scaling_ratio = jnp.ones_like(sea)
        local_face_stripes = as_tiles(local_region_quantity)
        upcoming_climate_estimate = (local_face_stripes.astype(jnp.float32) + scaling_ratio * prognosis_outcome).astype(jnp.bfloat16)
        cot_tiles = as_tiles(cotangent[comp]).astype(jnp.float32)
        grad_three = (scaling_ratio * cot_tiles).astype(jnp.bfloat16)
        closing_accumulated, dpad_two = back_all(border_fill_two, grad_three, stencil_produced)
        grad_hid_two = unpad(dpad_two)
        grad_two = (grad_hid_two * slope(act_two)).astype(jnp.bfloat16)
        central_accumulated, dpad_one = back_all(pad_one, grad_two, kernel_mid)
        grad_hid_one = unpad(dpad_one)
        grad_one = (grad_hid_one * slope(act_one)).astype(jnp.bfloat16)
        opening_accumulated, dpad_zero = back_all(pad_zero, grad_one, kernel_first)
        grad_inputs = unpad(dpad_zero)
        own_domain_adjoint = cot_tiles + grad_inputs[:, :FIELDS]
        partner_domain_adjoint = grad_inputs[:, FIELDS:]
        zero_float = jnp.zeros((), jnp.float32)
        return (linear_layout(upcoming_climate_estimate), own_domain_adjoint, partner_domain_adjoint, jnp.where(opening_keep, opening_accumulated, zero_float), jnp.where(central_keep, central_accumulated, zero_float), jnp.where(closing_keep, closing_accumulated, zero_float))
    air_component_slice = component(0)
    marine_component_slice = component(1)
    atmos_grad = air_component_slice[1].at[:, :COUPLED].add(marine_component_slice[2])
    ocean_grad = marine_component_slice[1].at[:, :COUPLED].add(air_component_slice[2])
    upcoming_climate_estimate = jnp.stack([air_component_slice[0], marine_component_slice[0]], 0)
    condition_adjoint_grid = jnp.stack([linear_layout(atmos_grad), linear_layout(ocean_grad)], 0)
    opening_filter_adjoint = jnp.stack([air_component_slice[3], marine_component_slice[3]], 0)
    central_filter_adjoint = jnp.stack([air_component_slice[4].reshape(-1), marine_component_slice[4].reshape(-1)], 0)
    closing_filter_adjoint = jnp.stack([air_component_slice[5].reshape(-1), marine_component_slice[5].reshape(-1)], 0)
    return (upcoming_climate_estimate, condition_adjoint_grid, opening_filter_adjoint, central_filter_adjoint, closing_filter_adjoint)
```

```python
import functools

import jax
import jax.numpy as jnp
import numpy as np
from jax import lax
from jax.experimental import pallas as pl
from jax.experimental.pallas import tpu as pltpu
from jax.sharding import Mesh, PartitionSpec as P

FIELDS = 16
COUPLED = 8
TS = 16
CELLS = TS * TS
ROW = 4
ROWS = 32
TILES = ROW * ROWS
LINE = ROW * CELLS
HID = 256
PADC = 128
CHUNK = 24
BF = jnp.bfloat16
F32 = jnp.float32

FACE = ("y", "z", "xh", "core")
ROW_AXES = ("y", "z")
LINE_AXES = ("comp", "xh", "core")

EDGE_MAP = (
    ((0, False), (2, True), (1, True), (3, False)),
    ((1, False), (3, True), (0, True), (2, False)),
    ((2, False), (1, False), (3, True), (0, True)),
    ((3, False), (0, False), (2, True), (1, True)),
)

STRIPS = (
    [(col, 2, 8 + col) for col in range(4)]
    + [(3, 0, 8)]
    + [(col, 3, col) for col in range(4)]
    + [(0, 1, 3)]
    + [(col - 1, 0, 4 + col) for col in (1, 2, 3)]
    + [(col + 1, 1, 4 + col) for col in (0, 1, 2)]
)


def edge_cells(slot, flip):
    along = np.arange(TS)
    if flip:
        along = along[::-1]
    if slot == 0:
        return along * TS + TS - 1
    if slot == 1:
        return along * TS
    if slot == 2:
        return (TS - 1) * TS + along
    return along


STRIP_CELLS = np.stack(
    [
        np.stack([source * CELLS + edge_cells(*EDGE_MAP[side][turn]) for turn in range(4)])
        for source, side, _ in STRIPS
    ]
).astype(np.int32)
STRIP_PICK = np.zeros((len(STRIPS), 12, 4), np.int32)
for number, (_, side, reader) in enumerate(STRIPS):
    STRIP_PICK[number, reader, side] = 1


def strip_index(turn_table, row):
    around = jnp.concatenate([turn_table[-ROW:], turn_table, turn_table[:ROW]], 0)
    window = lax.dynamic_slice(around, (ROW * row, 0), (3 * ROW, 4))
    turns = jnp.sum(STRIP_PICK * window[None], (1, 2))
    hit = turns[:, None] == jnp.arange(4, dtype=jnp.int32)[None]
    return jnp.sum(jnp.where(hit[:, :, None], STRIP_CELLS, 0), 1).reshape(-1)


def dot(left, right):
    return jnp.dot(left, right, preferred_element_type=F32)


def dot_nt(left, right):
    return lax.dot_general(left, right, (((1,), (1,)), ((), ())), preferred_element_type=F32)


def one_hot(shape, axis, index):
    return (lax.broadcasted_iota(jnp.int32, shape, axis) == index).astype(F32).astype(BF)


def edge_spread(column):
    rows = lax.broadcasted_iota(jnp.int32, (CELLS, TS), 0)
    cols = lax.broadcasted_iota(jnp.int32, (CELLS, TS), 1)
    return (rows == cols * TS + column).astype(F32).astype(BF)


def edge_take(column):
    rows = lax.broadcasted_iota(jnp.int32, (TS, CELLS), 0)
    cols = lax.broadcasted_iota(jnp.int32, (TS, CELLS), 1)
    return (cols == rows * TS + column).astype(F32).astype(BF)


def shift_cells(value, step, axis):
    along = lax.broadcasted_iota(jnp.int32, value.shape, axis)
    moved = pltpu.roll(value, step % TS, axis)
    edge = 0 if step == 1 else TS - 1
    return jnp.where(along == edge, 0.0, moved)


def fill(out_ref, tiles, local, from_prev, from_next):
    depth = tiles.shape[1]
    spread_west, spread_east = edge_spread(0), edge_spread(TS - 1)
    for col in range(ROW):
        south = from_prev[TS * col : TS * (col + 1)]
        north = from_next[TS * col : TS * (col + 1)]
        west = from_prev[4 * TS : 5 * TS] if col == 0 else local[TS * (col - 1) : TS * col]
        east = from_next[4 * TS : 5 * TS] if col == 3 else local[TS * (3 + col) : TS * (4 + col)]
        own = tiles[CELLS * col : CELLS * (col + 1)]
        wide = own.astype(F32).reshape(TS, TS, depth)
        left = shift_cells(wide, 1, 1) + dot(spread_west, west).reshape(TS, TS, depth)
        right = shift_cells(wide, -1, 1) + dot(spread_east, east).reshape(TS, TS, depth)
        out_ref[col, 1 : TS + 1, :, 0:depth] = left.astype(BF)
        out_ref[col, 1 : TS + 1, :, depth : 2 * depth] = own.reshape(TS, TS, depth)
        out_ref[col, 1 : TS + 1, :, 2 * depth : 3 * depth] = right.astype(BF)
        for line, strip in ((0, south), (TS + 1, north)):
            wide = strip.astype(F32)
            out_ref[col, line, :, 0:depth] = shift_cells(wide, 1, 0).astype(BF)
            out_ref[col, line, :, depth : 2 * depth] = strip
            out_ref[col, line, :, 2 * depth : 3 * depth] = shift_cells(wide, -1, 0).astype(BF)


def conv_tile(filled_ref, weights_ref, col):
    width = filled_ref.shape[3]
    total = None
    for a in range(3):
        piece = dot(filled_ref[col, a : a + TS].reshape(CELLS, width), weights_ref[a])
        total = piece if total is None else total + piece
    return total


def fold_tile(grad, weights_ref, pad_ref):
    deep = grad.shape[1]
    lines = grad.reshape(TS, TS, deep)
    pad_ref[...] = jnp.zeros_like(pad_ref)
    for a in range(3):
        pad_ref[a : a + TS, :, deep * a : deep * (a + 1)] = lines
    total = dot(pad_ref[...].reshape((TS + 2) * TS, 3 * deep), weights_ref[...])
    depth = total.shape[1] // 3
    total = total.reshape(TS + 2, TS, 3 * depth)
    left, mid, right = (total[:, :, depth * b : depth * (b + 1)] for b in range(3))
    merged = mid + shift_cells(left, -1, 1) + shift_cells(right, 1, 1)
    inner = merged[1 : TS + 1].reshape(CELLS, depth)
    south = merged[0].astype(BF)
    north = merged[TS + 1].astype(BF)
    west = dot(edge_take(0), left[1 : TS + 1].reshape(CELLS, depth).astype(BF)).astype(BF)
    east = dot(edge_take(TS - 1), right[1 : TS + 1].reshape(CELLS, depth).astype(BF)).astype(BF)
    return inner, south, north, west, east


def fold_row(grad_of, weights_ref, pad_ref, inner_ref, prev_ref, next_ref, local_ref):
    for col in range(ROW):
        inner, south, north, west, east = fold_tile(grad_of(col), weights_ref, pad_ref)
        inner_ref[CELLS * col : CELLS * (col + 1)] = inner
        prev_ref[TS * col : TS * (col + 1)] = south
        next_ref[TS * col : TS * (col + 1)] = north
        if col == 0:
            prev_ref[4 * TS : 5 * TS] = west
        else:
            local_ref[TS * (col - 1) : TS * col] = west
        if col == 3:
            next_ref[4 * TS : 5 * TS] = east
        else:
            local_ref[TS * (3 + col) : TS * (4 + col)] = east


def sigmoid(values):
    return 1.0 / (1.0 + jnp.exp(-values))


def slope(values):
    sig = sigmoid(values)
    return sig * (1.0 + values * (1.0 - sig))


UP = slice(0, 80)
DOWN = slice(80, 160)
LOCAL = slice(160, 256)


def gate_kernel(gates_ref, kernel_ref, out_ref):
    count, groups = gates_ref.shape
    width = 4 * groups
    rows = lax.broadcasted_iota(jnp.int32, (groups, width), 0)
    cols = lax.broadcasted_iota(jnp.int32, (groups, width), 1)
    repeat = ((cols >> 2) == rows).astype(F32).astype(BF)
    wide = dot(gates_ref[...].astype(F32).astype(BF), repeat)
    lane = lax.broadcasted_iota(jnp.int32, (count, width), 1) & 3
    out_ref[...] = jnp.where(keep_of(wide, lane), kernel_ref[...].astype(F32), 0.0).astype(BF)


def keep_of(wide, lane):
    low = jnp.where(wide >= 4.5, 2, jnp.where(wide >= 2.5, 1, 0))
    high = jnp.where(wide < 0.5, 1, jnp.where((wide < 1.5) | ((wide > 2.5) & (wide < 3.5)), 2, 3))
    return (lane == low) | (lane == high)


def start_kernel(own_ref, other_ref, index_ref, field_ref, grad_ref, strips_ref):
    for col in range(ROW):
        own = own_ref[col].astype(F32)
        other = other_ref[col].astype(F32)
        blank = jnp.zeros((PADC - FIELDS - COUPLED, CELLS), F32)
        field = jnp.concatenate([own[:FIELDS], other, blank], 0)
        field_ref[CELLS * col : CELLS * (col + 1)] = field.T.astype(BF)
        blank = jnp.zeros((PADC - FIELDS, CELLS), F32)
        grad = jnp.concatenate([own[FIELDS:], blank], 0)
        grad_ref[CELLS * col : CELLS * (col + 1)] = grad.T.astype(BF)
    take = one_hot((256, LINE), 1, index_ref[...])
    strips_ref[...] = dot(take, field_ref[...]).astype(BF)


def first_kernel_body(
    field_ref, local_ref, prev_ref, next_ref, grad_ref, first_ref, out_back_ref, index_col_ref, index_row_ref,
    filled_ref, act_ref, hid_ref, strips_ref, up_ref, down_ref, inner_ref,
    pad_ref, back_local_ref,
):
    fill(filled_ref, field_ref[...], local_ref[...], prev_ref[...], next_ref[...])
    for col in range(ROW):
        act = conv_tile(filled_ref, first_ref, col)
        act_ref[CELLS * col : CELLS * (col + 1)] = act
        hid_ref[CELLS * col : CELLS * (col + 1)] = (act * sigmoid(act)).astype(BF)
    take = one_hot((256, LINE), 1, index_col_ref[...])
    strips = dot(take, hid_ref[...]).astype(BF)
    strips_ref[...] = strips[LOCAL]
    up_ref[0:80] = strips[UP]
    down_ref[0:80] = strips[DOWN]
    fold_row(
        lambda col: grad_ref[CELLS * col : CELLS * (col + 1)],
        out_back_ref, pad_ref, inner_ref, down_ref.at[80:160], up_ref.at[80:160], back_local_ref,
    )
    give = one_hot((LINE, 96), 0, index_row_ref[:, LOCAL])
    inner_ref[...] += dot(give, back_local_ref[...])


def mid_kernel_body(
    hid_ref, local_ref, prev_ref, next_ref, inner_two_ref, mid_ref, mid_back_ref, index_col_ref, index_row_ref,
    filled_ref, grad_ref, hid_two_ref, strips_ref, up_ref, down_ref, inner_ref,
    pad_ref, back_local_ref,
):
    fill(filled_ref, hid_ref[...], local_ref[...], prev_ref[0:80], next_ref[0:80])
    give_up = one_hot((LINE, 80), 0, index_row_ref[:, UP])
    give_down = one_hot((LINE, 80), 0, index_row_ref[:, DOWN])
    grad_hid = inner_two_ref[...] + dot(give_up, next_ref[80:160]) + dot(give_down, prev_ref[80:160])
    for col in range(ROW):
        rows = slice(CELLS * col, CELLS * (col + 1))
        act = conv_tile(filled_ref, mid_ref, col)
        sig = sigmoid(act)
        hid_two_ref[rows] = (act * sig).astype(BF)
        grad_ref[rows] = (grad_hid[rows] * (sig * (1.0 + act * (1.0 - sig)))).astype(BF)
    take = one_hot((256, LINE), 1, index_col_ref[...])
    strips = dot(take, hid_two_ref[...]).astype(BF)
    strips_ref[...] = strips[LOCAL]
    up_ref[0:80] = strips[UP]
    down_ref[0:80] = strips[DOWN]
    fold_row(
        lambda col: grad_ref[CELLS * col : CELLS * (col + 1)],
        mid_back_ref, pad_ref, inner_ref, down_ref.at[80:160], up_ref.at[80:160], back_local_ref,
    )
    give = one_hot((LINE, 96), 0, index_row_ref[:, LOCAL])
    inner_ref[...] += dot(give, back_local_ref[...])


def gather_rows(filled_ref, a):
    return jnp.concatenate(
        [filled_ref[col, a : a + TS].reshape(CELLS, filled_ref.shape[3]) for col in range(ROW)], 0
    )


def mid_term_body(filled_ref, grad_ref, pick_ref, out_ref, flat_ref):
    turned = grad_ref[...].astype(F32).T.astype(BF)
    width = filled_ref.shape[3]
    for a in range(3):
        flat_ref[:, width * a : width * (a + 1)] = dot(turned, gather_rows(filled_ref, a)).astype(BF)
    pick = one_hot((16 * CHUNK, 1152), 1, pick_ref[...])
    for half in range(2):
        out_ref[16 * CHUNK * half : 16 * CHUNK * (half + 1)] = dot_nt(pick, flat_ref[:, 1152 * half : 1152 * (half + 1)])


def last_kernel_body(
    col_ref, hid_two_ref, local_ref, prev_ref, next_ref, inner_ref, act_ref, filled_zero_ref, grad_three_ref,
    out_ref, first_back_ref, index_row_ref, mid_part_ref, pick_out_ref, pick_first_ref, slot_ref,
    result_ref, buffer_ref, dx_ref, up_ref, down_ref,
    filled_ref, pad_ref, grad_ref, dx_all_ref, back_local_ref, flat_ref, flat_zero_ref,
):
    own = pl.multiple_of(col_ref[0] * CELLS, CELLS)
    fill(filled_ref, hid_two_ref[...], local_ref[...], prev_ref[0:80], next_ref[0:80])
    width = filled_ref.shape[3]
    mine = filled_ref.at[col_ref[0]]
    total = None
    for a in range(3):
        piece = dot(mine[a : a + TS].reshape(CELLS, width), out_ref[a])
        total = piece if total is None else total + piece
    result_ref[...] = total.T[:FIELDS]
    give_up = one_hot((LINE, 80), 0, index_row_ref[:, UP])
    give_down = one_hot((LINE, 80), 0, index_row_ref[:, DOWN])
    grad_hid = inner_ref[...] + dot(give_up, next_ref[80:160]) + dot(give_down, prev_ref[80:160])
    grad_ref[...] = (grad_hid * slope(act_ref[...])).astype(BF)
    fold_row(
        lambda col: grad_ref[CELLS * col : CELLS * (col + 1)],
        first_back_ref, pad_ref, dx_all_ref, down_ref, up_ref, back_local_ref,
    )
    give = one_hot((LINE, 96), 0, index_row_ref[:, LOCAL])
    dx_all_ref[...] += dot(give, back_local_ref[...])
    dx_ref[...] = dx_all_ref[pl.ds(own, CELLS)]
    three = grad_three_ref[...].astype(F32).T
    repeated = jnp.concatenate([three[:FIELDS]] * 9 + [jnp.zeros((HID - 9 * FIELDS, LINE), F32)], 0).astype(BF)
    slots = lax.broadcasted_iota(jnp.int32, (HID, width), 0) >> 4
    for a in range(3):
        term = dot(repeated, gather_rows(filled_ref, a))
        flat_ref[:, width * a : width * (a + 1)] = jnp.where(
            slots == slot_ref[:, width * a : width * (a + 1)], term, 0.0
        ).astype(BF)
    turned = grad_ref[...].astype(F32).T.astype(BF)
    zero_width = filled_zero_ref.shape[3]
    for a in range(3):
        flat_zero_ref[:, zero_width * a : zero_width * (a + 1)] = dot(
            turned, gather_rows(filled_zero_ref, a)
        ).astype(BF)
    along = lax.broadcasted_iota(jnp.int32, (16 * CHUNK, 1152), 1)
    low = pick_out_ref[...]
    pick_out = ((along >= low) & (along < low + 9)).astype(F32).astype(BF)
    for half in range(2):
        rows = slice(16 * CHUNK * half, 16 * CHUNK * (half + 1))
        pick_first = one_hot((16 * CHUNK, 1152), 1, pick_first_ref[rows])
        buffer_ref[rows] = (
            mid_part_ref[rows]
            + dot_nt(pick_out, flat_ref[:, 1152 * half : 1152 * (half + 1)])
            + dot_nt(pick_first, flat_zero_ref[...])
        ).astype(BF)


def finish_kernel(dx_ref, next_ref, prev_ref, index_row_ref, base_ref, out_ref):
    base = base_ref[0]
    rows = lax.broadcasted_iota(jnp.int32, (CELLS, 80), 0) + base
    give_up = (rows == index_row_ref[:, UP]).astype(F32).astype(BF)
    give_down = (rows == index_row_ref[:, DOWN]).astype(F32).astype(BF)
    total = dx_ref[...] + dot(give_up, next_ref[...]) + dot(give_down, prev_ref[...])
    out_ref[...] = total.T[: FIELDS + COUPLED]


VMEM = pl.BlockSpec(memory_space=pltpu.VMEM)
SMEM = pl.BlockSpec(memory_space=pltpu.SMEM)


def call(body, out, args, scratch=(), scalars=(), name=None, flops=0):
    specs = [SMEM if position in scalars else VMEM for position in range(len(args))]
    size = sum(int(np.prod(item.shape)) * item.dtype.itemsize for item in list(args) + list(out))
    return pl.pallas_call(
        body,
        out_shape=[jax.ShapeDtypeStruct(item.shape, item.dtype) for item in out],
        in_specs=specs,
        out_specs=[VMEM] * len(out),
        scratch_shapes=list(scratch),
        compiler_params=pltpu.CompilerParams(vmem_limit_bytes=60 * 1024 * 1024),
        cost_estimate=pl.CostEstimate(flops=flops, bytes_accessed=size, transcendentals=0),
        name=name,
    )(*args)


def sds(shape, kind):
    return jax.ShapeDtypeStruct(shape, kind)


def row_shift(value, step):
    pairs = [(face, (face + ROW * step) % TILES) for face in range(TILES)]
    return lax.ppermute(value, FACE, pairs)


def body(
    state, cotangent, land_sea, turn_table, first_kernel, mid_kernel, out_kernel, first_gates, mid_gates, out_gates
):
    comp = lax.axis_index("comp")
    row = lax.axis_index(ROW_AXES)
    col = lax.axis_index(("xh", "core"))
    tile = row * ROW + col
    own_state = state[0]
    sea = land_sea.astype(F32)
    weight = jnp.where(comp == 1, sea, jnp.ones_like(sea))
    cot = cotangent[0].astype(F32)
    grad_three = (weight * cot).astype(BF)

    packed = jnp.concatenate([own_state, grad_three], 0)
    line = lax.all_to_all(jnp.broadcast_to(packed[None], (8, 32, CELLS)), LINE_AXES, 0, 0)
    line = line.reshape(2, ROW, 32, CELLS)
    own = jnp.where(comp == 0, line[0], line[1])
    other = jnp.where(comp == 0, line[1, :, :COUPLED], line[0, :, :COUPLED])

    index = strip_index(turn_table, row)
    index_col, index_row = index.reshape(256, 1), index.reshape(1, 256)
    field, grad_cells, strips_zero = call(
        start_kernel,
        [sds((LINE, PADC), BF), sds((LINE, PADC), BF), sds((256, PADC), BF)],
        [own, other, index_col], name="start",
    )
    prev_zero = row_shift(strips_zero[UP], 1)
    next_zero = row_shift(strips_zero[DOWN], -1)

    def gated(gates, kernel, name):
        return call(gate_kernel, [sds(kernel.shape, BF)], [gates, kernel], name=name)[0]

    gated_first = gated(first_gates[0], first_kernel[0], "gate_first")
    gated_mid = gated(mid_gates[0], mid_kernel[0], "gate_mid")
    gated_out = gated(out_gates[0], out_kernel[0], "gate_out")
    pad_in = PADC - FIELDS - COUPLED
    first_w = jnp.pad(gated_first.reshape(3, 3, FIELDS + COUPLED, HID), ((0, 0), (0, 0), (0, pad_in), (0, 0)))
    first_w = first_w.reshape(3, 3 * PADC, HID)
    first_back = first_w.transpose(0, 2, 1).reshape(3 * HID, 3 * PADC)
    mid_w = gated_mid.reshape(3, 3 * HID, HID)
    mid_back = mid_w.transpose(0, 2, 1).reshape(3 * HID, 3 * HID)
    out_w = jnp.pad(gated_out, ((0, 0), (0, PADC - FIELDS))).reshape(3, 3 * HID, PADC)
    out_back = out_w.transpose(0, 2, 1).reshape(3 * PADC, 3 * HID)

    exchange = [sds((160, HID), BF), sds((160, HID), BF)]
    filled_zero, act_one, hid_one, local_one, up_one, down_one, inner_two = call(
        first_kernel_body,
        [sds((ROW, TS + 2, TS, 3 * PADC), BF), sds((LINE, HID), F32), sds((LINE, HID), BF), sds((96, HID), BF)]
        + exchange + [sds((LINE, HID), F32)],
        [field, strips_zero[LOCAL], prev_zero, next_zero, grad_cells, first_w, out_back, index_col, index_row],
        scratch=[pltpu.VMEM((TS + 2, TS, 3 * PADC), BF), pltpu.VMEM((96, HID), BF)],
        name="layer_one",
    )
    prev_one = row_shift(up_one, 1)
    next_one = row_shift(down_one, -1)

    filled_one, grad_two, hid_two, local_two, up_two, down_two, inner_one = call(
        mid_kernel_body,
        [sds((ROW, TS + 2, TS, 3 * HID), BF), sds((LINE, HID), BF), sds((LINE, HID), BF), sds((96, HID), BF)]
        + exchange + [sds((LINE, HID), F32)],
        [hid_one, local_one, prev_one, next_one, inner_two, mid_w, mid_back, index_col, index_row],
        scratch=[pltpu.VMEM((TS + 2, TS, 3 * HID), BF), pltpu.VMEM((96, HID), BF)],
        name="layer_two",
    )
    prev_two = row_shift(up_two, 1)
    next_two = row_shift(down_two, -1)

    place = jnp.arange(16 * CHUNK, dtype=jnp.int32)
    block, inside = place // CHUNK, place % CHUNK
    begin = 72 * block + 18 * col
    pick_mid = jnp.where(inside < 18, begin + inside, -1).reshape(-1, 1)
    pick_out = jnp.where((inside >= 18) & (inside < 20), begin + 9 * (inside - 18), -100).reshape(-1, 1)
    place = jnp.arange(32 * CHUNK, dtype=jnp.int32)
    block, inside = place // CHUNK, place % CHUNK
    wanted = 8 * block + 2 * col + inside - 20
    real = (inside >= 20) & (inside < 22) & (wanted < 9 * (FIELDS + COUPLED))
    depth = FIELDS + COUPLED
    pick_first = jnp.where(real, (wanted // depth) * PADC + wanted % depth, -1).reshape(-1, 1)
    kernel_row = jnp.arange(9 * HID, dtype=jnp.int32)
    slot = ((kernel_row % 72 - 18 * col + 72) % 9).reshape(1, -1)

    mid_part = call(
        mid_term_body,
        [sds((32 * CHUNK, HID), F32)],
        [filled_one, grad_two, pick_mid],
        scratch=[pltpu.VMEM((HID, 9 * HID), BF)],
        name="mid_term", flops=2 * 10**9,
    )[0]

    result, buffer, dx_own, up_three, down_three = call(
        last_kernel_body,
        [sds((FIELDS, CELLS), F32), sds((32 * CHUNK, HID), BF), sds((CELLS, PADC), F32), sds((80, PADC), BF),
         sds((80, PADC), BF)],
        [col.reshape(1), hid_two, local_two, prev_two, next_two, inner_one, act_one, filled_zero, grad_cells,
         out_w, first_back, index_row, mid_part, pick_out, pick_first, slot],
        scratch=[
            pltpu.VMEM((ROW, TS + 2, TS, 3 * HID), BF), pltpu.VMEM((TS + 2, TS, 3 * HID), BF),
            pltpu.VMEM((LINE, HID), BF), pltpu.VMEM((LINE, PADC), F32), pltpu.VMEM((96, PADC), BF),
            pltpu.VMEM((HID, 9 * HID), BF), pltpu.VMEM((HID, 9 * PADC), BF),
        ],
        scalars=(0,), name="layer_three",
    )
    prev_three = row_shift(up_three, 1)
    next_three = row_shift(down_three, -1)
    estimate = (own_state.astype(F32) + weight * result).astype(BF)

    spread = lax.all_to_all(buffer.reshape(ROWS, CHUNK, HID), ROW_AXES, 0, 0)
    summed = jnp.sum(spread.astype(F32), 0)

    dx = call(
        finish_kernel, [sds((FIELDS + COUPLED, CELLS), F32)],
        [dx_own, next_three, prev_three, index_row, (col * CELLS).reshape(1)], scalars=(4,), name="finish",
    )[0]
    returned = lax.ppermute(dx[FIELDS:], "comp", [(0, 1), (1, 0)])
    adjoint = cot + dx[:FIELDS] + jnp.pad(returned, ((0, FIELDS - COUPLED), (0, 0)))

    shared = jnp.broadcast_to(summed[20:22].astype(BF)[None], (TILES, 2, HID))
    opening = lax.all_to_all(shared, FACE, 0, 0).reshape(2 * TILES, HID)[: 9 * depth].astype(F32)

    def keep_mask(gates):
        groups = gates.shape[1]
        repeat = (np.arange(4 * groups)[None] // 4 == np.arange(groups)[:, None]).astype(np.float32)
        wide = dot(gates.astype(BF), jnp.asarray(repeat, BF))
        return keep_of(wide, jnp.arange(4 * groups, dtype=jnp.int32)[None] & 3)

    opening = jnp.where(keep_mask(first_gates[0]), opening, 0.0)
    rows_mid = lax.dynamic_slice(mid_gates[0], (18 * tile, 0), (18, HID // 4))
    central = jnp.where(keep_mask(rows_mid), summed[:18], 0.0).reshape(1, 18 * HID)
    rows_out = lax.dynamic_slice(out_gates[0], (18 * tile, 0), (18, FIELDS // 4))
    closing = summed[18:20, : 9 * FIELDS].reshape(18, FIELDS)
    closing = jnp.where(keep_mask(rows_out), closing, 0.0).reshape(1, 18 * FIELDS)
    return estimate[None], adjoint[None], opening[None], central, closing


def solution(mesh):
    fine = Mesh(mesh.devices.reshape(2, 4, 8, 2, 2), ("comp",) + FACE)
    whole = P("comp", None, None)
    in_specs = (P("comp", None, FACE), P("comp", None, FACE), P(FACE), P()) + (whole,) * 6
    out_specs = (P("comp", None, FACE), P("comp", None, FACE), whole, P("comp", FACE), P("comp", FACE))
    return jax.shard_map(body, mesh=fine, in_specs=in_specs, out_specs=out_specs, check_vma=False)
```

```python
import jax
import jax.numpy as jnp
import numpy as np
from jax import lax
from jax.experimental import pallas as pl
from jax.experimental.pallas import tpu as pltpu
from jax.sharding import Mesh, PartitionSpec as P


FIELDS = 16
COUPLED = 8
TS = 16
CELLS = TS * TS
ROW = 4
ROWS = 32
TILES = ROW * ROWS
LINE = ROW * CELLS
HID = 256
PADC = 128
CHUNK = 24
SHARE = 16
BF = jnp.bfloat16
F32 = jnp.float32

FACE = ("y", "z", "xh", "core")
ROW_AXES = ("y", "z")
LINE_AXES = ("comp", "xh", "core")

EDGE_MAP = (
    ((0, False), (2, True), (1, True), (3, False)),
    ((1, False), (3, True), (0, True), (2, False)),
    ((2, False), (1, False), (3, True), (0, True)),
    ((3, False), (0, False), (2, True), (1, True)),
)

STRIPS = (
    [(col, 2, 8 + col) for col in range(4)]
    + [(3, 0, 8)]
    + [(col, 3, col) for col in range(4)]
    + [(0, 1, 3)]
    + [(col - 1, 0, 4 + col) for col in (1, 2, 3)]
    + [(col + 1, 1, 4 + col) for col in (0, 1, 2)]
)


def edge_line(slot, flip):
    first, step = ((TS - 1, TS), (0, TS), ((TS - 1) * TS, 1), (0, 1))[slot]
    if flip:
        first, step = first + (TS - 1) * step, -step
    return first, step


def dot(left, right):
    return jnp.dot(left, right, preferred_element_type=F32)


def dot_nt(left, right):
    return lax.dot_general(left, right, (((1,), (1,)), ((), ())), preferred_element_type=F32)


def dot_tn(left, right):
    return lax.dot_general(left, right, (((0,), (0,)), ((), ())), preferred_element_type=F32)


def dot_exact(left, right):
    high = right.astype(BF)
    rest = right - high.astype(F32)
    mid = rest.astype(BF)
    low = (rest - mid.astype(F32)).astype(BF)
    return dot(left, high) + (dot(left, mid) + dot(left, low))


def dot_exact_right(left, right):
    high = left.astype(BF)
    rest = left - high.astype(F32)
    mid = rest.astype(BF)
    low = (rest - mid.astype(F32)).astype(BF)
    return dot(high, right) + (dot(mid, right) + dot(low, right))


def fetch(sources, buffers, sems):
    copies = [
        pltpu.make_async_copy(source, buffer, sems.at[place])
        for place, (source, buffer) in enumerate(zip(sources, buffers))
    ]
    for copy in copies:
        copy.start()
    return copies


def one_hot(shape, axis, index):
    return (lax.broadcasted_iota(jnp.int32, shape, axis) == index).astype(F32).astype(BF)


def edge_spread(column):
    rows = lax.broadcasted_iota(jnp.int32, (CELLS, TS), 0)
    cols = lax.broadcasted_iota(jnp.int32, (CELLS, TS), 1)
    return (rows == cols * TS + column).astype(F32).astype(BF)


def edge_take(column):
    rows = lax.broadcasted_iota(jnp.int32, (TS, CELLS), 0)
    cols = lax.broadcasted_iota(jnp.int32, (TS, CELLS), 1)
    return (cols == rows * TS + column).astype(F32).astype(BF)


def shift_cells(value, step, axis):
    along = lax.broadcasted_iota(jnp.int32, value.shape, axis)
    moved = pltpu.roll(value, step % TS, axis)
    edge = 0 if step == 1 else TS - 1
    return jnp.where(along == edge, 0.0, moved)


def fill(out_ref, tiles, local, from_prev, from_next):
    depth = tiles.shape[1]
    spread_west, spread_east = edge_spread(0), edge_spread(TS - 1)
    for col in range(ROW):
        south = from_prev[TS * col : TS * (col + 1)]
        north = from_next[TS * col : TS * (col + 1)]
        west = from_prev[4 * TS : 5 * TS] if col == 0 else local[TS * (col - 1) : TS * col]
        east = from_next[4 * TS : 5 * TS] if col == 3 else local[TS * (3 + col) : TS * (4 + col)]
        own = tiles[CELLS * col : CELLS * (col + 1)]
        wide = own.astype(F32).reshape(TS, TS, depth)
        left = shift_cells(wide, 1, 1) + dot(spread_west, west).reshape(TS, TS, depth)
        right = shift_cells(wide, -1, 1) + dot(spread_east, east).reshape(TS, TS, depth)
        out_ref[col, 1 : TS + 1, :, 0:depth] = left.astype(BF)
        out_ref[col, 1 : TS + 1, :, depth : 2 * depth] = own.reshape(TS, TS, depth)
        out_ref[col, 1 : TS + 1, :, 2 * depth : 3 * depth] = right.astype(BF)
        for line, strip in ((0, south), (TS + 1, north)):
            wide = strip.astype(F32)
            out_ref[col, line, :, 0:depth] = shift_cells(wide, 1, 0).astype(BF)
            out_ref[col, line, :, depth : 2 * depth] = strip
            out_ref[col, line, :, 2 * depth : 3 * depth] = shift_cells(wide, -1, 0).astype(BF)


def conv_tile(filled_ref, weights_ref, col):
    width = filled_ref.shape[3]
    total = None
    for a in range(3):
        piece = dot(filled_ref[col, a : a + TS].reshape(CELLS, width), weights_ref[a])
        total = piece if total is None else total + piece
    return total


def fold_tile(grad, weights_ref, pad_ref):
    deep = grad.shape[1]
    lines = grad.reshape(TS, TS, deep)
    for a in range(3):
        pad_ref[a : a + TS, :, deep * a : deep * (a + 1)] = lines
    total = dot(pad_ref[...].reshape((TS + 2) * TS, 3 * deep), weights_ref[...])
    depth = total.shape[1] // 3
    total = total.reshape(TS + 2, TS, 3 * depth)
    left, mid, right = (total[:, :, depth * b : depth * (b + 1)] for b in range(3))
    merged = mid + shift_cells(left, -1, 1) + shift_cells(right, 1, 1)
    inner = merged[1 : TS + 1].reshape(CELLS, depth)
    south = merged[0].astype(BF)
    north = merged[TS + 1].astype(BF)
    west = dot(edge_take(0), left[1 : TS + 1].reshape(CELLS, depth).astype(BF)).astype(BF)
    east = dot(edge_take(TS - 1), right[1 : TS + 1].reshape(CELLS, depth).astype(BF)).astype(BF)
    return inner, south, north, west, east


def fold_row(grad_of, weights_ref, pad_ref, inner_ref, prev_ref, next_ref, local_ref):
    pad_ref[...] = jnp.zeros_like(pad_ref)
    for col in range(ROW):
        inner, south, north, west, east = fold_tile(grad_of(col), weights_ref, pad_ref)
        inner_ref[CELLS * col : CELLS * (col + 1)] = inner
        prev_ref[TS * col : TS * (col + 1)] = south
        next_ref[TS * col : TS * (col + 1)] = north
        if col == 0:
            prev_ref[4 * TS : 5 * TS] = west
        else:
            local_ref[TS * (col - 1) : TS * col] = west
        if col == 3:
            next_ref[4 * TS : 5 * TS] = east
        else:
            local_ref[TS * (3 + col) : TS * (4 + col)] = east


def sigmoid(values):
    return 1.0 / (1.0 + jnp.exp(-values))


def slope(values):
    sig = sigmoid(values)
    return sig * (1.0 + values * (1.0 - sig))


UP = slice(0, 80)
DOWN = slice(80, 160)
LOCAL = slice(160, 256)


def keep_of(wide, lane):
    low = jnp.where(wide >= 4.5, 2, jnp.where(wide >= 2.5, 1, 0))
    high = jnp.where(wide < 0.5, 1, jnp.where((wide < 1.5) | ((wide > 2.5) & (wide < 3.5)), 2, 3))
    return lane == low, lane == high


def kept_pair(planes, gates):
    one, two, three, four = planes
    low = jnp.where(gates >= 4.5, three, jnp.where(gates >= 2.5, two, one))
    high = jnp.where(gates < 0.5, two, jnp.where((gates < 1.5) | ((gates > 2.5) & (gates < 3.5)), three, four))
    return low, high


def eye(rows, cols):
    return one_hot((rows, cols), 1, lax.broadcasted_iota(jnp.int32, (rows, cols), 0))


def repeat_four(groups, width):
    rows = lax.broadcasted_iota(jnp.int32, (groups, width), 0)
    cols = lax.broadcasted_iota(jnp.int32, (groups, width), 1)
    return ((cols >> 2) == rows).astype(F32).astype(BF)


def plane_order():
    rows = lax.broadcasted_iota(jnp.int32, (HID, HID), 0)
    return one_hot((HID, HID), 1, 4 * (rows & 63) + (rows >> 6))


def pack_kernel(state_hbm, cot_hbm, sea_hbm, out_ref, state_ref, cot_ref, sea_ref, sems):
    copies = fetch((state_hbm, cot_hbm, sea_hbm), (state_ref, cot_ref, sea_ref), sems)
    for copy in copies:
        copy.wait()
    comp = lax.axis_index("comp")
    weight = jnp.where(comp == 1, sea_ref[...].astype(F32), 1.0)
    grad = (weight * cot_ref[...].astype(F32)).astype(BF)
    for place in range(8):
        out_ref[place, 0:FIELDS] = state_ref[...]
        out_ref[place, FIELDS : 2 * FIELDS] = grad


def kept_rows(gates, kernel):
    outputs = kernel.shape[0]
    rows = lax.broadcasted_iota(jnp.int32, (outputs, outputs // 4), 0) >> 2
    wide = dot(one_hot((outputs, outputs // 4), 1, rows), gates)
    low, high = keep_of(wide, lax.broadcasted_iota(jnp.int32, wide.shape, 0) & 3)
    return jnp.where(low | high, kernel, 0.0)


def prepare_kernel(
    turn_ref, first_gates_hbm, mid_gates_hbm, out_gates_hbm, first_hbm, mid_hbm, out_hbm,
    take_ref, give_ref, first_w_ref, first_back_ref, mid_w_ref, mid_back_ref, out_w_ref, out_back_ref,
    first_turned_ref, mid_turned_ref, out_turned_ref, first_wide_ref,
    first_gates_ref, mid_gates_ref, out_gates_ref, first_ref, mid_ref, out_ref, sems,
):
    copies = fetch(
        (first_gates_hbm, mid_gates_hbm, out_gates_hbm, first_hbm, mid_hbm, out_hbm),
        (first_gates_ref, mid_gates_ref, out_gates_ref, first_ref, mid_ref, out_ref), sems,
    )
    row = lax.axis_index(ROW_AXES)
    strip_of = lax.broadcasted_iota(jnp.int32, (8, 256), 1) >> 4
    along = lax.broadcasted_iota(jnp.int32, (8, 256), 1) & 15
    cells = jnp.zeros((8, 256), jnp.int32)
    for number, (source, side, reader) in enumerate(STRIPS):
        turn = turn_ref[side, lax.rem(ROW * row + reader - ROW + TILES, TILES)]
        first, step = edge_line(*EDGE_MAP[side][3])
        for turns in range(3):
            one, two = edge_line(*EDGE_MAP[side][turns])
            first, step = jnp.where(turn == turns, one, first), jnp.where(turn == turns, two, step)
        first = first + source * CELLS
        cells = jnp.where(strip_of == number, first + step * along, cells)
        place = lax.broadcasted_iota(jnp.int32, (TS, LINE), 1)
        wanted = first + step * lax.broadcasted_iota(jnp.int32, (TS, LINE), 0)
        take_ref[TS * number : TS * (number + 1)] = (place == wanted).astype(F32).astype(BF)
    give_ref[...] = one_hot((LINE, 256), 0, cells[0:1])
    for copy in copies:
        copy.wait()
    depth = FIELDS + COUPLED
    count = 9 * depth
    gates = first_gates_ref[...].astype(F32).astype(BF)
    wide = dot_tn(gates, repeat_four(HID // 4, HID))
    first_wide_ref[...] = wide.astype(BF)
    low, high = keep_of(wide, lax.broadcasted_iota(jnp.int32, (count, HID), 1) & 3)
    kernel = jnp.where(low | high, first_ref[...].astype(F32), 0.0)
    blank = jnp.zeros((PADC - depth, HID), F32)
    for a in range(3):
        for b in range(3):
            rows = slice(depth * (3 * a + b), depth * (3 * a + b + 1))
            first_w_ref[a, PADC * b : PADC * (b + 1)] = jnp.concatenate([kernel[rows], blank], 0).astype(BF)
        first_back_ref[HID * a : HID * (a + 1)] = dot_nt(eye(HID, HID), first_w_ref[a]).astype(BF)
    place = lax.broadcasted_iota(jnp.int32, (count, 9 * PADC), 0)
    tap = (place * 2731) >> 16
    first_turned_ref[...] = dot(gates, one_hot((count, 9 * PADC), 1, tap * PADC + place - depth * tap)).astype(BF)
    for a in range(3):
        cols = slice(3 * HID * a, 3 * HID * (a + 1))
        gates = mid_gates_ref[:, cols].astype(F32).astype(BF)
        mid_turned_ref[:, cols] = gates
        mid_back_ref[HID * a : HID * (a + 1)] = kept_rows(gates, dot_nt(eye(HID, HID), mid_ref[cols])).astype(BF)
        mid_w_ref[a] = dot_tn(mid_back_ref[HID * a : HID * (a + 1)], eye(HID, HID)).astype(BF)
        gates = out_gates_ref[:, cols].astype(F32).astype(BF)
        out_turned_ref[:, cols] = dot(eye(8, 4), gates).astype(BF)
        kernel = kept_rows(gates, out_ref[:, cols].astype(F32))
        kernel = jnp.concatenate([kernel, jnp.zeros((PADC - FIELDS, 3 * HID), F32)], 0)
        out_back_ref[PADC * a : PADC * (a + 1)] = kernel.astype(BF)
        out_w_ref[a] = kernel.T.astype(BF)


def start_kernel(line_ref, take_ref, field_ref, grad_ref, strips_ref):
    comp = lax.axis_index("comp")
    for col in range(ROW):
        own = line_ref[comp, col].astype(F32)
        other = line_ref[1 - comp, col][:FIELDS].astype(F32)[:COUPLED]
        blank = jnp.zeros((PADC - FIELDS - COUPLED, CELLS), F32)
        field = jnp.concatenate([own[:FIELDS], other, blank], 0)
        field_ref[CELLS * col : CELLS * (col + 1)] = field.T.astype(BF)
        blank = jnp.zeros((PADC - FIELDS, CELLS), F32)
        grad = jnp.concatenate([own[FIELDS:], blank], 0)
        grad_ref[CELLS * col : CELLS * (col + 1)] = grad.T.astype(BF)
    strips_ref[...] = dot(take_ref[...], field_ref[...]).astype(BF)


def send_strips(strips, up_ref, down_ref, local_ref):
    up_ref[0:80] = strips[UP]
    down_ref[0:80] = strips[DOWN]
    local_ref[0:96] = strips[LOCAL]


def back_strips(prev_ref, next_ref, local_ref):
    return jnp.concatenate([next_ref[80:160], prev_ref[80:160], local_ref[96:192]], 0)


def layer_one_kernel(
    field_ref, strips_ref, prev_ref, next_ref, grad_ref, first_ref, out_back_ref, take_ref,
    filled_ref, act_ref, hid_ref, local_ref, up_ref, down_ref, inner_ref,
    pad_ref,
):
    fill(filled_ref, field_ref[...], strips_ref[LOCAL], prev_ref[...], next_ref[...])
    for col in range(ROW):
        act = conv_tile(filled_ref, first_ref, col)
        act_ref[CELLS * col : CELLS * (col + 1)] = act
        hid_ref[CELLS * col : CELLS * (col + 1)] = (act * sigmoid(act)).astype(BF)
    send_strips(dot(take_ref[...], hid_ref[...]).astype(BF), up_ref, down_ref, local_ref)
    fold_row(
        lambda col: grad_ref[CELLS * col : CELLS * (col + 1)],
        out_back_ref, pad_ref, inner_ref, down_ref.at[80:160], up_ref.at[80:160], local_ref.at[96:192],
    )


def layer_two_kernel(
    hid_ref, local_in_ref, prev_ref, next_ref, inner_two_ref, mid_ref, mid_back_ref, take_ref, give_ref,
    filled_ref, grad_ref, hid_two_ref, local_ref, up_ref, down_ref, inner_ref,
    pad_ref,
):
    fill(filled_ref, hid_ref[...], local_in_ref[0:96], prev_ref[0:80], next_ref[0:80])
    strips = back_strips(prev_ref, next_ref, local_in_ref)
    for col in range(ROW):
        rows = slice(CELLS * col, CELLS * (col + 1))
        grad_hid = inner_two_ref[rows] + dot(give_ref[rows], strips)
        act = conv_tile(filled_ref, mid_ref, col)
        sig = sigmoid(act)
        hid_two_ref[rows] = (act * sig).astype(BF)
        grad_ref[rows] = (grad_hid * (sig * (1.0 + act * (1.0 - sig)))).astype(BF)
    send_strips(dot(take_ref[...], hid_two_ref[...]).astype(BF), up_ref, down_ref, local_ref)
    fold_row(
        lambda col: grad_ref[CELLS * col : CELLS * (col + 1)],
        mid_back_ref, pad_ref, inner_ref, down_ref.at[80:160], up_ref.at[80:160], local_ref.at[96:192],
    )


def gather_rows(filled_ref, a):
    return jnp.concatenate(
        [filled_ref[col, a : a + TS].reshape(CELLS, filled_ref.shape[3]) for col in range(ROW)], 0
    )


def term_pairs(filled_ref, grad, gates_ref, flat_ref):
    turned = dot_nt(plane_order(), grad).astype(BF)
    width = filled_ref.shape[3]
    for a in range(3):
        cols = slice(width * a, width * (a + 1))
        term = dot(turned, gather_rows(filled_ref, a))
        low, high = kept_pair([term[64 * m : 64 * (m + 1)] for m in range(4)], gates_ref[:, cols].astype(F32))
        flat_ref[0:64, cols] = low.astype(BF)
        flat_ref[64:128, cols] = high.astype(BF)


def mid_term_kernel(filled_ref, grad_ref, gates_ref, part_ref, pick_out_ref, pick_first_ref, flat_ref):
    col = lax.axis_index(("xh", "core"))
    term_pairs(filled_ref, grad_ref[...], gates_ref, flat_ref)
    shape = (16 * CHUNK, 1152)
    place = lax.broadcasted_iota(jnp.int32, shape, 0)
    block = (place * 2731) >> 16
    inside = place - CHUNK * block
    ahead = lax.broadcasted_iota(jnp.int32, shape, 1) - (72 * block + 18 * col)
    pick = ((ahead == inside) & (inside < 18)).astype(F32).astype(BF)
    late = ahead - 9 * (inside - 18)
    pick_out_ref[...] = ((late >= 0) & (late < 9) & (inside >= 18) & (inside < 20)).astype(F32).astype(BF)
    shape = (4 * SHARE, 1152)
    place = lax.broadcasted_iota(jnp.int32, shape, 0)
    inside = place & 15
    wanted = 14 * (4 * (place >> 4) + col) + inside
    tap = (wanted * 2731) >> 16
    target = tap * PADC + wanted - (FIELDS + COUPLED) * tap
    real = (inside < 14) & (wanted < 9 * (FIELDS + COUPLED))
    pick_first_ref[...] = ((lax.broadcasted_iota(jnp.int32, shape, 1) == target) & real).astype(F32).astype(BF)
    for half in range(2):
        part_ref[16 * CHUNK * half : 16 * CHUNK * (half + 1)] = dot_nt(
            pick, flat_ref[:, 1152 * half : 1152 * (half + 1)]
        )


def terms_kernel(
    hid_two_ref, local_ref, prev_ref, next_ref, inner_ref, act_ref, filled_zero_ref, grad_three_ref, give_ref,
    part_ref, pick_out_ref, pick_first_ref, first_gates_ref, out_gates_ref,
    buffer_ref, filled_ref, grad_ref,
    flat_ref, flat_zero_ref,
):
    fill(filled_ref, hid_two_ref[...], local_ref[0:96], prev_ref[0:80], next_ref[0:80])
    strips = back_strips(prev_ref, next_ref, local_ref)
    for col in range(ROW):
        rows = slice(CELLS * col, CELLS * (col + 1))
        grad_hid = inner_ref[rows] + dot(give_ref[rows], strips)
        grad_ref[rows] = (grad_hid * slope(act_ref[rows])).astype(BF)
    place = lax.broadcasted_iota(jnp.int32, (32, PADC), 0)
    group = place & 7
    wanted = jnp.where(group < 4, 4 * group + (place >> 3), -1)
    turned = dot_nt(one_hot((32, PADC), 1, wanted), grad_three_ref[...]).astype(BF)
    width = filled_ref.shape[3]
    for a in range(3):
        cols = slice(width * a, width * (a + 1))
        term = dot(turned, gather_rows(filled_ref, a))
        low, high = kept_pair([term[8 * m : 8 * (m + 1)] for m in range(4)], out_gates_ref[:, cols].astype(F32))
        pair = low + pltpu.roll(high, 4, 0)
        wide = jnp.broadcast_to(pair[None], (16, 8, width)).reshape(128, width)
        kernel_row = lax.broadcasted_iota(jnp.int32, (128, width), 1) + width * a
        slot = kernel_row - 9 * ((kernel_row * 7282) >> 16)
        mine = (lax.broadcasted_iota(jnp.int32, (128, width), 0) >> 3) == slot
        flat_ref[:, cols] = jnp.where(mine, wide, 0.0).astype(BF)
    term_pairs(filled_zero_ref, grad_ref[...], first_gates_ref, flat_zero_ref)
    for half in range(2):
        rows = slice(16 * CHUNK * half, 16 * CHUNK * (half + 1))
        part = part_ref[rows] + dot_nt(pick_out_ref[...], flat_ref[:, 1152 * half : 1152 * (half + 1)])
        buffer_ref[16 * half : 16 * (half + 1), 0:CHUNK] = part.astype(BF).reshape(16, CHUNK, PADC)
    share = dot_nt(pick_first_ref[...], flat_zero_ref[...]).astype(BF)
    for place in range(ROWS):
        kind = place // 8
        buffer_ref[place, CHUNK : CHUNK + SHARE] = share[SHARE * kind : SHARE * (kind + 1)]


def last_kernel(
    filled_ref, grad_ref, out_ref, first_back_ref, state_ref, sea_ref,
    estimate_ref, dx_ref, up_ref, down_ref, local_ref,
    pad_ref, dx_all_ref,
):
    comp = lax.axis_index("comp")
    col = lax.axis_index(("xh", "core"))
    width = filled_ref.shape[3]
    fold_row(
        lambda col: grad_ref[CELLS * col : CELLS * (col + 1)],
        first_back_ref, pad_ref, dx_all_ref, down_ref, up_ref, local_ref,
    )
    dx_ref[...] = dx_all_ref[pl.ds(pl.multiple_of(col * CELLS, CELLS), CELLS)]
    mine = filled_ref.at[col]
    total = None
    for a in range(3):
        piece = dot(mine[a : a + TS].reshape(CELLS, width), out_ref[a])
        total = piece if total is None else total + piece
    weight = jnp.where(comp == 1, sea_ref[...].astype(F32), 1.0)
    estimate_ref[...] = (state_ref[...].astype(F32) + weight * total.T[:FIELDS]).astype(BF)


def sum_kernel(spread_ref, share_ref, sum_ref):
    total = spread_ref[0].astype(F32)
    for place in range(1, ROWS):
        total = total + spread_ref[place].astype(F32)
    sum_ref[...] = total[:CHUNK]
    share = total[CHUNK:].astype(BF)
    for place in range(16):
        share_ref[place] = share


def finish_kernel(
    dx_ref, next_ref, prev_ref, local_ref, give_ref, cot_ref, sum_ref, mid_gates_ref, out_gates_ref,
    own_ref, send_ref, central_ref, closing_ref,
):
    col = lax.axis_index(("xh", "core"))
    give = give_ref[pl.ds(pl.multiple_of(col * CELLS, CELLS), CELLS)]
    strips = jnp.concatenate([next_ref[...], prev_ref[...], local_ref[...]], 0)
    total = (dx_ref[...] + dot(give, strips)).T
    own_ref[...] = cot_ref[...].astype(F32) + total[:FIELDS]
    send_ref[...] = total[FIELDS : FIELDS + COUPLED]
    tile = lax.axis_index(FACE)
    place = lax.broadcasted_iota(jnp.int32, (CHUNK, 9 * HID), 0)
    mine = one_hot((CHUNK, 9 * HID), 1, jnp.where(place < 18, 18 * tile + place, -1))
    sums = sum_ref[...]
    repeat = repeat_four(HID // 4, HID)
    wide = dot(dot_nt(mine, mid_gates_ref[...]).astype(BF), repeat)
    low, high = keep_of(wide, lax.broadcasted_iota(jnp.int32, (CHUNK, HID), 1) & 3)
    lows, highs = dot_exact_right(sums[:, :64], repeat), dot_exact_right(sums[:, 64:], repeat)
    central = jnp.where(low, lows, jnp.where(high, highs, 0.0))
    for line in range(18):
        central_ref[:, HID * line : HID * (line + 1)] = central[line : line + 1]
    place = lax.broadcasted_iota(jnp.int32, (CHUNK, CHUNK), 0)
    late = (place >= 9).astype(jnp.int32)
    spread = dot_exact(one_hot((CHUNK, CHUNK), 1, 18 + late), sums)
    place = lax.broadcasted_iota(jnp.int32, (CHUNK, PADC), 0)
    slot = place - 9 * (place >= 9).astype(jnp.int32)
    lane = lax.broadcasted_iota(jnp.int32, (CHUNK, PADC), 1)
    spread = jnp.where((lane >> 3) == slot, spread, 0.0)
    flat = 3 * PADC
    from_lane = lax.broadcasted_iota(jnp.int32, (PADC, flat), 0) & 7
    group = (lax.broadcasted_iota(jnp.int32, (PADC, flat), 1) & 15) >> 2
    lows = dot_exact_right(spread, (from_lane == group).astype(F32).astype(BF))
    highs = dot_exact_right(spread, (from_lane == group + 4).astype(F32).astype(BF))
    group = (lax.broadcasted_iota(jnp.int32, (8, flat), 1) & 15) >> 2
    wide = dot(dot_nt(mine, out_gates_ref[...]).astype(BF), one_hot((8, flat), 0, group))
    lane = lax.broadcasted_iota(jnp.int32, (CHUNK, flat), 1)
    low, high = keep_of(wide, lane & 3)
    closing = jnp.where(low, lows, jnp.where(high, highs, 0.0))
    here = lax.broadcasted_iota(jnp.int32, (CHUNK, flat), 0) == (lane >> 4)
    closing_ref[...] = jnp.sum(jnp.where(here, closing, 0.0), 0, keepdims=True)[:, : 18 * FIELDS]


def opening_kernel(share_ref, wide_ref, out_ref):
    count = 9 * (FIELDS + COUPLED)
    wanted = lax.broadcasted_iota(jnp.int32, (count, 16 * SHARE), 0)
    block = (wanted * 4682) >> 16
    pick = one_hot((count, 16 * SHARE), 1, SHARE * block + wanted - 14 * block)
    pairs = dot(pick, share_ref[...]).astype(BF)
    repeat = repeat_four(HID // 4, HID)
    low, high = keep_of(wide_ref[...].astype(F32), lax.broadcasted_iota(jnp.int32, (count, HID), 1) & 3)
    out_ref[...] = jnp.where(low, dot(pairs[:, :64], repeat), jnp.where(high, dot(pairs[:, 64:], repeat), 0.0))


VMEM = pl.BlockSpec(memory_space=pltpu.VMEM)
SMEM = pl.BlockSpec(memory_space=pltpu.SMEM)
HBM = pl.BlockSpec(memory_space=pltpu.HBM)


def call(body, out, args, scratch=(), scalars=(), far=(), flops=0, limit=10):
    specs = [SMEM if place in scalars else HBM if place in far else VMEM for place in range(len(args))]
    size = sum(int(np.prod(item.shape)) * item.dtype.itemsize for item in list(args) + list(out))
    return pl.pallas_call(
        body,
        out_shape=[jax.ShapeDtypeStruct(item.shape, item.dtype) for item in out],
        in_specs=specs,
        out_specs=[VMEM] * len(out),
        scratch_shapes=list(scratch),
        compiler_params=pltpu.CompilerParams(vmem_limit_bytes=limit * 1024 * 1024),
        cost_estimate=pl.CostEstimate(flops=flops, bytes_accessed=size, transcendentals=0),
    )(*args)


def sds(shape, kind):
    return jax.ShapeDtypeStruct(shape, kind)


def row_shift(value, step):
    pairs = [(face, (face + ROW * step) % TILES) for face in range(TILES)]
    return lax.ppermute(value, FACE, pairs)


def body(
    state, cotangent, land_sea, turn_table, first_kernel, mid_kernel, out_kernel, first_gates, mid_gates, out_gates
):
    sea = land_sea.reshape(1, CELLS)
    depth = FIELDS + COUPLED

    packed = call(pack_kernel, [sds((8, 2 * FIELDS, CELLS), BF)], [state[0], cotangent[0], sea],
        scratch=[
            pltpu.VMEM((FIELDS, CELLS), BF), pltpu.VMEM((FIELDS, CELLS), BF), pltpu.VMEM((1, CELLS), jnp.int32),
            pltpu.SemaphoreType.DMA((3,)),
        ],
        far=(0, 1, 2),
    )[0]
    line = lax.all_to_all(packed, LINE_AXES, 0, 0).reshape(2, ROW, 2 * FIELDS, CELLS)

    (
        take, give, first_w, first_back, mid_w, mid_back, out_w, out_back, first_turned, mid_turned, out_turned,
        first_wide,
    ) = call(
        prepare_kernel,
        [
            sds((256, LINE), BF), sds((LINE, 256), BF), sds((3, 3 * PADC, HID), BF), sds((3 * HID, 3 * PADC), BF),
            sds((3, 3 * HID, HID), BF), sds((3 * HID, 3 * HID), BF), sds((3, 3 * HID, PADC), BF),
            sds((3 * PADC, 3 * HID), BF), sds((64, 9 * PADC), BF), sds((64, 9 * HID), BF), sds((8, 9 * HID), BF),
            sds((9 * depth, HID), BF),
        ],
        [turn_table.T, first_gates[0].T, mid_gates[0].T, out_gates[0].T, first_kernel[0], mid_kernel[0],
         out_kernel[0].T],
        scratch=[
            pltpu.VMEM((64, 9 * depth), jnp.int32), pltpu.VMEM((64, 9 * HID), jnp.int32),
            pltpu.VMEM((4, 9 * HID), jnp.int32), pltpu.VMEM((9 * depth, HID), BF), pltpu.VMEM((9 * HID, HID), BF),
            pltpu.VMEM((FIELDS, 9 * HID), BF), pltpu.SemaphoreType.DMA((6,)),
        ],
        scalars=(0,), far=(1, 2, 3, 4, 5, 6), flops=5 * 10**9,
    )

    field, grad_cells, strips_zero = call(
        start_kernel,
        [sds((LINE, PADC), BF), sds((LINE, PADC), BF), sds((256, PADC), BF)], [line, take],
    )
    prev_zero = row_shift(strips_zero[UP], 1)
    next_zero = row_shift(strips_zero[DOWN], -1)

    exchange = [sds((192, HID), BF), sds((160, HID), BF), sds((160, HID), BF), sds((LINE, HID), F32)]
    filled_zero, act_one, hid_one, local_one, up_one, down_one, inner_two = call(
        layer_one_kernel,
        [sds((ROW, TS + 2, TS, 3 * PADC), BF), sds((LINE, HID), F32), sds((LINE, HID), BF)] + exchange,
        [field, strips_zero, prev_zero, next_zero, grad_cells, first_w, out_back, take],
        scratch=[pltpu.VMEM((TS + 2, TS, 3 * PADC), BF)],
    )
    prev_one = row_shift(up_one, 1)
    next_one = row_shift(down_one, -1)

    filled_one, grad_two, hid_two, local_two, up_two, down_two, inner_one = call(
        layer_two_kernel,
        [sds((ROW, TS + 2, TS, 3 * HID), BF), sds((LINE, HID), BF), sds((LINE, HID), BF)] + exchange,
        [hid_one, local_one, prev_one, next_one, inner_two, mid_w, mid_back, take, give],
        scratch=[pltpu.VMEM((TS + 2, TS, 3 * HID), BF)],
    )
    prev_two = row_shift(up_two, 1)
    next_two = row_shift(down_two, -1)

    part, pick_out, pick_first = call(
        mid_term_kernel,
        [sds((32 * CHUNK, PADC), F32), sds((16 * CHUNK, 1152), BF), sds((4 * SHARE, 1152), BF)],
        [filled_one, grad_two, mid_turned],
        scratch=[pltpu.VMEM((PADC, 9 * HID), BF)], flops=2 * 10**9,
    )

    buffer, filled_two, grad_one = call(
        terms_kernel,
        [sds((ROWS, CHUNK + SHARE, PADC), BF), sds((ROW, TS + 2, TS, 3 * HID), BF), sds((LINE, HID), BF)],
        [hid_two, local_two, prev_two, next_two, inner_one, act_one, filled_zero, grad_cells, give,
         part, pick_out, pick_first, first_turned, out_turned],
        scratch=[pltpu.VMEM((PADC, 9 * HID), BF), pltpu.VMEM((PADC, 9 * PADC), BF)],
    )
    spread = lax.all_to_all(buffer, ROW_AXES, 0, 0)

    estimate, dx_own, up_three, down_three, local_three = call(
        last_kernel,
        [sds((FIELDS, CELLS), BF), sds((CELLS, PADC), F32), sds((80, PADC), BF), sds((80, PADC), BF),
         sds((96, PADC), BF)],
        [filled_two, grad_one, out_w, first_back, state[0], sea],
        scratch=[pltpu.VMEM((TS + 2, TS, 3 * HID), BF), pltpu.VMEM((LINE, PADC), F32)], flops=2 * 10**9,
    )
    prev_three = row_shift(up_three, 1)
    next_three = row_shift(down_three, -1)

    shared, summed = call(sum_kernel, [sds((16, SHARE, PADC), BF), sds((CHUNK, PADC), F32)], [spread])
    opened = lax.all_to_all(shared, ("y", "xh", "core"), 0, 0).reshape(16 * SHARE, PADC)

    own, send, central, closing = call(
        finish_kernel,
        [sds((FIELDS, CELLS), F32), sds((COUPLED, CELLS), F32), sds((1, 18 * HID), F32), sds((1, 18 * FIELDS), F32)],
        [dx_own, next_three, prev_three, local_three, give, cotangent[0], summed, mid_turned, out_turned],
    )
    returned = lax.ppermute(send, "comp", [(0, 1), (1, 0)])
    adjoint = own + jnp.pad(returned, ((0, FIELDS - COUPLED), (0, 0)))
    opening = call(opening_kernel, [sds((9 * depth, HID), F32)], [opened, first_wide])[0]
    return estimate[None], adjoint[None], opening[None], central, closing


def solution(mesh):
    fine = Mesh(mesh.devices.reshape(2, 4, 8, 2, 2), ("comp",) + FACE)
    whole = P("comp", None, None)
    in_specs = (P("comp", None, FACE), P("comp", None, FACE), P(FACE), P()) + (whole,) * 6
    out_specs = (P("comp", None, FACE), P("comp", None, FACE), whole, P("comp", FACE), P("comp", FACE))

    return jax.shard_map(body, mesh=fine, in_specs=in_specs, out_specs=out_specs, check_vma=False)
```

```python
import jax
import jax.numpy as jnp
import numpy as np
from jax import lax
from jax.experimental import pallas as pl
from jax.experimental.pallas import tpu as pltpu
from jax.sharding import Mesh, PartitionSpec as P


FIELDS = 16
COUPLED = 8
TS = 16
CELLS = TS * TS
ROW = 4
ROWS = 32
TILES = ROW * ROWS
LINE = ROW * CELLS
HID = 256
PADC = 128
CHUNK = 24
SHARE = 16
DEPTH = FIELDS + COUPLED

GIVE = 0
TAKE = GIVE + LINE
FIRST_W = TAKE + LINE
OUT_BACK = FIRST_W + 9 * PADC
BANK_ONE = OUT_BACK + 9 * PADC
MID_W = 0
MID_BACK = MID_W + 9 * HID
MID_GATES = MID_BACK + 9 * HID
FIRST_GATES = MID_GATES + 9 * 64
OUT_GATES = FIRST_GATES + 5 * 64
BANK_TWO = OUT_GATES + 9 * 16
NARROW = 0
FIRST_WIDE = NARROW + 9 * HID
GIVE_OWN = FIRST_WIDE + 224
OWN_GATES = GIVE_OWN + CELLS
BANK_THREE = OWN_GATES + 32
BF = jnp.bfloat16
F32 = jnp.float32

FACE = ("y", "z", "xh", "core")
ROW_AXES = ("y", "z")
LINE_AXES = ("comp", "xh", "core")

EDGE_MAP = (
    ((0, False), (2, True), (1, True), (3, False)),
    ((1, False), (3, True), (0, True), (2, False)),
    ((2, False), (1, False), (3, True), (0, True)),
    ((3, False), (0, False), (2, True), (1, True)),
)

STRIPS = (
    [(col, 2, 8 + col) for col in range(4)]
    + [(3, 0, 8)]
    + [(col, 3, col) for col in range(4)]
    + [(0, 1, 3)]
    + [(col - 1, 0, 4 + col) for col in (1, 2, 3)]
    + [(col + 1, 1, 4 + col) for col in (0, 1, 2)]
)


def edge_line(slot, flip):
    first, step = ((TS - 1, TS), (0, TS), ((TS - 1) * TS, 1), (0, 1))[slot]
    if flip:
        first, step = first + (TS - 1) * step, -step
    return first, step


def dot(left, right):
    return jnp.dot(left, right, preferred_element_type=F32)


def dot_nt(left, right):
    return lax.dot_general(left, right, (((1,), (1,)), ((), ())), preferred_element_type=F32)


def dot_tn(left, right):
    return lax.dot_general(left, right, (((0,), (0,)), ((), ())), preferred_element_type=F32)


def dot_exact(left, right):
    high = right.astype(BF)
    rest = right - high.astype(F32)
    mid = rest.astype(BF)
    low = (rest - mid.astype(F32)).astype(BF)
    return dot(left, high) + (dot(left, mid) + dot(left, low))


def dot_exact_right(left, right):
    high = left.astype(BF)
    rest = left - high.astype(F32)
    mid = rest.astype(BF)
    low = (rest - mid.astype(F32)).astype(BF)
    return dot(high, right) + (dot(mid, right) + dot(low, right))


def fetch(sources, buffers, sems):
    copies = [
        pltpu.make_async_copy(source, buffer, sems.at[place])
        for place, (source, buffer) in enumerate(zip(sources, buffers))
    ]
    for copy in copies:
        copy.start()
    return copies


def one_hot(shape, axis, index):
    return (lax.broadcasted_iota(jnp.int32, shape, axis) == index).astype(F32).astype(BF)


def edge_spread(column):
    rows = lax.broadcasted_iota(jnp.int32, (CELLS, TS), 0)
    cols = lax.broadcasted_iota(jnp.int32, (CELLS, TS), 1)
    return (rows == cols * TS + column).astype(F32).astype(BF)


def edge_take(column):
    rows = lax.broadcasted_iota(jnp.int32, (TS, CELLS), 0)
    cols = lax.broadcasted_iota(jnp.int32, (TS, CELLS), 1)
    return (cols == rows * TS + column).astype(F32).astype(BF)


def shift_cells(value, step, axis):
    along = lax.broadcasted_iota(jnp.int32, value.shape, axis)
    moved = pltpu.roll(value, step % TS, axis)
    edge = 0 if step == 1 else TS - 1
    return jnp.where(along == edge, 0.0, moved)


def fill(out_ref, tiles, local, from_prev, from_next):
    depth = tiles.shape[1]
    spread_west, spread_east = edge_spread(0), edge_spread(TS - 1)
    for col in range(ROW):
        south = from_prev[TS * col : TS * (col + 1)]
        north = from_next[TS * col : TS * (col + 1)]
        west = from_prev[4 * TS : 5 * TS] if col == 0 else local[TS * (col - 1) : TS * col]
        east = from_next[4 * TS : 5 * TS] if col == 3 else local[TS * (3 + col) : TS * (4 + col)]
        own = tiles[CELLS * col : CELLS * (col + 1)]
        wide = own.astype(F32).reshape(TS, TS, depth)
        left = shift_cells(wide, 1, 1) + dot(spread_west, west).reshape(TS, TS, depth)
        right = shift_cells(wide, -1, 1) + dot(spread_east, east).reshape(TS, TS, depth)
        out_ref[col, 1 : TS + 1, :, 0:depth] = left.astype(BF)
        out_ref[col, 1 : TS + 1, :, depth : 2 * depth] = own.reshape(TS, TS, depth)
        out_ref[col, 1 : TS + 1, :, 2 * depth : 3 * depth] = right.astype(BF)
        for line, strip in ((0, south), (TS + 1, north)):
            wide = strip.astype(F32)
            out_ref[col, line, :, 0:depth] = shift_cells(wide, 1, 0).astype(BF)
            out_ref[col, line, :, depth : 2 * depth] = strip
            out_ref[col, line, :, 2 * depth : 3 * depth] = shift_cells(wide, -1, 0).astype(BF)


def take_strips(bank_ref, cells_ref):
    total = None
    for col in range(ROW):
        block = slice(TAKE + CELLS * col, TAKE + CELLS * (col + 1))
        piece = dot(bank_ref[block], cells_ref[CELLS * col : CELLS * (col + 1)])
        total = piece if total is None else total + piece
    return total.astype(BF)


def conv_tile(filled_ref, bank_ref, base, col, lanes=slice(None)):
    width = filled_ref.shape[3]
    total = None
    for a in range(3):
        weights = bank_ref[base + width * a : base + width * (a + 1), lanes]
        piece = dot(filled_ref[col, a : a + TS].reshape(CELLS, width), weights)
        total = piece if total is None else total + piece
    return total


def fold_tile(grad, bank_ref, base, lanes, pad_ref):
    deep = grad.shape[1]
    lines = grad.reshape(TS, TS, deep)
    for a in range(3):
        pad_ref[a : a + TS, :, deep * a : deep * (a + 1)] = lines
    padded = pad_ref[...].reshape((TS + 2) * TS, 3 * deep)
    left, mid, right = (
        dot(padded, bank_ref[base + 3 * deep * b : base + 3 * deep * (b + 1), lanes]) for b in range(3)
    )
    depth = mid.shape[1]
    left, mid, right = (part.reshape(TS + 2, TS, depth) for part in (left, mid, right))
    merged = mid + shift_cells(left, -1, 1) + shift_cells(right, 1, 1)
    inner = merged[1 : TS + 1].reshape(CELLS, depth)
    south = merged[0].astype(BF)
    north = merged[TS + 1].astype(BF)
    west = dot(edge_take(0), left[1 : TS + 1].reshape(CELLS, depth).astype(BF)).astype(BF)
    east = dot(edge_take(TS - 1), right[1 : TS + 1].reshape(CELLS, depth).astype(BF)).astype(BF)
    return inner, south, north, west, east


def fold_row(grad_of, bank_ref, base, lanes, pad_ref, inner_ref, prev_ref, next_ref, local_ref):
    pad_ref[...] = jnp.zeros_like(pad_ref)
    for col in range(ROW):
        inner, south, north, west, east = fold_tile(grad_of(col), bank_ref, base, lanes, pad_ref)
        inner_ref[CELLS * col : CELLS * (col + 1)] = inner
        prev_ref[TS * col : TS * (col + 1)] = south
        next_ref[TS * col : TS * (col + 1)] = north
        if col == 0:
            prev_ref[4 * TS : 5 * TS] = west
        else:
            local_ref[TS * (col - 1) : TS * col] = west
        if col == 3:
            next_ref[4 * TS : 5 * TS] = east
        else:
            local_ref[TS * (3 + col) : TS * (4 + col)] = east


def sigmoid(values):
    return 1.0 / (1.0 + jnp.exp(-values))


def slope(values):
    sig = sigmoid(values)
    return sig * (1.0 + values * (1.0 - sig))


UP = slice(0, 80)
DOWN = slice(80, 160)
LOCAL = slice(160, 256)


def keep_of(wide, lane):
    low = jnp.where(wide >= 4.5, 2, jnp.where(wide >= 2.5, 1, 0))
    high = jnp.where(wide < 0.5, 1, jnp.where((wide < 1.5) | ((wide > 2.5) & (wide < 3.5)), 2, 3))
    return lane == low, lane == high


def kept_pair(planes, gates):
    one, two, three, four = planes
    low = jnp.where(gates >= 4.5, three, jnp.where(gates >= 2.5, two, one))
    high = jnp.where(gates < 0.5, two, jnp.where((gates < 1.5) | ((gates > 2.5) & (gates < 3.5)), three, four))
    return low, high


def eye(rows, cols):
    return one_hot((rows, cols), 1, lax.broadcasted_iota(jnp.int32, (rows, cols), 0))


def repeat_four(groups, width):
    rows = lax.broadcasted_iota(jnp.int32, (groups, width), 0)
    cols = lax.broadcasted_iota(jnp.int32, (groups, width), 1)
    return ((cols >> 2) == rows).astype(F32).astype(BF)


def plane_order():
    rows = lax.broadcasted_iota(jnp.int32, (HID, HID), 0)
    return one_hot((HID, HID), 1, 4 * (rows & 63) + (rows >> 6))


def pack_kernel(state_hbm, cot_hbm, sea_hbm, out_ref, state_ref, cot_ref, sea_ref, sems):
    copies = fetch((state_hbm, cot_hbm, sea_hbm), (state_ref, cot_ref, sea_ref), sems)
    for copy in copies:
        copy.wait()
    comp = lax.axis_index("comp")
    weight = jnp.where(comp == 1, sea_ref[...].astype(F32), 1.0)
    grad = (weight * cot_ref[...].astype(F32)).astype(BF)
    for place in range(8):
        out_ref[place, 0:FIELDS] = state_ref[...]
        out_ref[place, FIELDS : 2 * FIELDS] = grad


def kept_rows(gates, kernel):
    outputs = kernel.shape[0]
    rows = lax.broadcasted_iota(jnp.int32, (outputs, outputs // 4), 0) >> 2
    wide = dot(one_hot((outputs, outputs // 4), 1, rows), gates)
    low, high = keep_of(wide, lax.broadcasted_iota(jnp.int32, wide.shape, 0) & 3)
    return jnp.where(low | high, kernel, 0.0)


def prepare_early_kernel(
    turn_hbm, first_gates_hbm, out_gates_hbm, first_hbm, out_hbm, bank_ref,
    turn_ref, first_gates_ref, out_gates_ref, first_ref, out_ref, sems,
):
    copies = fetch(
        (turn_hbm, first_gates_hbm, out_gates_hbm, first_hbm, out_hbm),
        (turn_ref, first_gates_ref, out_gates_ref, first_ref, out_ref), sems,
    )
    for copy in copies:
        copy.wait()
    row = lax.axis_index(ROW_AXES)
    strip_of = lax.broadcasted_iota(jnp.int32, (8, 256), 1) >> 4
    along = lax.broadcasted_iota(jnp.int32, (8, 256), 1) & 15
    cells = jnp.zeros((8, 256), jnp.int32)
    for number, (source, side, reader) in enumerate(STRIPS):
        turn = turn_ref[side, lax.rem(ROW * row + reader - ROW + TILES, TILES)]
        first, step = edge_line(*EDGE_MAP[side][3])
        for turns in range(3):
            one, two = edge_line(*EDGE_MAP[side][turns])
            first, step = jnp.where(turn == turns, one, first), jnp.where(turn == turns, two, step)
        first = first + source * CELLS
        cells = jnp.where(strip_of == number, first + step * along, cells)
        place = lax.broadcasted_iota(jnp.int32, (TS, LINE), 1)
        wanted = first + step * lax.broadcasted_iota(jnp.int32, (TS, LINE), 0)
        hit = (place == wanted).astype(F32).astype(BF)
        for col in range(ROW):
            at = TAKE + CELLS * col + TS * number
            bank_ref[at : at + TS] = hit[:, CELLS * col : CELLS * (col + 1)]
    bank_ref[GIVE : GIVE + LINE] = one_hot((LINE, 256), 0, cells[0:1])
    count = 9 * DEPTH
    wide = dot_tn(first_gates_ref[...].astype(F32).astype(BF), repeat_four(HID // 4, HID))
    low, high = keep_of(wide, lax.broadcasted_iota(jnp.int32, (count, HID), 1) & 3)
    kernel = jnp.where(low | high, first_ref[...].astype(F32), 0.0)
    blank = jnp.zeros((PADC - DEPTH, HID), F32)
    for tap in range(9):
        block = jnp.concatenate([kernel[DEPTH * tap : DEPTH * (tap + 1)], blank], 0)
        bank_ref[FIRST_W + PADC * tap : FIRST_W + PADC * (tap + 1)] = block.astype(BF)
        cols = slice(HID * tap, HID * (tap + 1))
        kernel_out = kept_rows(out_gates_ref[:, cols].astype(F32).astype(BF), out_ref[:, cols].astype(F32))
        kernel_out = jnp.concatenate([kernel_out, jnp.zeros((PADC - FIELDS, HID), F32)], 0)
        at = OUT_BACK + PADC * (3 * (tap % 3) + tap // 3)
        bank_ref[at : at + PADC] = kernel_out.astype(BF)


def prepare_late_kernel(
    early_ref, first_gates_hbm, mid_gates_hbm, out_gates_hbm, mid_hbm, two_ref, three_ref,
    first_gates_ref, mid_gates_ref, out_gates_ref, mid_ref, sems,
):
    copies = fetch(
        (first_gates_hbm, mid_gates_hbm, out_gates_hbm, mid_hbm),
        (first_gates_ref, mid_gates_ref, out_gates_ref, mid_ref), sems,
    )
    col = lax.axis_index(("xh", "core"))
    tile = lax.axis_index(FACE)
    three_ref[GIVE_OWN : GIVE_OWN + CELLS] = early_ref[pl.ds(pl.multiple_of(GIVE + CELLS * col, CELLS), CELLS)]
    for a in range(3):
        for b in range(3):
            tap = 3 * a + b
            block = early_ref[FIRST_W + PADC * tap : FIRST_W + PADC * (tap + 1)]
            at = NARROW + HID * (3 * b + a)
            three_ref[at : at + HID, :PADC] = dot_nt(eye(HID, HID), block).astype(BF)
            at = OUT_BACK + PADC * (3 * b + a)
            block = early_ref[at : at + PADC]
            at = NARROW + HID * tap
            three_ref[at : at + HID, PADC:] = dot_tn(block, eye(PADC, PADC)).astype(BF)
    for copy in copies:
        copy.wait()
    count = 9 * DEPTH
    gates = first_gates_ref[...].astype(F32).astype(BF)
    three_ref[FIRST_WIDE : FIRST_WIDE + count] = dot_tn(gates, repeat_four(HID // 4, HID)).astype(BF)
    place = lax.broadcasted_iota(jnp.int32, (count, 9 * PADC), 0)
    tap = (place * 2731) >> 16
    spread = dot(gates, one_hot((count, 9 * PADC), 1, tap * PADC + place - DEPTH * tap)).astype(BF)
    for b in range(4):
        two_ref[FIRST_GATES + 64 * b : FIRST_GATES + 64 * (b + 1)] = spread[:, HID * b : HID * (b + 1)]
    two_ref[FIRST_GATES + 256 : FIRST_GATES + 320, :PADC] = spread[:, 4 * HID :]
    place = lax.broadcasted_iota(jnp.int32, (32, 9 * HID), 0)
    mine = one_hot((32, 9 * HID), 1, jnp.where(place < 18, 18 * tile + place, -1))
    gates = mid_gates_ref[...].astype(F32).astype(BF)
    three_ref[OWN_GATES : OWN_GATES + 32, :64] = dot_nt(mine, gates).astype(BF)
    out_gates = dot(eye(PADC, 4), out_gates_ref[...].astype(F32).astype(BF)).astype(BF)
    three_ref[OWN_GATES : OWN_GATES + 32, PADC:] = dot_nt(mine, out_gates).astype(BF)
    for a in range(3):
        for b in range(3):
            tap = 3 * a + b
            cols = slice(HID * tap, HID * (tap + 1))
            two_ref[MID_GATES + 64 * tap : MID_GATES + 64 * (tap + 1)] = gates[:, cols]
            turned = kept_rows(gates[:, cols], dot_nt(eye(HID, HID), mid_ref[cols])).astype(BF)
            at = MID_BACK + HID * (3 * b + a)
            two_ref[at : at + HID] = turned
            at = MID_W + HID * tap
            two_ref[at : at + HID] = dot_tn(turned, eye(HID, HID)).astype(BF)
            two_ref[OUT_GATES + 16 * tap : OUT_GATES + 16 * (tap + 1)] = out_gates[:16, cols]


def bank_gates(bank_ref, base, rows, blocks):
    step = max(rows, 16)
    return jnp.concatenate(
        [bank_ref[base + step * b : base + step * (b + 1)][:rows] for b in blocks], 1
    )


def start_kernel(line_ref, bank_ref, field_ref, grad_ref, strips_ref):
    comp = lax.axis_index("comp")
    for col in range(ROW):
        own = line_ref[comp, col].astype(F32)
        other = line_ref[1 - comp, col][:FIELDS].astype(F32)[:COUPLED]
        blank = jnp.zeros((PADC - FIELDS - COUPLED, CELLS), F32)
        field = jnp.concatenate([own[:FIELDS], other, blank], 0)
        field_ref[CELLS * col : CELLS * (col + 1)] = field.T.astype(BF)
        blank = jnp.zeros((PADC - FIELDS, CELLS), F32)
        grad = jnp.concatenate([own[FIELDS:], blank], 0)
        grad_ref[CELLS * col : CELLS * (col + 1)] = grad.T.astype(BF)
    strips_ref[...] = take_strips(bank_ref, field_ref)


def send_strips(strips, up_ref, down_ref, local_ref):
    up_ref[0:80] = strips[UP]
    down_ref[0:80] = strips[DOWN]
    local_ref[0:96] = strips[LOCAL]


def back_strips(prev_ref, next_ref, local_ref):
    return jnp.concatenate([next_ref[80:160], prev_ref[80:160], local_ref[96:192]], 0)


def layer_one_kernel(
    field_ref, strips_ref, prev_ref, next_ref, grad_ref, bank_ref,
    filled_ref, act_ref, hid_ref, local_ref, up_ref, down_ref, inner_ref,
    pad_ref,
):
    fill(filled_ref, field_ref[...], strips_ref[LOCAL], prev_ref[...], next_ref[...])
    for col in range(ROW):
        act = conv_tile(filled_ref, bank_ref, FIRST_W, col)
        act_ref[CELLS * col : CELLS * (col + 1)] = act
        hid_ref[CELLS * col : CELLS * (col + 1)] = (act * sigmoid(act)).astype(BF)
    send_strips(take_strips(bank_ref, hid_ref), up_ref, down_ref, local_ref)
    fold_row(
        lambda col: grad_ref[CELLS * col : CELLS * (col + 1)],
        bank_ref, OUT_BACK, slice(None), pad_ref, inner_ref, down_ref.at[80:160], up_ref.at[80:160], local_ref.at[96:192],
    )


def layer_two_kernel(
    hid_ref, local_in_ref, prev_ref, next_ref, inner_two_ref, early_ref, bank_ref,
    filled_ref, grad_ref, hid_two_ref, local_ref, up_ref, down_ref, inner_ref,
    pad_ref,
):
    fill(filled_ref, hid_ref[...], local_in_ref[0:96], prev_ref[0:80], next_ref[0:80])
    strips = back_strips(prev_ref, next_ref, local_in_ref)
    for col in range(ROW):
        rows = slice(CELLS * col, CELLS * (col + 1))
        grad_hid = inner_two_ref[rows] + dot(early_ref[rows], strips)
        act = conv_tile(filled_ref, bank_ref, MID_W, col)
        sig = sigmoid(act)
        hid_two_ref[rows] = (act * sig).astype(BF)
        grad_ref[rows] = (grad_hid * (sig * (1.0 + act * (1.0 - sig)))).astype(BF)
    send_strips(take_strips(early_ref, hid_two_ref), up_ref, down_ref, local_ref)
    fold_row(
        lambda col: grad_ref[CELLS * col : CELLS * (col + 1)],
        bank_ref, MID_BACK, slice(None), pad_ref, inner_ref, down_ref.at[80:160], up_ref.at[80:160], local_ref.at[96:192],
    )


def gather_rows(filled_ref, a):
    return jnp.concatenate(
        [filled_ref[col, a : a + TS].reshape(CELLS, filled_ref.shape[3]) for col in range(ROW)], 0
    )


def term_pairs(filled_ref, grad, gates_of, flat_ref):
    turned = dot_nt(plane_order(), grad).astype(BF)
    width = filled_ref.shape[3]
    for a in range(3):
        cols = slice(width * a, width * (a + 1))
        term = dot(turned, gather_rows(filled_ref, a))
        low, high = kept_pair([term[64 * m : 64 * (m + 1)] for m in range(4)], gates_of(a).astype(F32))
        flat_ref[0:64, cols] = low.astype(BF)
        flat_ref[64:128, cols] = high.astype(BF)


def mid_term_kernel(filled_ref, grad_ref, bank_ref, part_ref, pick_out_ref, pick_first_ref, flat_ref):
    col = lax.axis_index(("xh", "core"))
    term_pairs(
        filled_ref, grad_ref[...], lambda a: bank_gates(bank_ref, MID_GATES, 64, range(3 * a, 3 * a + 3)), flat_ref
    )
    shape = (16 * CHUNK, 1152)
    place = lax.broadcasted_iota(jnp.int32, shape, 0)
    block = (place * 2731) >> 16
    inside = place - CHUNK * block
    ahead = lax.broadcasted_iota(jnp.int32, shape, 1) - (72 * block + 18 * col)
    pick = ((ahead == inside) & (inside < 18)).astype(F32).astype(BF)
    late = ahead - 9 * (inside - 18)
    pick_out_ref[...] = ((late >= 0) & (late < 9) & (inside >= 18) & (inside < 20)).astype(F32).astype(BF)
    shape = (4 * SHARE, 1152)
    place = lax.broadcasted_iota(jnp.int32, shape, 0)
    inside = place & 15
    wanted = 14 * (4 * (place >> 4) + col) + inside
    tap = (wanted * 2731) >> 16
    target = tap * PADC + wanted - (FIELDS + COUPLED) * tap
    real = (inside < 14) & (wanted < 9 * (FIELDS + COUPLED))
    pick_first_ref[...] = ((lax.broadcasted_iota(jnp.int32, shape, 1) == target) & real).astype(F32).astype(BF)
    for half in range(2):
        part_ref[16 * CHUNK * half : 16 * CHUNK * (half + 1)] = dot_nt(
            pick, flat_ref[:, 1152 * half : 1152 * (half + 1)]
        )


def terms_kernel(
    hid_two_ref, local_ref, prev_ref, next_ref, inner_ref, act_ref, filled_zero_ref, grad_three_ref, early_ref, bank_ref,
    part_ref, pick_out_ref, pick_first_ref,
    buffer_ref, mine_ref, grad_ref,
    filled_ref, flat_ref, flat_zero_ref,
):
    fill(filled_ref, hid_two_ref[...], local_ref[0:96], prev_ref[0:80], next_ref[0:80])
    strips = back_strips(prev_ref, next_ref, local_ref)
    for col in range(ROW):
        rows = slice(CELLS * col, CELLS * (col + 1))
        grad_hid = inner_ref[rows] + dot(early_ref[rows], strips)
        grad_ref[rows] = (grad_hid * slope(act_ref[rows])).astype(BF)
    place = lax.broadcasted_iota(jnp.int32, (32, PADC), 0)
    group = place & 7
    wanted = jnp.where(group < 4, 4 * group + (place >> 3), -1)
    turned = dot_nt(one_hot((32, PADC), 1, wanted), grad_three_ref[...]).astype(BF)
    width = filled_ref.shape[3]
    for a in range(3):
        cols = slice(width * a, width * (a + 1))
        term = dot(turned, gather_rows(filled_ref, a))
        gates = bank_gates(bank_ref, OUT_GATES, 16, range(3 * a, 3 * a + 3)).astype(F32)[:8]
        low, high = kept_pair([term[8 * m : 8 * (m + 1)] for m in range(4)], gates)
        pair = low + pltpu.roll(high, 4, 0)
        wide = jnp.broadcast_to(pair[None], (16, 8, width)).reshape(128, width)
        kernel_row = lax.broadcasted_iota(jnp.int32, (128, width), 1) + width * a
        slot = kernel_row - 9 * ((kernel_row * 7282) >> 16)
        mine = (lax.broadcasted_iota(jnp.int32, (128, width), 0) >> 3) == slot
        flat_ref[:, cols] = jnp.where(mine, wide, 0.0).astype(BF)
    gates = jnp.concatenate(
        [bank_ref[FIRST_GATES + 64 * b : FIRST_GATES + 64 * (b + 1)] for b in range(4)]
        + [bank_ref[FIRST_GATES + 256 : FIRST_GATES + 320, :PADC]], 1,
    )
    term_pairs(
        filled_zero_ref, grad_ref[...], lambda a: gates[:, 3 * PADC * a : 3 * PADC * (a + 1)], flat_zero_ref
    )
    for half in range(2):
        rows = slice(16 * CHUNK * half, 16 * CHUNK * (half + 1))
        part = part_ref[rows] + dot_nt(pick_out_ref[...], flat_ref[:, 1152 * half : 1152 * (half + 1)])
        buffer_ref[16 * half : 16 * (half + 1), 0:CHUNK] = part.astype(BF).reshape(16, CHUNK, PADC)
    mine_ref[...] = filled_ref[lax.axis_index(("xh", "core"))]
    share = dot_nt(pick_first_ref[...], flat_zero_ref[...]).astype(BF)
    for place in range(ROWS):
        kind = place // 8
        buffer_ref[place, CHUNK : CHUNK + SHARE] = share[SHARE * kind : SHARE * (kind + 1)]


def last_kernel(
    mine_ref, grad_ref, bank_ref, state_ref, sea_ref,
    estimate_ref, dx_ref, up_ref, down_ref, local_ref,
    pad_ref, dx_all_ref,
):
    comp = lax.axis_index("comp")
    col = lax.axis_index(("xh", "core"))
    width = mine_ref.shape[2]
    fold_row(
        lambda col: grad_ref[CELLS * col : CELLS * (col + 1)],
        bank_ref, NARROW, slice(0, PADC), pad_ref, dx_all_ref, down_ref, up_ref, local_ref,
    )
    dx_ref[...] = dx_all_ref[pl.ds(pl.multiple_of(col * CELLS, CELLS), CELLS)]
    total = None
    for a in range(3):
        weights = bank_ref[NARROW + width * a : NARROW + width * (a + 1), PADC:]
        piece = dot(mine_ref[a : a + TS].reshape(CELLS, width), weights)
        total = piece if total is None else total + piece
    weight = jnp.where(comp == 1, sea_ref[...].astype(F32), 1.0)
    estimate_ref[...] = (state_ref[...].astype(F32) + weight * total.T[:FIELDS]).astype(BF)


def sum_kernel(spread_ref, share_ref, sum_ref):
    total = spread_ref[0].astype(F32)
    for place in range(1, ROWS):
        total = total + spread_ref[place].astype(F32)
    sum_ref[...] = total[:CHUNK]
    share = total[CHUNK:].astype(BF)
    for place in range(16):
        share_ref[place] = share


def finish_kernel(
    dx_ref, next_ref, prev_ref, local_ref, bank_ref, cot_ref, sum_ref,
    own_ref, send_ref, central_ref, closing_ref,
):
    give = bank_ref[GIVE_OWN : GIVE_OWN + CELLS]
    strips = jnp.concatenate([next_ref[...], prev_ref[...], local_ref[...]], 0)
    total = (dx_ref[...] + dot(give, strips)).T
    own_ref[...] = cot_ref[...].astype(F32) + total[:FIELDS]
    send_ref[...] = total[FIELDS : FIELDS + COUPLED]
    sums = sum_ref[...]
    repeat = repeat_four(HID // 4, HID)
    wide = dot(bank_ref[OWN_GATES : OWN_GATES + 32, :64], repeat)[:CHUNK]
    low, high = keep_of(wide, lax.broadcasted_iota(jnp.int32, (CHUNK, HID), 1) & 3)
    lows, highs = dot_exact_right(sums[:, :64], repeat), dot_exact_right(sums[:, 64:], repeat)
    central = jnp.where(low, lows, jnp.where(high, highs, 0.0))
    for line in range(18):
        central_ref[:, HID * line : HID * (line + 1)] = central[line : line + 1]
    place = lax.broadcasted_iota(jnp.int32, (CHUNK, CHUNK), 0)
    late = (place >= 9).astype(jnp.int32)
    spread = dot_exact(one_hot((CHUNK, CHUNK), 1, 18 + late), sums)
    place = lax.broadcasted_iota(jnp.int32, (CHUNK, PADC), 0)
    slot = place - 9 * (place >= 9).astype(jnp.int32)
    lane = lax.broadcasted_iota(jnp.int32, (CHUNK, PADC), 1)
    spread = jnp.where((lane >> 3) == slot, spread, 0.0)
    flat = 3 * PADC
    from_lane = lax.broadcasted_iota(jnp.int32, (PADC, flat), 0) & 7
    group = (lax.broadcasted_iota(jnp.int32, (PADC, flat), 1) & 15) >> 2
    lows = dot_exact_right(spread, (from_lane == group).astype(F32).astype(BF))
    highs = dot_exact_right(spread, (from_lane == group + 4).astype(F32).astype(BF))
    group = (lax.broadcasted_iota(jnp.int32, (PADC, flat), 1) & 15) >> 2
    wide = dot(bank_ref[OWN_GATES : OWN_GATES + 32, PADC:], one_hot((PADC, flat), 0, group))[:CHUNK]
    lane = lax.broadcasted_iota(jnp.int32, (CHUNK, flat), 1)
    low, high = keep_of(wide, lane & 3)
    closing = jnp.where(low, lows, jnp.where(high, highs, 0.0))
    here = lax.broadcasted_iota(jnp.int32, (CHUNK, flat), 0) == (lane >> 4)
    closing_ref[...] = jnp.sum(jnp.where(here, closing, 0.0), 0, keepdims=True)[:, : 18 * FIELDS]


def opening_kernel(share_ref, bank_ref, out_ref):
    count = 9 * (FIELDS + COUPLED)
    wanted = lax.broadcasted_iota(jnp.int32, (count, 16 * SHARE), 0)
    block = (wanted * 4682) >> 16
    pick = one_hot((count, 16 * SHARE), 1, SHARE * block + wanted - 14 * block)
    pairs = dot(pick, share_ref[...]).astype(BF)
    repeat = repeat_four(HID // 4, HID)
    low, high = keep_of(bank_ref[FIRST_WIDE : FIRST_WIDE + count].astype(F32), lax.broadcasted_iota(jnp.int32, (count, HID), 1) & 3)
    out_ref[...] = jnp.where(low, dot(pairs[:, :64], repeat), jnp.where(high, dot(pairs[:, 64:], repeat), 0.0))


VMEM = pl.BlockSpec(memory_space=pltpu.VMEM)
SMEM = pl.BlockSpec(memory_space=pltpu.SMEM)
HBM = pl.BlockSpec(memory_space=pltpu.HBM)


def call(body, out, args, scratch=(), scalars=(), far=(), flops=0, limit=10):
    args = [pltpu.with_memory_space_constraint(arg, pltpu.HBM) if place in far else arg for place, arg in enumerate(args)]
    specs = [SMEM if place in scalars else HBM if place in far else VMEM for place in range(len(args))]
    size = sum(int(np.prod(item.shape)) * item.dtype.itemsize for item in list(args) + list(out))
    return pl.pallas_call(
        body,
        out_shape=[jax.ShapeDtypeStruct(item.shape, item.dtype) for item in out],
        in_specs=specs,
        out_specs=[VMEM] * len(out),
        scratch_shapes=list(scratch),
        compiler_params=pltpu.CompilerParams(vmem_limit_bytes=limit * 1024 * 1024),
        cost_estimate=pl.CostEstimate(flops=flops, bytes_accessed=size, transcendentals=0),
    )(*args)


def sds(shape, kind):
    return jax.ShapeDtypeStruct(shape, kind)


def row_shift(value, step):
    pairs = [(face, (face + ROW * step) % TILES) for face in range(TILES)]
    return lax.ppermute(value, FACE, pairs)


def body(
    state, cotangent, land_sea, turn_table, first_kernel, mid_kernel, out_kernel, first_gates, mid_gates, out_gates
):
    sea = land_sea.reshape(1, CELLS)

    packed = call(pack_kernel, [sds((8, 2 * FIELDS, CELLS), BF)], [state[0], cotangent[0], sea],
        scratch=[
            pltpu.VMEM((FIELDS, CELLS), BF), pltpu.VMEM((FIELDS, CELLS), BF), pltpu.VMEM((1, CELLS), jnp.int32),
            pltpu.SemaphoreType.DMA((3,)),
        ],
        far=(0, 1, 2),
    )[0]
    line = lax.all_to_all(packed, LINE_AXES, 0, 0).reshape(2, ROW, 2 * FIELDS, CELLS)

    turns, out_turned = turn_table.T, out_gates[0].T
    first_turned, mid_turned = first_gates[0].T, mid_gates[0].T
    early = call(
        prepare_early_kernel, [sds((BANK_ONE, HID), BF)],
        [turns, first_turned, out_turned, first_kernel[0], out_kernel[0].T],
        scratch=[
            pltpu.SMEM((4, TILES), jnp.int32), pltpu.VMEM((64, 9 * DEPTH), jnp.int32),
            pltpu.VMEM((4, 9 * HID), jnp.int32), pltpu.VMEM((9 * DEPTH, HID), BF),
            pltpu.VMEM((FIELDS, 9 * HID), BF), pltpu.SemaphoreType.DMA((5,)),
        ],
        far=(0, 1, 2, 3, 4), flops=5 * 10**9,
    )[0]

    field, grad_cells, strips_zero = call(
        start_kernel,
        [sds((LINE, PADC), BF), sds((LINE, PADC), BF), sds((256, PADC), BF)], [line, early],
    )
    prev_zero = row_shift(strips_zero[UP], 1)
    next_zero = row_shift(strips_zero[DOWN], -1)
    two, three = call(
        prepare_late_kernel, [sds((BANK_TWO, HID), BF), sds((BANK_THREE, HID), BF)],
        [early, first_turned, mid_turned, out_turned, mid_kernel[0]],
        scratch=[
            pltpu.VMEM((64, 9 * DEPTH), jnp.int32), pltpu.VMEM((64, 9 * HID), jnp.int32),
            pltpu.VMEM((4, 9 * HID), jnp.int32), pltpu.VMEM((9 * HID, HID), BF), pltpu.SemaphoreType.DMA((4,)),
        ],
        far=(1, 2, 3, 4), flops=3 * 10**9,
    )

    exchange = [sds((192, HID), BF), sds((160, HID), BF), sds((160, HID), BF), sds((LINE, HID), F32)]
    filled_zero, act_one, hid_one, local_one, up_one, down_one, inner_two = call(
        layer_one_kernel,
        [sds((ROW, TS + 2, TS, 3 * PADC), BF), sds((LINE, HID), F32), sds((LINE, HID), BF)] + exchange,
        [field, strips_zero, prev_zero, next_zero, grad_cells, early],
        scratch=[pltpu.VMEM((TS + 2, TS, 3 * PADC), BF)],
    )
    prev_one = row_shift(up_one, 1)
    next_one = row_shift(down_one, -1)

    filled_one, grad_two, hid_two, local_two, up_two, down_two, inner_one = call(
        layer_two_kernel,
        [sds((ROW, TS + 2, TS, 3 * HID), BF), sds((LINE, HID), BF), sds((LINE, HID), BF)] + exchange,
        [hid_one, local_one, prev_one, next_one, inner_two, early, two],
        scratch=[pltpu.VMEM((TS + 2, TS, 3 * HID), BF)],
    )
    prev_two = row_shift(up_two, 1)
    next_two = row_shift(down_two, -1)

    part, pick_out, pick_first = call(
        mid_term_kernel,
        [sds((32 * CHUNK, PADC), F32), sds((16 * CHUNK, 1152), BF), sds((4 * SHARE, 1152), BF)],
        [filled_one, grad_two, two],
        scratch=[pltpu.VMEM((PADC, 9 * HID), BF)], flops=2 * 10**9,
    )

    buffer, mine_two, grad_one = call(
        terms_kernel,
        [sds((ROWS, CHUNK + SHARE, PADC), BF), sds((TS + 2, TS, 3 * HID), BF), sds((LINE, HID), BF)],
        [hid_two, local_two, prev_two, next_two, inner_one, act_one, filled_zero, grad_cells, early, two,
         part, pick_out, pick_first],
        scratch=[
            pltpu.VMEM((ROW, TS + 2, TS, 3 * HID), BF), pltpu.VMEM((PADC, 9 * HID), BF),
            pltpu.VMEM((PADC, 9 * PADC), BF),
        ],
    )
    spread = lax.all_to_all(buffer, ROW_AXES, 0, 0)

    estimate, dx_own, up_three, down_three, local_three = call(
        last_kernel,
        [sds((FIELDS, CELLS), BF), sds((CELLS, PADC), F32), sds((80, PADC), BF), sds((80, PADC), BF),
         sds((96, PADC), BF)],
        [mine_two, grad_one, three, state[0], sea],
        scratch=[pltpu.VMEM((TS + 2, TS, 3 * HID), BF), pltpu.VMEM((LINE, PADC), F32)], flops=2 * 10**9,
    )
    prev_three = row_shift(up_three, 1)
    next_three = row_shift(down_three, -1)

    shared, summed = call(sum_kernel, [sds((16, SHARE, PADC), BF), sds((CHUNK, PADC), F32)], [spread])
    opened = lax.all_to_all(shared, ("y", "xh", "core"), 0, 0).reshape(16 * SHARE, PADC)

    own, send, central, closing = call(
        finish_kernel,
        [sds((FIELDS, CELLS), F32), sds((COUPLED, CELLS), F32), sds((1, 18 * HID), F32), sds((1, 18 * FIELDS), F32)],
        [dx_own, next_three, prev_three, local_three, three, cotangent[0], summed],
    )
    returned = lax.ppermute(send, "comp", [(0, 1), (1, 0)])
    adjoint = own + jnp.pad(returned, ((0, FIELDS - COUPLED), (0, 0)))
    opening = call(opening_kernel, [sds((9 * DEPTH, HID), F32)], [opened, three])[0]
    return estimate[None], adjoint[None], opening[None], central, closing


def solution(mesh):
    fine = Mesh(mesh.devices.reshape(2, 4, 8, 2, 2), ("comp",) + FACE)
    whole = P("comp", None, None)
    in_specs = (P("comp", None, FACE), P("comp", None, FACE), P(FACE), P()) + (whole,) * 6
    out_specs = (P("comp", None, FACE), P("comp", None, FACE), whole, P("comp", FACE), P("comp", FACE))

    return jax.shard_map(body, mesh=fine, in_specs=in_specs, out_specs=out_specs, check_vma=False)
```

```python
import jax
import jax.numpy as jnp
import numpy as np
from jax import lax
from jax.experimental import pallas as pl
from jax.experimental.pallas import tpu as pltpu
from jax.sharding import Mesh, PartitionSpec as P


FIELDS = 16
COUPLED = 8
TS = 16
CELLS = TS * TS
ROW = 4
ROWS = 32
TILES = ROW * ROWS
LINE = ROW * CELLS
HID = 256
PADC = 128
CHUNK = 24
SHARE = 16
DEPTH = FIELDS + COUPLED

GIVE = 0
TAKE = GIVE + LINE
FIRST_W = TAKE + LINE
OUT_BACK = FIRST_W + 3 * PADC
MID_BACK = OUT_BACK + 3 * PADC
MID_GATES = MID_BACK + 9 * HID
BANK_ONE = MID_GATES + 9 * 64
MID_W = 0
FIRST_GATES = MID_W + 9 * HID
OUT_GATES = FIRST_GATES + 2 * 64
BANK_TWO = OUT_GATES + 9 * 16
LAST_W = 0
FIRST_WIDE = LAST_W + 6 * PADC
GIVE_OWN = FIRST_WIDE + 224
OWN_GATES = GIVE_OWN + CELLS
BANK_THREE = OWN_GATES + 32
BF = jnp.bfloat16
F32 = jnp.float32

FACE = ("y", "z", "xh", "core")
ROW_AXES = ("y", "z")
LINE_AXES = ("comp", "xh", "core")

EDGE_MAP = (
    ((0, False), (2, True), (1, True), (3, False)),
    ((1, False), (3, True), (0, True), (2, False)),
    ((2, False), (1, False), (3, True), (0, True)),
    ((3, False), (0, False), (2, True), (1, True)),
)

STRIPS = (
    [(col, 2, 8 + col) for col in range(4)]
    + [(3, 0, 8)]
    + [(col, 3, col) for col in range(4)]
    + [(0, 1, 3)]
    + [(col - 1, 0, 4 + col) for col in (1, 2, 3)]
    + [(col + 1, 1, 4 + col) for col in (0, 1, 2)]
)


def edge_line(slot, flip):
    first, step = ((TS - 1, TS), (0, TS), ((TS - 1) * TS, 1), (0, 1))[slot]
    if flip:
        first, step = first + (TS - 1) * step, -step
    return first, step


def dot(left, right):
    return jnp.dot(left, right, preferred_element_type=F32)


def dot_nt(left, right):
    return lax.dot_general(left, right, (((1,), (1,)), ((), ())), preferred_element_type=F32)


def dot_tn(left, right):
    return lax.dot_general(left, right, (((0,), (0,)), ((), ())), preferred_element_type=F32)


def dot_exact(left, right):
    high = right.astype(BF)
    rest = right - high.astype(F32)
    mid = rest.astype(BF)
    low = (rest - mid.astype(F32)).astype(BF)
    return dot(left, high) + (dot(left, mid) + dot(left, low))


def dot_exact_right(left, right):
    high = left.astype(BF)
    rest = left - high.astype(F32)
    mid = rest.astype(BF)
    low = (rest - mid.astype(F32)).astype(BF)
    return dot(high, right) + (dot(mid, right) + dot(low, right))


def fetch(sources, buffers, sems):
    copies = [
        pltpu.make_async_copy(source, buffer, sems.at[place])
        for place, (source, buffer) in enumerate(zip(sources, buffers))
    ]
    for copy in copies:
        copy.start()
    return copies


def one_hot(shape, axis, index):
    return (lax.broadcasted_iota(jnp.int32, shape, axis) == index).astype(F32).astype(BF)


def shift_cells(value, step, axis):
    along = lax.broadcasted_iota(jnp.int32, value.shape, axis)
    moved = pltpu.roll(value, step % TS, axis)
    edge = 0 if step == 1 else TS - 1
    return jnp.where(along == edge, 0.0, moved)


def shift_lines(lines, step, strip):
    along = lax.broadcasted_iota(jnp.int32, lines.shape, 1)
    moved = pltpu.roll(lines, step % TS, 1)
    edge = 0 if step == 1 else TS - 1
    return jnp.where(along == edge, jnp.broadcast_to(strip.astype(F32)[:, None, :], lines.shape), moved)


def fill(out_ref, tiles, local, from_prev, from_next):
    depth = tiles.shape[1]
    for col in range(ROW):
        south = from_prev[TS * col : TS * (col + 1)]
        north = from_next[TS * col : TS * (col + 1)]
        west = from_prev[4 * TS : 5 * TS] if col == 0 else local[TS * (col - 1) : TS * col]
        east = from_next[4 * TS : 5 * TS] if col == 3 else local[TS * (3 + col) : TS * (4 + col)]
        own = tiles[CELLS * col : CELLS * (col + 1)]
        wide = own.astype(F32).reshape(TS, TS, depth)
        left = shift_lines(wide, 1, west)
        right = shift_lines(wide, -1, east)
        out_ref[col, 1 : TS + 1, :, 0:depth] = left.astype(BF)
        out_ref[col, 1 : TS + 1, :, depth : 2 * depth] = own.reshape(TS, TS, depth)
        out_ref[col, 1 : TS + 1, :, 2 * depth : 3 * depth] = right.astype(BF)
        for line, strip in ((0, south), (TS + 1, north)):
            wide = strip.astype(F32)
            out_ref[col, line, :, 0:depth] = shift_cells(wide, 1, 0).astype(BF)
            out_ref[col, line, :, depth : 2 * depth] = strip
            out_ref[col, line, :, 2 * depth : 3 * depth] = shift_cells(wide, -1, 0).astype(BF)


def fill_packed(out_ref, tiles, local, from_prev, from_next):
    def choose(left, own, right):
        lane = lax.broadcasted_iota(jnp.int32, own.shape, own.ndim - 1)
        return jnp.where(lane < 32, left, jnp.where(lane < 64, own, right)).astype(BF)

    for col in range(ROW):
        south = from_prev[TS * col : TS * (col + 1)]
        north = from_next[TS * col : TS * (col + 1)]
        west = from_prev[4 * TS : 5 * TS] if col == 0 else local[TS * (col - 1) : TS * col]
        east = from_next[4 * TS : 5 * TS] if col == 3 else local[TS * (3 + col) : TS * (4 + col)]
        wide = tiles[CELLS * col : CELLS * (col + 1)].astype(F32).reshape(TS, TS, PADC)
        left = shift_lines(wide, 1, west)
        right = shift_lines(wide, -1, east)
        out_ref[col, 1 : TS + 1] = choose(left, wide, right)
        for line, strip in ((0, south), (TS + 1, north)):
            wide = strip.astype(F32)
            out_ref[col, line] = choose(shift_cells(wide, 1, 0), wide, shift_cells(wide, -1, 0))


def take_strips(bank_ref, cells_ref):
    total = None
    for col in range(ROW):
        block = slice(TAKE + CELLS * col, TAKE + CELLS * (col + 1))
        piece = dot(bank_ref[block], cells_ref[CELLS * col : CELLS * (col + 1)])
        total = piece if total is None else total + piece
    return total.astype(BF)


def conv_tile(filled_ref, bank_ref, base, col, lanes=slice(None)):
    width = filled_ref.shape[3]
    total = None
    for a in range(3):
        weights = bank_ref[base + width * a : base + width * (a + 1), lanes]
        piece = dot(filled_ref[col, a : a + TS].reshape(CELLS, width), weights)
        total = piece if total is None else total + piece
    return total


def pad_lines(grad, pad_ref):
    deep = grad.shape[1]
    lines = grad.reshape(TS, TS, deep)
    for a in range(3):
        pad_ref[a : a + TS, :, deep * a : deep * (a + 1)] = lines
    return pad_ref[...].reshape((TS + 2) * TS, 3 * deep)


def pad_lines_packed(grad):
    lines = grad.astype(F32).reshape(TS, TS, PADC)
    blank = jnp.zeros((1, TS, PADC), F32)
    lane = lax.broadcasted_iota(jnp.int32, (TS + 2, TS, PADC), 2)
    one, two, three = (
        jnp.concatenate([blank] * a + [lines] + [blank] * (2 - a), 0) for a in range(3)
    )
    padded = jnp.where(lane < 16, one, jnp.where(lane < 32, two, three))
    return padded.reshape((TS + 2) * TS, PADC).astype(BF)


def fold_tile(padded, bank_ref, base, lanes):
    deep = padded.shape[1]
    left, mid, right = (
        dot(padded, bank_ref[base + deep * b : base + deep * (b + 1), lanes]) for b in range(3)
    )
    depth = mid.shape[1]
    left, mid, right = (part.reshape(TS + 2, TS, depth) for part in (left, mid, right))
    merged = mid + shift_cells(left, -1, 1) + shift_cells(right, 1, 1)
    inner = merged[1 : TS + 1].reshape(CELLS, depth)
    south = merged[0].astype(BF)
    north = merged[TS + 1].astype(BF)
    west = left[1 : TS + 1, 0, :].astype(BF)
    east = right[1 : TS + 1, TS - 1, :].astype(BF)
    return inner, south, north, west, east


def fold_row(padded_of, bank_ref, base, lanes, inner_ref, prev_ref, next_ref, local_ref):
    for col in range(ROW):
        inner, south, north, west, east = fold_tile(padded_of(col), bank_ref, base, lanes)
        inner_ref[CELLS * col : CELLS * (col + 1)] = inner
        prev_ref[TS * col : TS * (col + 1)] = south
        next_ref[TS * col : TS * (col + 1)] = north
        if col == 0:
            prev_ref[4 * TS : 5 * TS] = west
        else:
            local_ref[TS * (col - 1) : TS * col] = west
        if col == 3:
            next_ref[4 * TS : 5 * TS] = east
        else:
            local_ref[TS * (3 + col) : TS * (4 + col)] = east


def sigmoid(values):
    return 1.0 / (1.0 + jnp.exp(-values))


def slope(values):
    sig = sigmoid(values)
    return sig * (1.0 + values * (1.0 - sig))


UP = slice(0, 80)
DOWN = slice(80, 160)
LOCAL = slice(160, 256)


def keep_of(wide, lane):
    low = jnp.where(wide >= 4.5, 2, jnp.where(wide >= 2.5, 1, 0))
    high = jnp.where(wide < 0.5, 1, jnp.where((wide < 1.5) | ((wide > 2.5) & (wide < 3.5)), 2, 3))
    return lane == low, lane == high


def kept_pair(planes, gates):
    one, two, three, four = planes
    low = jnp.where(gates >= 4.5, three, jnp.where(gates >= 2.5, two, one))
    high = jnp.where(gates < 0.5, two, jnp.where((gates < 1.5) | ((gates > 2.5) & (gates < 3.5)), three, four))
    return low, high


def eye(rows, cols):
    return one_hot((rows, cols), 1, lax.broadcasted_iota(jnp.int32, (rows, cols), 0))


def repeat_four(groups, width):
    rows = lax.broadcasted_iota(jnp.int32, (groups, width), 0)
    cols = lax.broadcasted_iota(jnp.int32, (groups, width), 1)
    return ((cols >> 2) == rows).astype(F32).astype(BF)


def plane_order():
    rows = lax.broadcasted_iota(jnp.int32, (HID, HID), 0)
    return one_hot((HID, HID), 1, 4 * (rows & 63) + (rows >> 6))


def pack_kernel(state_hbm, cot_hbm, sea_hbm, out_ref, state_ref, cot_ref, sea_ref, sems):
    copies = fetch((state_hbm, cot_hbm, sea_hbm), (state_ref, cot_ref, sea_ref), sems)
    for copy in copies:
        copy.wait()
    comp = lax.axis_index("comp")
    weight = jnp.where(comp == 1, sea_ref[...].astype(F32), 1.0)
    grad = (weight * cot_ref[...].astype(F32)).astype(BF)
    for place in range(8):
        out_ref[place, 0:FIELDS] = state_ref[...]
        out_ref[place, FIELDS : 2 * FIELDS] = grad


def kept_rows(gates, kernel):
    outputs = kernel.shape[0]
    rows = lax.broadcasted_iota(jnp.int32, (outputs, outputs // 4), 0) >> 2
    repeat = one_hot((outputs, outputs // 4), 1, rows)
    low = jnp.where(gates >= 4.5, 2.0, jnp.where(gates >= 2.5, 1.0, 0.0)).astype(BF)
    high = jnp.where(gates < 0.5, 1.0, jnp.where((gates < 1.5) | ((gates > 2.5) & (gates < 3.5)), 2.0, 3.0)).astype(BF)
    lane = (lax.broadcasted_iota(jnp.int32, kernel.shape, 0) & 3).astype(F32)
    return jnp.where((dot(repeat, low) == lane) | (dot(repeat, high) == lane), kernel, 0.0)


def prepare_early_kernel(
    turn_hbm, first_gates_hbm, out_gates_hbm, first_hbm, out_hbm, mid_gates_hbm, mid_hbm, bank_ref,
    turn_ref, first_gates_ref, out_gates_ref, first_ref, out_ref, mid_gates_ref, mid_ref, sems,
):
    copies = fetch(
        (turn_hbm, first_gates_hbm, out_gates_hbm, first_hbm, out_hbm, mid_gates_hbm, mid_hbm),
        (turn_ref, first_gates_ref, out_gates_ref, first_ref, out_ref, mid_gates_ref, mid_ref), sems,
    )
    copies[0].wait()
    row = lax.axis_index(ROW_AXES)
    strip_of = lax.broadcasted_iota(jnp.int32, (8, 256), 1) >> 4
    along = lax.broadcasted_iota(jnp.int32, (8, 256), 1) & 15
    cells = jnp.zeros((8, 256), jnp.int32)
    for number, (source, side, reader) in enumerate(STRIPS):
        turn = turn_ref[side, lax.rem(ROW * row + reader - ROW + TILES, TILES)]
        first, step = edge_line(*EDGE_MAP[side][3])
        for turns in range(3):
            one, two = edge_line(*EDGE_MAP[side][turns])
            first, step = jnp.where(turn == turns, one, first), jnp.where(turn == turns, two, step)
        first = first + source * CELLS
        cells = jnp.where(strip_of == number, first + step * along, cells)
        place = lax.broadcasted_iota(jnp.int32, (TS, LINE), 1)
        wanted = first + step * lax.broadcasted_iota(jnp.int32, (TS, LINE), 0)
        hit = (place == wanted).astype(F32).astype(BF)
        for col in range(ROW):
            at = TAKE + CELLS * col + TS * number
            bank_ref[at : at + TS] = hit[:, CELLS * col : CELLS * (col + 1)]
    bank_ref[GIVE : GIVE + LINE] = one_hot((LINE, 256), 0, cells[0:1])
    for copy in copies[1:]:
        copy.wait()
    count = 9 * DEPTH
    wide = dot_tn(first_gates_ref[...].astype(F32).astype(BF), repeat_four(HID // 4, HID))
    low, high = keep_of(wide, lax.broadcasted_iota(jnp.int32, (count, HID), 1) & 3)
    kernel = jnp.where(low | high, first_ref[...].astype(F32), 0.0)
    blank = jnp.zeros((32 - DEPTH, HID), F32)
    kernel_out = kept_rows(out_gates_ref[...].astype(F32), out_ref[...].astype(F32)).astype(BF)
    for a in range(3):
        pieces = []
        for b in range(3):
            tap = 3 * a + b
            pieces += [kernel[DEPTH * tap : DEPTH * (tap + 1)], blank]
            at = OUT_BACK + PADC * b + FIELDS * a
            bank_ref[at : at + FIELDS] = kernel_out[:, HID * tap : HID * (tap + 1)]
        pieces.append(jnp.zeros((32, HID), F32))
        bank_ref[FIRST_W + PADC * a : FIRST_W + PADC * (a + 1)] = jnp.concatenate(pieces, 0).astype(BF)
        bank_ref[OUT_BACK + PADC * a + 48 : OUT_BACK + PADC * (a + 1)] = jnp.zeros((PADC - 48, HID), BF)
    for tap in range(9):
        cols = slice(HID * tap, HID * (tap + 1))
        gates = mid_gates_ref[:, cols].astype(F32)
        bank_ref[MID_GATES + 64 * tap : MID_GATES + 64 * (tap + 1)] = gates.astype(BF)
        at = MID_BACK + HID * (3 * (tap % 3) + tap // 3)
        bank_ref[at : at + HID] = kept_rows(gates, dot_nt(eye(HID, HID), mid_ref[cols])).astype(BF)


def prepare_late_kernel(early_ref, first_gates_hbm, out_gates_hbm, two_ref, first_gates_ref, out_gates_ref, sems):
    copies = fetch((first_gates_hbm, out_gates_hbm), (first_gates_ref, out_gates_ref), sems)
    for a in range(3):
        for b in range(3):
            at = MID_BACK + HID * (3 * b + a)
            to = MID_W + HID * (3 * a + b)
            two_ref[to : to + HID] = dot_tn(early_ref[at : at + HID], eye(HID, HID)).astype(BF)
    for copy in copies:
        copy.wait()
    count = 9 * DEPTH
    place = lax.broadcasted_iota(jnp.int32, (count, 3 * PADC), 0)
    tap = (place * 2731) >> 16
    third = (tap * 11) >> 5
    target = PADC * third + 32 * (tap - 3 * third) + place - DEPTH * tap
    gates = first_gates_ref[...].astype(F32).astype(BF)
    spread = dot(gates, one_hot((count, 3 * PADC), 1, target)).astype(BF)
    two_ref[FIRST_GATES : FIRST_GATES + 64] = spread[:, :HID]
    two_ref[FIRST_GATES + 64 : FIRST_GATES + 128, :PADC] = spread[:, HID:]
    gates = dot(eye(16, 4), out_gates_ref[...].astype(F32).astype(BF)).astype(BF)
    for tap in range(9):
        two_ref[OUT_GATES + 16 * tap : OUT_GATES + 16 * (tap + 1)] = gates[:, HID * tap : HID * (tap + 1)]


def prepare_last_kernel(early_ref, first_gates_ref, out_gates_ref, act_ref, three_ref, slope_ref):
    slope_ref[...] = slope(act_ref[...])
    col = lax.axis_index(("xh", "core"))
    tile = lax.axis_index(FACE)
    three_ref[GIVE_OWN : GIVE_OWN + CELLS] = early_ref[pl.ds(pl.multiple_of(GIVE + CELLS * col, CELLS), CELLS)]
    three_ref[LAST_W : LAST_W + 6 * PADC] = early_ref[FIRST_W : FIRST_W + 6 * PADC]
    count = 9 * DEPTH
    gates = first_gates_ref[...].astype(F32).astype(BF)
    three_ref[FIRST_WIDE : FIRST_WIDE + count] = dot_tn(gates, repeat_four(HID // 4, HID)).astype(BF)
    place = lax.broadcasted_iota(jnp.int32, (32, 9 * HID), 0)
    mine = one_hot((32, 9 * HID), 1, jnp.where(place < 18, 18 * tile + place, -1))
    gates = bank_gates(early_ref, MID_GATES, 64, range(9))
    three_ref[OWN_GATES : OWN_GATES + 32, :64] = dot_nt(mine, gates).astype(BF)
    gates = dot(eye(PADC, 4), out_gates_ref[...].astype(F32).astype(BF)).astype(BF)
    three_ref[OWN_GATES : OWN_GATES + 32, PADC:] = dot_nt(mine, gates).astype(BF)


def bank_gates(bank_ref, base, rows, blocks):
    step = max(rows, 16)
    return jnp.concatenate(
        [bank_ref[base + step * b : base + step * (b + 1)][:rows] for b in blocks], 1
    )


def start_kernel(line_ref, bank_ref, field_ref, grad_ref, strips_ref):
    comp = lax.axis_index("comp")
    for col in range(ROW):
        own = line_ref[comp, col].astype(F32)
        other = line_ref[1 - comp, col][:FIELDS].astype(F32)[:COUPLED]
        blank = jnp.zeros((32 - DEPTH, CELLS), F32)
        field = jnp.concatenate([own[:FIELDS], other, blank] * 3 + [jnp.zeros((32, CELLS), F32)], 0)
        field_ref[CELLS * col : CELLS * (col + 1)] = field.T.astype(BF)
        grad = jnp.concatenate([own[FIELDS:]] * 3 + [jnp.zeros((PADC - 3 * FIELDS, CELLS), F32)], 0)
        grad_ref[CELLS * col : CELLS * (col + 1)] = grad.T.astype(BF)
    strips_ref[...] = take_strips(bank_ref, field_ref)


def send_strips(strips, up_ref, down_ref, local_ref):
    up_ref[0:80] = strips[UP]
    down_ref[0:80] = strips[DOWN]
    local_ref[0:96] = strips[LOCAL]


def back_strips(prev_ref, next_ref, local_ref):
    return jnp.concatenate([next_ref[80:160], prev_ref[80:160], local_ref[96:192]], 0)


def layer_one_kernel(
    field_ref, strips_ref, prev_ref, next_ref, grad_ref, bank_ref,
    filled_ref, act_ref, hid_ref, local_ref, up_ref, down_ref, inner_ref,
):
    fill_packed(filled_ref, field_ref[...], strips_ref[LOCAL], prev_ref[...], next_ref[...])
    for col in range(ROW):
        act = conv_tile(filled_ref, bank_ref, FIRST_W, col)
        act_ref[CELLS * col : CELLS * (col + 1)] = act
        hid_ref[CELLS * col : CELLS * (col + 1)] = (act * sigmoid(act)).astype(BF)
    send_strips(take_strips(bank_ref, hid_ref), up_ref, down_ref, local_ref)
    fold_row(
        lambda col: pad_lines_packed(grad_ref[CELLS * col : CELLS * (col + 1)]),
        bank_ref, OUT_BACK, slice(None), inner_ref, down_ref.at[80:160], up_ref.at[80:160], local_ref.at[96:192],
    )


def layer_two_kernel(
    hid_ref, local_in_ref, prev_ref, next_ref, inner_two_ref, early_ref, bank_ref,
    filled_ref, grad_ref, hid_two_ref, local_ref, up_ref, down_ref, inner_ref,
    pad_ref,
):
    fill(filled_ref, hid_ref[...], local_in_ref[0:96], prev_ref[0:80], next_ref[0:80])
    strips = back_strips(prev_ref, next_ref, local_in_ref)
    for col in range(ROW):
        rows = slice(CELLS * col, CELLS * (col + 1))
        grad_hid = inner_two_ref[rows] + dot(early_ref[rows], strips)
        act = conv_tile(filled_ref, bank_ref, MID_W, col)
        sig = sigmoid(act)
        hid_two_ref[rows] = (act * sig).astype(BF)
        grad_ref[rows] = (grad_hid * (sig * (1.0 + act * (1.0 - sig)))).astype(BF)
    send_strips(take_strips(early_ref, hid_two_ref), up_ref, down_ref, local_ref)
    pad_ref[...] = jnp.zeros_like(pad_ref)
    fold_row(
        lambda col: pad_lines(grad_ref[CELLS * col : CELLS * (col + 1)], pad_ref),
        early_ref, MID_BACK, slice(None), inner_ref, down_ref.at[80:160], up_ref.at[80:160], local_ref.at[96:192],
    )


def gather_rows(filled_ref, a):
    return jnp.concatenate(
        [filled_ref[col, a : a + TS].reshape(CELLS, filled_ref.shape[3]) for col in range(ROW)], 0
    )


def term_pairs(filled_ref, grad, gates_of, flat_ref):
    turned = dot_nt(plane_order(), grad).astype(BF)
    width = filled_ref.shape[3]
    for a in range(3):
        cols = slice(width * a, width * (a + 1))
        term = dot(turned, gather_rows(filled_ref, a))
        low, high = kept_pair([term[64 * m : 64 * (m + 1)] for m in range(4)], gates_of(a).astype(F32))
        flat_ref[0:64, cols] = low.astype(BF)
        flat_ref[64:128, cols] = high.astype(BF)


def mid_term_kernel(filled_ref, grad_ref, early_ref, part_ref, pick_out_ref, pick_first_ref, flat_ref):
    col = lax.axis_index(("xh", "core"))
    term_pairs(
        filled_ref, grad_ref[...], lambda a: bank_gates(early_ref, MID_GATES, 64, range(3 * a, 3 * a + 3)), flat_ref
    )
    shape = (16 * CHUNK, 1152)
    place = lax.broadcasted_iota(jnp.int32, shape, 0)
    block = (place * 2731) >> 16
    inside = place - CHUNK * block
    ahead = lax.broadcasted_iota(jnp.int32, shape, 1) - (72 * block + 18 * col)
    pick = ((ahead == inside) & (inside < 18)).astype(F32).astype(BF)
    late = ahead - 9 * (inside - 18)
    pick_out_ref[...] = ((late >= 0) & (late < 9) & (inside >= 18) & (inside < 20)).astype(F32).astype(BF)
    shape = (4 * SHARE, 3 * PADC)
    place = lax.broadcasted_iota(jnp.int32, shape, 0)
    inside = place & 15
    wanted = 14 * (4 * (place >> 4) + col) + inside
    tap = (wanted * 2731) >> 16
    third = (tap * 11) >> 5
    target = PADC * third + 32 * (tap - 3 * third) + wanted - DEPTH * tap
    real = (inside < 14) & (wanted < 9 * DEPTH)
    pick_first_ref[...] = ((lax.broadcasted_iota(jnp.int32, shape, 1) == target) & real).astype(F32).astype(BF)
    for half in range(2):
        part_ref[16 * CHUNK * half : 16 * CHUNK * (half + 1)] = dot_nt(
            pick, flat_ref[:, 1152 * half : 1152 * (half + 1)]
        )


def terms_kernel(
    hid_two_ref, local_ref, prev_ref, next_ref, inner_ref, slope_ref, filled_zero_ref, grad_three_ref, early_ref, bank_ref,
    part_ref, pick_out_ref, pick_first_ref,
    buffer_ref, mine_hbm, grad_ref,
    filled_ref, flat_ref, flat_zero_ref, sem,
):
    fill(filled_ref, hid_two_ref[...], local_ref[0:96], prev_ref[0:80], next_ref[0:80])
    keep = pltpu.make_async_copy(filled_ref.at[lax.axis_index(("xh", "core"))], mine_hbm, sem)
    keep.start()
    strips = back_strips(prev_ref, next_ref, local_ref)
    for col in range(ROW):
        rows = slice(CELLS * col, CELLS * (col + 1))
        grad_hid = inner_ref[rows] + dot(early_ref[rows], strips)
        grad_ref[rows] = (grad_hid * slope_ref[rows]).astype(BF)
    place = lax.broadcasted_iota(jnp.int32, (32, PADC), 0)
    group = place & 7
    wanted = jnp.where(group < 4, 4 * group + (place >> 3), -1)
    turned = dot_nt(one_hot((32, PADC), 1, wanted), grad_three_ref[...]).astype(BF)
    width = filled_ref.shape[3]
    for a in range(3):
        cols = slice(width * a, width * (a + 1))
        term = dot(turned, gather_rows(filled_ref, a))
        gates = bank_gates(bank_ref, OUT_GATES, 16, range(3 * a, 3 * a + 3)).astype(F32)[:8]
        low, high = kept_pair([term[8 * m : 8 * (m + 1)] for m in range(4)], gates)
        pair = low + pltpu.roll(high, 4, 0)
        wide = jnp.broadcast_to(pair[None], (16, 8, width)).reshape(128, width)
        kernel_row = lax.broadcasted_iota(jnp.int32, (128, width), 1) + width * a
        slot = kernel_row - 9 * ((kernel_row * 7282) >> 16)
        mine = (lax.broadcasted_iota(jnp.int32, (128, width), 0) >> 3) == slot
        flat_ref[:, cols] = jnp.where(mine, wide, 0.0).astype(BF)
    gates = [
        bank_ref[FIRST_GATES : FIRST_GATES + 64, :PADC], bank_ref[FIRST_GATES : FIRST_GATES + 64, PADC:],
        bank_ref[FIRST_GATES + 64 : FIRST_GATES + 128, :PADC],
    ]
    term_pairs(filled_zero_ref, grad_ref[...], lambda a: gates[a], flat_zero_ref)
    for half in range(2):
        rows = slice(16 * CHUNK * half, 16 * CHUNK * (half + 1))
        part = part_ref[rows] + dot_nt(pick_out_ref[...], flat_ref[:, 1152 * half : 1152 * (half + 1)])
        buffer_ref[16 * half : 16 * (half + 1), 0:CHUNK] = part.astype(BF).reshape(16, CHUNK, PADC)
    share = dot_nt(pick_first_ref[...], flat_zero_ref[...]).astype(BF)
    for place in range(ROWS):
        kind = place // 8
        buffer_ref[place, CHUNK : CHUNK + SHARE] = share[SHARE * kind : SHARE * (kind + 1)]
    keep.wait()


def last_kernel(
    mine_ref, grad_ref, bank_ref, state_ref, sea_ref,
    estimate_ref, dx_ref, up_ref, down_ref, local_ref,
    pad_ref, dx_all_ref, narrow_ref,
):
    for a in range(3):
        for b in range(3):
            at = LAST_W + PADC * a + 32 * b
            block = jnp.concatenate([bank_ref[at : at + 32], jnp.zeros((PADC - 32, HID), BF)], 0)
            to = HID * (3 * b + a)
            narrow_ref[to : to + HID, :PADC] = dot_nt(eye(HID, HID), block).astype(BF)
            at = LAST_W + PADC * (3 + b) + FIELDS * a
            block = jnp.concatenate([bank_ref[at : at + FIELDS], jnp.zeros((PADC - FIELDS, HID), BF)], 0)
            to = HID * (3 * a + b)
            narrow_ref[to : to + HID, PADC:] = dot_tn(block, eye(PADC, PADC)).astype(BF)
    comp = lax.axis_index("comp")
    col = lax.axis_index(("xh", "core"))
    width = mine_ref.shape[2]
    pad_ref[...] = jnp.zeros_like(pad_ref)
    fold_row(
        lambda col: pad_lines(grad_ref[CELLS * col : CELLS * (col + 1)], pad_ref),
        narrow_ref, 0, slice(0, PADC), dx_all_ref, down_ref, up_ref, local_ref,
    )
    dx_ref[...] = dx_all_ref[pl.ds(pl.multiple_of(col * CELLS, CELLS), CELLS)]
    total = None
    for a in range(3):
        weights = narrow_ref[width * a : width * (a + 1), PADC:]
        piece = dot(mine_ref[a : a + TS].reshape(CELLS, width), weights)
        total = piece if total is None else total + piece
    weight = jnp.where(comp == 1, sea_ref[...].astype(F32), 1.0)
    estimate_ref[...] = (state_ref[...].astype(F32) + weight * total.T[:FIELDS]).astype(BF)


def sum_kernel(spread_ref, share_ref, sum_ref):
    total = spread_ref[0].astype(F32)
    for place in range(1, ROWS):
        total = total + spread_ref[place].astype(F32)
    sum_ref[...] = total[:CHUNK]
    share = total[CHUNK:].astype(BF)
    for place in range(16):
        share_ref[place] = share


def finish_kernel(
    dx_ref, next_ref, prev_ref, local_ref, bank_ref, cot_ref, sum_ref,
    own_ref, send_ref, central_ref, closing_ref,
):
    give = bank_ref[GIVE_OWN : GIVE_OWN + CELLS]
    strips = jnp.concatenate([next_ref[...], prev_ref[...], local_ref[...]], 0)
    total = (dx_ref[...] + dot(give, strips)).T
    own_ref[...] = cot_ref[...].astype(F32) + total[:FIELDS]
    send_ref[...] = total[FIELDS : FIELDS + COUPLED]
    sums = sum_ref[...]
    repeat = repeat_four(HID // 4, HID)
    wide = dot(bank_ref[OWN_GATES : OWN_GATES + 32, :64], repeat)[:CHUNK]
    low, high = keep_of(wide, lax.broadcasted_iota(jnp.int32, (CHUNK, HID), 1) & 3)
    lows, highs = dot_exact_right(sums[:, :64], repeat), dot_exact_right(sums[:, 64:], repeat)
    central = jnp.where(low, lows, jnp.where(high, highs, 0.0))
    for line in range(18):
        central_ref[:, HID * line : HID * (line + 1)] = central[line : line + 1]
    place = lax.broadcasted_iota(jnp.int32, (CHUNK, CHUNK), 0)
    late = (place >= 9).astype(jnp.int32)
    spread = dot_exact(one_hot((CHUNK, CHUNK), 1, 18 + late), sums)
    place = lax.broadcasted_iota(jnp.int32, (CHUNK, PADC), 0)
    slot = place - 9 * (place >= 9).astype(jnp.int32)
    lane = lax.broadcasted_iota(jnp.int32, (CHUNK, PADC), 1)
    spread = jnp.where((lane >> 3) == slot, spread, 0.0)
    flat = 3 * PADC
    from_lane = lax.broadcasted_iota(jnp.int32, (PADC, flat), 0) & 7
    group = (lax.broadcasted_iota(jnp.int32, (PADC, flat), 1) & 15) >> 2
    lows = dot_exact_right(spread, (from_lane == group).astype(F32).astype(BF))
    highs = dot_exact_right(spread, (from_lane == group + 4).astype(F32).astype(BF))
    group = (lax.broadcasted_iota(jnp.int32, (PADC, flat), 1) & 15) >> 2
    wide = dot(bank_ref[OWN_GATES : OWN_GATES + 32, PADC:], one_hot((PADC, flat), 0, group))[:CHUNK]
    lane = lax.broadcasted_iota(jnp.int32, (CHUNK, flat), 1)
    low, high = keep_of(wide, lane & 3)
    closing = jnp.where(low, lows, jnp.where(high, highs, 0.0))
    here = lax.broadcasted_iota(jnp.int32, (CHUNK, flat), 0) == (lane >> 4)
    closing_ref[...] = jnp.sum(jnp.where(here, closing, 0.0), 0, keepdims=True)[:, : 18 * FIELDS]


def opening_kernel(share_ref, bank_ref, out_ref):
    count = 9 * (FIELDS + COUPLED)
    wanted = lax.broadcasted_iota(jnp.int32, (count, 16 * SHARE), 0)
    block = (wanted * 4682) >> 16
    pick = one_hot((count, 16 * SHARE), 1, SHARE * block + wanted - 14 * block)
    pairs = dot(pick, share_ref[...]).astype(BF)
    repeat = repeat_four(HID // 4, HID)
    low, high = keep_of(bank_ref[FIRST_WIDE : FIRST_WIDE + count].astype(F32), lax.broadcasted_iota(jnp.int32, (count, HID), 1) & 3)
    out_ref[...] = jnp.where(low, dot(pairs[:, :64], repeat), jnp.where(high, dot(pairs[:, 64:], repeat), 0.0))


VMEM = pl.BlockSpec(memory_space=pltpu.VMEM)
SMEM = pl.BlockSpec(memory_space=pltpu.SMEM)
HBM = pl.BlockSpec(memory_space=pltpu.HBM)


def call(body, out, args, scratch=(), scalars=(), far=(), far_out=(), flops=0, limit=10):
    args = [pltpu.with_memory_space_constraint(arg, pltpu.HBM) if place in far else arg for place, arg in enumerate(args)]
    specs = [SMEM if place in scalars else HBM if place in far else VMEM for place in range(len(args))]
    size = sum(int(np.prod(item.shape)) * item.dtype.itemsize for item in list(args) + list(out))
    return pl.pallas_call(
        body,
        out_shape=[jax.ShapeDtypeStruct(item.shape, item.dtype) for item in out],
        in_specs=specs,
        out_specs=[HBM if place in far_out else VMEM for place in range(len(out))],
        scratch_shapes=list(scratch),
        compiler_params=pltpu.CompilerParams(vmem_limit_bytes=limit * 1024 * 1024),
        cost_estimate=pl.CostEstimate(flops=flops, bytes_accessed=size, transcendentals=0),
    )(*args)


def sds(shape, kind):
    return jax.ShapeDtypeStruct(shape, kind)


def row_shift(value, step):
    pairs = [(face, (face + ROW * step) % TILES) for face in range(TILES)]
    return lax.ppermute(value, FACE, pairs)


def body(
    state, cotangent, land_sea, turn_table, first_kernel, mid_kernel, out_kernel, first_gates, mid_gates, out_gates
):
    sea = land_sea.reshape(1, CELLS)

    packed = call(pack_kernel, [sds((8, 2 * FIELDS, CELLS), BF)], [state[0], cotangent[0], sea],
        scratch=[
            pltpu.VMEM((FIELDS, CELLS), BF), pltpu.VMEM((FIELDS, CELLS), BF), pltpu.VMEM((1, CELLS), jnp.int32),
            pltpu.SemaphoreType.DMA((3,)),
        ],
        far=(0, 1, 2),
    )[0]
    line = lax.all_to_all(packed, LINE_AXES, 0, 0).reshape(2, ROW, 2 * FIELDS, CELLS)

    turns, out_turned = turn_table.T, out_gates[0].T
    first_turned, mid_turned = first_gates[0].T, mid_gates[0].T
    early = call(
        prepare_early_kernel, [sds((BANK_ONE, HID), BF)],
        [turns, first_turned, out_turned, first_kernel[0], out_kernel[0].T, mid_turned, mid_kernel[0]],
        scratch=[
            pltpu.SMEM((4, TILES), jnp.int32), pltpu.VMEM((64, 9 * DEPTH), jnp.int32),
            pltpu.VMEM((4, 9 * HID), jnp.int32), pltpu.VMEM((9 * DEPTH, HID), BF),
            pltpu.VMEM((FIELDS, 9 * HID), BF), pltpu.VMEM((64, 9 * HID), jnp.int32),
            pltpu.VMEM((9 * HID, HID), BF), pltpu.SemaphoreType.DMA((7,)),
        ],
        far=(0, 1, 2, 3, 4, 5, 6), flops=5 * 10**9,
    )[0]

    field, grad_cells, strips_zero = call(
        start_kernel,
        [sds((LINE, PADC), BF), sds((LINE, PADC), BF), sds((256, PADC), BF)], [line, early],
    )
    prev_zero = row_shift(strips_zero[UP], 1)
    next_zero = row_shift(strips_zero[DOWN], -1)
    two = call(
        prepare_late_kernel, [sds((BANK_TWO, HID), BF)], [early, first_turned, out_turned],
        scratch=[
            pltpu.VMEM((64, 9 * DEPTH), jnp.int32), pltpu.VMEM((4, 9 * HID), jnp.int32),
            pltpu.SemaphoreType.DMA((2,)),
        ],
        far=(1, 2), flops=10**9,
    )[0]
    exchange = [sds((192, HID), BF), sds((160, HID), BF), sds((160, HID), BF), sds((LINE, HID), F32)]
    filled_zero, act_one, hid_one, local_one, up_one, down_one, inner_two = call(
        layer_one_kernel,
        [sds((ROW, TS + 2, TS, PADC), BF), sds((LINE, HID), F32), sds((LINE, HID), BF)] + exchange,
        [field, strips_zero, prev_zero, next_zero, grad_cells, early],
    )
    prev_one = row_shift(up_one, 1)
    next_one = row_shift(down_one, -1)

    three, slope_one = call(
        prepare_last_kernel, [sds((BANK_THREE, HID), BF), sds((LINE, HID), F32)],
        [early, first_turned, out_turned, act_one], flops=10**9,
    )

    filled_one, grad_two, hid_two, local_two, up_two, down_two, inner_one = call(
        layer_two_kernel,
        [sds((ROW, TS + 2, TS, 3 * HID), BF), sds((LINE, HID), BF), sds((LINE, HID), BF)] + exchange,
        [hid_one, local_one, prev_one, next_one, inner_two, early, two],
        scratch=[pltpu.VMEM((TS + 2, TS, 3 * HID), BF)],
    )
    prev_two = row_shift(up_two, 1)
    next_two = row_shift(down_two, -1)

    part, pick_out, pick_first = call(
        mid_term_kernel,
        [sds((32 * CHUNK, PADC), F32), sds((16 * CHUNK, 1152), BF), sds((4 * SHARE, 3 * PADC), BF)],
        [filled_one, grad_two, early],
        scratch=[pltpu.VMEM((PADC, 9 * HID), BF)], flops=2 * 10**9,
    )

    buffer, mine_two, grad_one = call(
        terms_kernel,
        [sds((ROWS, CHUNK + SHARE, PADC), BF), sds((TS + 2, TS, 3 * HID), BF), sds((LINE, HID), BF)],
        [hid_two, local_two, prev_two, next_two, inner_one, slope_one, filled_zero, grad_cells, early, two,
         part, pick_out, pick_first],
        scratch=[
            pltpu.VMEM((ROW, TS + 2, TS, 3 * HID), BF), pltpu.VMEM((PADC, 9 * HID), BF),
            pltpu.VMEM((PADC, 3 * PADC), BF), pltpu.SemaphoreType.DMA,
        ],
        far_out=(1,),
    )
    spread = lax.all_to_all(buffer, ROW_AXES, 0, 0)

    estimate, dx_own, up_three, down_three, local_three = call(
        last_kernel,
        [sds((FIELDS, CELLS), BF), sds((CELLS, PADC), F32), sds((80, PADC), BF), sds((80, PADC), BF),
         sds((96, PADC), BF)],
        [mine_two, grad_one, three, state[0], sea],
        scratch=[
            pltpu.VMEM((TS + 2, TS, 3 * HID), BF), pltpu.VMEM((LINE, PADC), F32),
            pltpu.VMEM((9 * HID, HID), BF),
        ],
        flops=2 * 10**9,
    )
    prev_three = row_shift(up_three, 1)
    next_three = row_shift(down_three, -1)

    shared, summed = call(sum_kernel, [sds((16, SHARE, PADC), BF), sds((CHUNK, PADC), F32)], [spread])
    opened = lax.all_to_all(shared, ("y", "xh", "core"), 0, 0).reshape(16 * SHARE, PADC)

    own, send, central, closing = call(
        finish_kernel,
        [sds((FIELDS, CELLS), F32), sds((COUPLED, CELLS), F32), sds((1, 18 * HID), F32), sds((1, 18 * FIELDS), F32)],
        [dx_own, next_three, prev_three, local_three, three, cotangent[0], summed],
    )
    returned = lax.ppermute(send, "comp", [(0, 1), (1, 0)])
    adjoint = own + jnp.pad(returned, ((0, FIELDS - COUPLED), (0, 0)))
    opening = call(opening_kernel, [sds((9 * DEPTH, HID), F32)], [opened, three])[0]
    return estimate[None], adjoint[None], opening[None], central, closing


def solution(mesh):
    fine = Mesh(mesh.devices.reshape(2, 4, 8, 2, 2), ("comp",) + FACE)
    whole = P("comp", None, None)
    in_specs = (P("comp", None, FACE), P("comp", None, FACE), P(FACE), P()) + (whole,) * 6
    out_specs = (P("comp", None, FACE), P("comp", None, FACE), whole, P("comp", FACE), P("comp", FACE))

    return jax.shard_map(body, mesh=fine, in_specs=in_specs, out_specs=out_specs, check_vma=False)
```

```python
import jax
import jax.numpy as jnp
import numpy as np
from jax import lax
from jax.experimental import pallas as pl
from jax.experimental.pallas import tpu as pltpu
from jax.sharding import Mesh, PartitionSpec as P


FIELDS = 16
COUPLED = 8
TS = 16
CELLS = TS * TS
ROW = 4
ROWS = 32
TILES = ROW * ROWS
LINE = ROW * CELLS
HID = 256
PADC = 128
CHUNK = 24
SHARE = 16
DEPTH = FIELDS + COUPLED

GIVE = 0
TAKE = GIVE + LINE
FIRST_W = TAKE + LINE
OUT_BACK = FIRST_W + 3 * PADC
BANK_ONE = OUT_BACK + 3 * PADC
MID_BACK = 0
MID_GATES = MID_BACK + 9 * HID
BANK_MID = MID_GATES + 9 * 64
MID_W = 0
FIRST_GATES = MID_W + 9 * HID
OUT_GATES = FIRST_GATES + 2 * 64
BANK_TWO = OUT_GATES + 9 * 16
FIRST_WIDE = 0
GIVE_OWN = FIRST_WIDE + 224
OWN_GATES = GIVE_OWN + CELLS
BANK_THREE = OWN_GATES + 32
BF = jnp.bfloat16
F32 = jnp.float32

FACE = ("y", "z", "xh", "core")
ROW_AXES = ("y", "z")
LINE_AXES = ("comp", "xh", "core")

EDGE_MAP = (
    ((0, False), (2, True), (1, True), (3, False)),
    ((1, False), (3, True), (0, True), (2, False)),
    ((2, False), (1, False), (3, True), (0, True)),
    ((3, False), (0, False), (2, True), (1, True)),
)

STRIPS = (
    [(col, 2, 8 + col) for col in range(4)]
    + [(3, 0, 8)]
    + [(col, 3, col) for col in range(4)]
    + [(0, 1, 3)]
    + [(col - 1, 0, 4 + col) for col in (1, 2, 3)]
    + [(col + 1, 1, 4 + col) for col in (0, 1, 2)]
)


def edge_line(slot, flip):
    first, step = ((TS - 1, TS), (0, TS), ((TS - 1) * TS, 1), (0, 1))[slot]
    if flip:
        first, step = first + (TS - 1) * step, -step
    return first, step


def dot(left, right):
    return jnp.dot(left, right, preferred_element_type=F32)


def dot_nt(left, right):
    return lax.dot_general(left, right, (((1,), (1,)), ((), ())), preferred_element_type=F32)


def dot_tn(left, right):
    return lax.dot_general(left, right, (((0,), (0,)), ((), ())), preferred_element_type=F32)


def dot_exact(left, right):
    high = right.astype(BF)
    rest = right - high.astype(F32)
    mid = rest.astype(BF)
    low = (rest - mid.astype(F32)).astype(BF)
    return dot(left, high) + (dot(left, mid) + dot(left, low))


def dot_exact_right(left, right):
    high = left.astype(BF)
    rest = left - high.astype(F32)
    mid = rest.astype(BF)
    low = (rest - mid.astype(F32)).astype(BF)
    return dot(high, right) + (dot(mid, right) + dot(low, right))


def fetch(sources, buffers, sems):
    copies = [
        pltpu.make_async_copy(source, buffer, sems.at[place])
        for place, (source, buffer) in enumerate(zip(sources, buffers))
    ]
    for copy in copies:
        copy.start()
    return copies


def one_hot(shape, axis, index):
    return (lax.broadcasted_iota(jnp.int32, shape, axis) == index).astype(F32).astype(BF)


def shift_cells(value, step, axis):
    along = lax.broadcasted_iota(jnp.int32, value.shape, axis)
    moved = pltpu.roll(value, step % TS, axis)
    edge = 0 if step == 1 else TS - 1
    return jnp.where(along == edge, 0.0, moved)


def shift_lines(lines, step, strip):
    along = lax.broadcasted_iota(jnp.int32, lines.shape, 1)
    moved = pltpu.roll(lines, step % TS, 1)
    edge = 0 if step == 1 else TS - 1
    return jnp.where(along == edge, jnp.broadcast_to(strip.astype(F32)[:, None, :], lines.shape), moved)


def fill(out_ref, tiles, local, from_prev, from_next):
    depth = tiles.shape[1]
    for col in range(ROW):
        south = from_prev[TS * col : TS * (col + 1)]
        north = from_next[TS * col : TS * (col + 1)]
        west = from_prev[4 * TS : 5 * TS] if col == 0 else local[TS * (col - 1) : TS * col]
        east = from_next[4 * TS : 5 * TS] if col == 3 else local[TS * (3 + col) : TS * (4 + col)]
        own = tiles[CELLS * col : CELLS * (col + 1)]
        wide = own.astype(F32).reshape(TS, TS, depth)
        left = shift_lines(wide, 1, west)
        right = shift_lines(wide, -1, east)
        out_ref[col, 1 : TS + 1, :, 0:depth] = left.astype(BF)
        out_ref[col, 1 : TS + 1, :, depth : 2 * depth] = own.reshape(TS, TS, depth)
        out_ref[col, 1 : TS + 1, :, 2 * depth : 3 * depth] = right.astype(BF)
        for line, strip in ((0, south), (TS + 1, north)):
            wide = strip.astype(F32)
            out_ref[col, line, :, 0:depth] = shift_cells(wide, 1, 0).astype(BF)
            out_ref[col, line, :, depth : 2 * depth] = strip
            out_ref[col, line, :, 2 * depth : 3 * depth] = shift_cells(wide, -1, 0).astype(BF)


def fill_packed(out_ref, tiles, local, from_prev, from_next):
    def choose(left, own, right):
        lane = lax.broadcasted_iota(jnp.int32, own.shape, own.ndim - 1)
        return jnp.where(lane < 32, left, jnp.where(lane < 64, own, right)).astype(BF)

    for col in range(ROW):
        south = from_prev[TS * col : TS * (col + 1)]
        north = from_next[TS * col : TS * (col + 1)]
        west = from_prev[4 * TS : 5 * TS] if col == 0 else local[TS * (col - 1) : TS * col]
        east = from_next[4 * TS : 5 * TS] if col == 3 else local[TS * (3 + col) : TS * (4 + col)]
        wide = tiles[CELLS * col : CELLS * (col + 1)].astype(F32).reshape(TS, TS, PADC)
        left = shift_lines(wide, 1, west)
        right = shift_lines(wide, -1, east)
        out_ref[col, 1 : TS + 1] = choose(left, wide, right)
        for line, strip in ((0, south), (TS + 1, north)):
            wide = strip.astype(F32)
            out_ref[col, line] = choose(shift_cells(wide, 1, 0), wide, shift_cells(wide, -1, 0))


def take_strips(bank_ref, cells_ref):
    total = None
    for col in range(ROW):
        block = slice(TAKE + CELLS * col, TAKE + CELLS * (col + 1))
        piece = dot(bank_ref[block], cells_ref[CELLS * col : CELLS * (col + 1)])
        total = piece if total is None else total + piece
    return total.astype(BF)


def conv_tile(filled_ref, bank_ref, base, col, lanes=slice(None)):
    width = filled_ref.shape[3]
    total = None
    for a in range(3):
        weights = bank_ref[base + width * a : base + width * (a + 1), lanes]
        piece = dot(filled_ref[col, a : a + TS].reshape(CELLS, width), weights)
        total = piece if total is None else total + piece
    return total


def pad_lines(grad, pad_ref):
    deep = grad.shape[1]
    lines = grad.reshape(TS, TS, deep)
    for a in range(3):
        pad_ref[a : a + TS, :, deep * a : deep * (a + 1)] = lines
    return pad_ref[...].reshape((TS + 2) * TS, 3 * deep)


def pad_lines_packed(grad):
    lines = grad.astype(F32).reshape(TS, TS, PADC)
    blank = jnp.zeros((1, TS, PADC), F32)
    lane = lax.broadcasted_iota(jnp.int32, (TS + 2, TS, PADC), 2)
    one, two, three = (
        jnp.concatenate([blank] * a + [lines] + [blank] * (2 - a), 0) for a in range(3)
    )
    padded = jnp.where(lane < 16, one, jnp.where(lane < 32, two, three))
    return padded.reshape((TS + 2) * TS, PADC).astype(BF)


def fold_tile(padded, bank_ref, base, lanes):
    deep = padded.shape[1]
    left, mid, right = (
        dot(padded, bank_ref[base + deep * b : base + deep * (b + 1), lanes]) for b in range(3)
    )
    depth = mid.shape[1]
    left, mid, right = (part.reshape(TS + 2, TS, depth) for part in (left, mid, right))
    merged = mid + shift_cells(left, -1, 1) + shift_cells(right, 1, 1)
    inner = merged[1 : TS + 1].reshape(CELLS, depth)
    south = merged[0].astype(BF)
    north = merged[TS + 1].astype(BF)
    west = left[1 : TS + 1, 0, :].astype(BF)
    east = right[1 : TS + 1, TS - 1, :].astype(BF)
    return inner, south, north, west, east


def fold_row(padded_of, bank_ref, base, lanes, inner_ref, prev_ref, next_ref, local_ref):
    for col in range(ROW):
        inner, south, north, west, east = fold_tile(padded_of(col), bank_ref, base, lanes)
        inner_ref[CELLS * col : CELLS * (col + 1)] = inner
        prev_ref[TS * col : TS * (col + 1)] = south
        next_ref[TS * col : TS * (col + 1)] = north
        if col == 0:
            prev_ref[4 * TS : 5 * TS] = west
        else:
            local_ref[TS * (col - 1) : TS * col] = west
        if col == 3:
            next_ref[4 * TS : 5 * TS] = east
        else:
            local_ref[TS * (3 + col) : TS * (4 + col)] = east


def sigmoid(values):
    return 1.0 / (1.0 + jnp.exp(-values))


def slope(values):
    sig = sigmoid(values)
    return sig * (1.0 + values * (1.0 - sig))


UP = slice(0, 80)
DOWN = slice(80, 160)
LOCAL = slice(160, 256)


def keep_of(wide, lane):
    low = jnp.where(wide >= 4.5, 2, jnp.where(wide >= 2.5, 1, 0))
    high = jnp.where(wide < 0.5, 1, jnp.where((wide < 1.5) | ((wide > 2.5) & (wide < 3.5)), 2, 3))
    return lane == low, lane == high


def kept_pair(planes, gates):
    one, two, three, four = planes
    low = jnp.where(gates >= 4.5, three, jnp.where(gates >= 2.5, two, one))
    high = jnp.where(gates < 0.5, two, jnp.where((gates < 1.5) | ((gates > 2.5) & (gates < 3.5)), three, four))
    return low, high


def eye(rows, cols):
    return one_hot((rows, cols), 1, lax.broadcasted_iota(jnp.int32, (rows, cols), 0))


def repeat_four(groups, width):
    rows = lax.broadcasted_iota(jnp.int32, (groups, width), 0)
    cols = lax.broadcasted_iota(jnp.int32, (groups, width), 1)
    return ((cols >> 2) == rows).astype(F32).astype(BF)


def plane_order():
    rows = lax.broadcasted_iota(jnp.int32, (HID, HID), 0)
    return one_hot((HID, HID), 1, 4 * (rows & 63) + (rows >> 6))


def pack_kernel(state_hbm, cot_hbm, sea_hbm, out_ref, state_ref, cot_ref, sea_ref, sems):
    copies = fetch((state_hbm, cot_hbm, sea_hbm), (state_ref, cot_ref, sea_ref), sems)
    for copy in copies:
        copy.wait()
    comp = lax.axis_index("comp")
    weight = jnp.where(comp == 1, sea_ref[...].astype(F32), 1.0)
    grad = (weight * cot_ref[...].astype(F32)).astype(BF)
    for place in range(8):
        out_ref[place, 0:FIELDS] = state_ref[...]
        out_ref[place, FIELDS : 2 * FIELDS] = grad


def kept_rows(gates, kernel):
    outputs = kernel.shape[0]
    rows = lax.broadcasted_iota(jnp.int32, (outputs, outputs // 4), 0) >> 2
    repeat = one_hot((outputs, outputs // 4), 1, rows)
    low = jnp.where(gates >= 4.5, 2.0, jnp.where(gates >= 2.5, 1.0, 0.0)).astype(BF)
    high = jnp.where(gates < 0.5, 1.0, jnp.where((gates < 1.5) | ((gates > 2.5) & (gates < 3.5)), 2.0, 3.0)).astype(BF)
    lane = (lax.broadcasted_iota(jnp.int32, kernel.shape, 0) & 3).astype(F32)
    return jnp.where((dot(repeat, low) == lane) | (dot(repeat, high) == lane), kernel, 0.0)


def prepare_early_kernel(
    turn_hbm, first_gates_hbm, out_gates_hbm, first_hbm, out_hbm, mid_gates_hbm, mid_hbm, bank_ref, middle_ref,
    turn_ref, first_gates_ref, out_gates_ref, first_ref, out_ref, mid_gates_ref, mid_ref, sems,
):
    copies = fetch(
        (turn_hbm, first_gates_hbm, out_gates_hbm, first_hbm, out_hbm, mid_gates_hbm, mid_hbm),
        (turn_ref, first_gates_ref, out_gates_ref, first_ref, out_ref, mid_gates_ref, mid_ref), sems,
    )
    copies[0].wait()
    row = lax.axis_index(ROW_AXES)
    strip_of = lax.broadcasted_iota(jnp.int32, (8, 256), 1) >> 4
    along = lax.broadcasted_iota(jnp.int32, (8, 256), 1) & 15
    cells = jnp.zeros((8, 256), jnp.int32)
    for number, (source, side, reader) in enumerate(STRIPS):
        turn = turn_ref[side, lax.rem(ROW * row + reader - ROW + TILES, TILES)]
        first, step = edge_line(*EDGE_MAP[side][3])
        for turns in range(3):
            one, two = edge_line(*EDGE_MAP[side][turns])
            first, step = jnp.where(turn == turns, one, first), jnp.where(turn == turns, two, step)
        first = first + source * CELLS
        cells = jnp.where(strip_of == number, first + step * along, cells)
        place = lax.broadcasted_iota(jnp.int32, (TS, LINE), 1)
        wanted = first + step * lax.broadcasted_iota(jnp.int32, (TS, LINE), 0)
        hit = (place == wanted).astype(F32).astype(BF)
        for col in range(ROW):
            at = TAKE + CELLS * col + TS * number
            bank_ref[at : at + TS] = hit[:, CELLS * col : CELLS * (col + 1)]
    bank_ref[GIVE : GIVE + LINE] = one_hot((LINE, 256), 0, cells[0:1])
    for copy in copies[1:]:
        copy.wait()
    count = 9 * DEPTH
    wide = dot_tn(first_gates_ref[...].astype(F32).astype(BF), repeat_four(HID // 4, HID))
    low, high = keep_of(wide, lax.broadcasted_iota(jnp.int32, (count, HID), 1) & 3)
    kernel = jnp.where(low | high, first_ref[...].astype(F32), 0.0)
    blank = jnp.zeros((32 - DEPTH, HID), F32)
    kernel_out = kept_rows(out_gates_ref[...].astype(F32), out_ref[...].astype(F32)).astype(BF)
    for a in range(3):
        pieces = []
        for b in range(3):
            tap = 3 * a + b
            pieces += [kernel[DEPTH * tap : DEPTH * (tap + 1)], blank]
            at = OUT_BACK + PADC * b + FIELDS * a
            bank_ref[at : at + FIELDS] = kernel_out[:, HID * tap : HID * (tap + 1)]
        pieces.append(jnp.zeros((32, HID), F32))
        bank_ref[FIRST_W + PADC * a : FIRST_W + PADC * (a + 1)] = jnp.concatenate(pieces, 0).astype(BF)
        bank_ref[OUT_BACK + PADC * a + 48 : OUT_BACK + PADC * (a + 1)] = jnp.zeros((PADC - 48, HID), BF)
    for tap in range(9):
        cols = slice(HID * tap, HID * (tap + 1))
        gates = mid_gates_ref[:, cols].astype(F32)
        middle_ref[MID_GATES + 64 * tap : MID_GATES + 64 * (tap + 1)] = gates.astype(BF)
        at = MID_BACK + HID * (3 * (tap % 3) + tap // 3)
        middle_ref[at : at + HID] = kept_rows(gates, dot_nt(eye(HID, HID), mid_ref[cols])).astype(BF)


def prepare_late_kernel(middle_ref, first_gates_hbm, out_gates_hbm, two_ref, first_gates_ref, out_gates_ref, sems):
    copies = fetch((first_gates_hbm, out_gates_hbm), (first_gates_ref, out_gates_ref), sems)
    for a in range(3):
        for b in range(3):
            at = MID_BACK + HID * (3 * b + a)
            to = MID_W + HID * (3 * a + b)
            two_ref[to : to + HID] = dot_tn(middle_ref[at : at + HID], eye(HID, HID)).astype(BF)
    for copy in copies:
        copy.wait()
    count = 9 * DEPTH
    place = lax.broadcasted_iota(jnp.int32, (count, 3 * PADC), 0)
    tap = (place * 2731) >> 16
    third = (tap * 11) >> 5
    target = PADC * third + 32 * (tap - 3 * third) + place - DEPTH * tap
    gates = first_gates_ref[...].astype(F32).astype(BF)
    spread = dot(gates, one_hot((count, 3 * PADC), 1, target)).astype(BF)
    two_ref[FIRST_GATES : FIRST_GATES + 64] = spread[:, :HID]
    two_ref[FIRST_GATES + 64 : FIRST_GATES + 128, :PADC] = spread[:, HID:]
    gates = dot(eye(16, 4), out_gates_ref[...].astype(F32).astype(BF)).astype(BF)
    for tap in range(9):
        two_ref[OUT_GATES + 16 * tap : OUT_GATES + 16 * (tap + 1)] = gates[:, HID * tap : HID * (tap + 1)]


def prepare_last_kernel(early_ref, middle_ref, first_gates_ref, out_gates_ref, act_ref, three_ref, slope_ref):
    slope_ref[...] = slope(act_ref[...])
    col = lax.axis_index(("xh", "core"))
    tile = lax.axis_index(FACE)
    three_ref[GIVE_OWN : GIVE_OWN + CELLS] = early_ref[pl.ds(pl.multiple_of(GIVE + CELLS * col, CELLS), CELLS)]
    count = 9 * DEPTH
    gates = first_gates_ref[...].astype(F32).astype(BF)
    three_ref[FIRST_WIDE : FIRST_WIDE + count] = dot_tn(gates, repeat_four(HID // 4, HID)).astype(BF)
    place = lax.broadcasted_iota(jnp.int32, (32, 9 * HID), 0)
    mine = one_hot((32, 9 * HID), 1, jnp.where(place < 18, 18 * tile + place, -1))
    gates = bank_gates(middle_ref, MID_GATES, 64, range(9))
    three_ref[OWN_GATES : OWN_GATES + 32, :64] = dot_nt(mine, gates).astype(BF)
    gates = dot(eye(PADC, 4), out_gates_ref[...].astype(F32).astype(BF)).astype(BF)
    three_ref[OWN_GATES : OWN_GATES + 32, PADC:] = dot_nt(mine, gates).astype(BF)


def bank_gates(bank_ref, base, rows, blocks):
    step = max(rows, 16)
    return jnp.concatenate(
        [bank_ref[base + step * b : base + step * (b + 1)][:rows] for b in blocks], 1
    )


def start_kernel(line_ref, bank_ref, field_ref, grad_ref, strips_ref):
    comp = lax.axis_index("comp")
    for col in range(ROW):
        own = line_ref[comp, col].astype(F32)
        other = line_ref[1 - comp, col][:FIELDS].astype(F32)[:COUPLED]
        blank = jnp.zeros((32 - DEPTH, CELLS), F32)
        field = jnp.concatenate([own[:FIELDS], other, blank] * 3 + [jnp.zeros((32, CELLS), F32)], 0)
        field_ref[CELLS * col : CELLS * (col + 1)] = field.T.astype(BF)
        grad = jnp.concatenate([own[FIELDS:]] * 3 + [jnp.zeros((PADC - 3 * FIELDS, CELLS), F32)], 0)
        grad_ref[CELLS * col : CELLS * (col + 1)] = grad.T.astype(BF)
    strips_ref[...] = take_strips(bank_ref, field_ref)


def send_strips(strips, up_ref, down_ref, local_ref):
    up_ref[0:80] = strips[UP]
    down_ref[0:80] = strips[DOWN]
    local_ref[0:96] = strips[LOCAL]


def back_strips(prev_ref, next_ref, local_ref):
    return jnp.concatenate([next_ref[80:160], prev_ref[80:160], local_ref[96:192]], 0)


def layer_one_kernel(
    field_ref, strips_ref, prev_ref, next_ref, grad_ref, bank_ref,
    filled_ref, act_ref, hid_ref, local_ref, up_ref, down_ref, inner_ref,
):
    fill_packed(filled_ref, field_ref[...], strips_ref[LOCAL], prev_ref[...], next_ref[...])
    for col in range(ROW):
        act = conv_tile(filled_ref, bank_ref, FIRST_W, col)
        act_ref[CELLS * col : CELLS * (col + 1)] = act
        hid_ref[CELLS * col : CELLS * (col + 1)] = (act * sigmoid(act)).astype(BF)
    send_strips(take_strips(bank_ref, hid_ref), up_ref, down_ref, local_ref)
    fold_row(
        lambda col: pad_lines_packed(grad_ref[CELLS * col : CELLS * (col + 1)]),
        bank_ref, OUT_BACK, slice(None), inner_ref, down_ref.at[80:160], up_ref.at[80:160], local_ref.at[96:192],
    )


def layer_two_kernel(
    hid_ref, local_in_ref, prev_ref, next_ref, inner_two_ref, early_ref, middle_ref, bank_ref,
    filled_ref, grad_ref, hid_two_ref, local_ref, up_ref, down_ref, inner_ref,
    pad_ref,
):
    fill(filled_ref, hid_ref[...], local_in_ref[0:96], prev_ref[0:80], next_ref[0:80])
    strips = back_strips(prev_ref, next_ref, local_in_ref)
    for col in range(ROW):
        rows = slice(CELLS * col, CELLS * (col + 1))
        grad_hid = inner_two_ref[rows] + dot(early_ref[rows], strips)
        act = conv_tile(filled_ref, bank_ref, MID_W, col)
        sig = sigmoid(act)
        hid_two_ref[rows] = (act * sig).astype(BF)
        grad_ref[rows] = (grad_hid * (sig * (1.0 + act * (1.0 - sig)))).astype(BF)
    send_strips(take_strips(early_ref, hid_two_ref), up_ref, down_ref, local_ref)
    pad_ref[...] = jnp.zeros_like(pad_ref)
    fold_row(
        lambda col: pad_lines(grad_ref[CELLS * col : CELLS * (col + 1)], pad_ref),
        middle_ref, MID_BACK, slice(None), inner_ref, down_ref.at[80:160], up_ref.at[80:160], local_ref.at[96:192],
    )


def gather_rows(filled_ref, a):
    return jnp.concatenate(
        [filled_ref[col, a : a + TS].reshape(CELLS, filled_ref.shape[3]) for col in range(ROW)], 0
    )


def term_pairs(filled_ref, grad, gates_of, flat_ref):
    turned = dot_nt(plane_order(), grad).astype(BF)
    width = filled_ref.shape[3]
    for a in range(3):
        cols = slice(width * a, width * (a + 1))
        term = dot(turned, gather_rows(filled_ref, a))
        low, high = kept_pair([term[64 * m : 64 * (m + 1)] for m in range(4)], gates_of(a).astype(F32))
        flat_ref[0:64, cols] = low.astype(BF)
        flat_ref[64:128, cols] = high.astype(BF)


def mid_term_kernel(filled_ref, grad_ref, middle_ref, part_ref, pick_out_ref, pick_first_ref, flat_ref):
    col = lax.axis_index(("xh", "core"))
    term_pairs(
        filled_ref, grad_ref[...], lambda a: bank_gates(middle_ref, MID_GATES, 64, range(3 * a, 3 * a + 3)), flat_ref
    )
    shape = (16 * CHUNK, 1152)
    place = lax.broadcasted_iota(jnp.int32, shape, 0)
    block = (place * 2731) >> 16
    inside = place - CHUNK * block
    ahead = lax.broadcasted_iota(jnp.int32, shape, 1) - (72 * block + 18 * col)
    pick = ((ahead == inside) & (inside < 18)).astype(F32).astype(BF)
    late = ahead - 9 * (inside - 18)
    pick_out_ref[...] = ((late >= 0) & (late < 9) & (inside >= 18) & (inside < 20)).astype(F32).astype(BF)
    shape = (4 * SHARE, 3 * PADC)
    place = lax.broadcasted_iota(jnp.int32, shape, 0)
    inside = place & 15
    wanted = 14 * (4 * (place >> 4) + col) + inside
    tap = (wanted * 2731) >> 16
    third = (tap * 11) >> 5
    target = PADC * third + 32 * (tap - 3 * third) + wanted - DEPTH * tap
    real = (inside < 14) & (wanted < 9 * DEPTH)
    pick_first_ref[...] = ((lax.broadcasted_iota(jnp.int32, shape, 1) == target) & real).astype(F32).astype(BF)
    for half in range(2):
        part_ref[16 * CHUNK * half : 16 * CHUNK * (half + 1)] = dot_nt(
            pick, flat_ref[:, 1152 * half : 1152 * (half + 1)]
        )


def terms_kernel(
    hid_two_ref, local_ref, prev_ref, next_ref, inner_ref, slope_ref, filled_zero_ref, grad_three_ref, early_ref, bank_ref,
    part_ref, pick_out_ref, pick_first_ref,
    buffer_ref, mine_hbm, grad_ref,
    filled_ref, flat_ref, flat_zero_ref, sem,
):
    fill(filled_ref, hid_two_ref[...], local_ref[0:96], prev_ref[0:80], next_ref[0:80])
    keep = pltpu.make_async_copy(filled_ref.at[lax.axis_index(("xh", "core"))], mine_hbm, sem)
    keep.start()
    strips = back_strips(prev_ref, next_ref, local_ref)
    for col in range(ROW):
        rows = slice(CELLS * col, CELLS * (col + 1))
        grad_hid = inner_ref[rows] + dot(early_ref[rows], strips)
        grad_ref[rows] = (grad_hid * slope_ref[rows]).astype(BF)
    place = lax.broadcasted_iota(jnp.int32, (32, PADC), 0)
    group = place & 7
    wanted = jnp.where(group < 4, 4 * group + (place >> 3), -1)
    turned = dot_nt(one_hot((32, PADC), 1, wanted), grad_three_ref[...]).astype(BF)
    width = filled_ref.shape[3]
    for a in range(3):
        cols = slice(width * a, width * (a + 1))
        term = dot(turned, gather_rows(filled_ref, a))
        gates = bank_gates(bank_ref, OUT_GATES, 16, range(3 * a, 3 * a + 3)).astype(F32)[:8]
        low, high = kept_pair([term[8 * m : 8 * (m + 1)] for m in range(4)], gates)
        pair = low + pltpu.roll(high, 4, 0)
        wide = jnp.broadcast_to(pair[None], (16, 8, width)).reshape(128, width)
        kernel_row = lax.broadcasted_iota(jnp.int32, (128, width), 1) + width * a
        slot = kernel_row - 9 * ((kernel_row * 7282) >> 16)
        mine = (lax.broadcasted_iota(jnp.int32, (128, width), 0) >> 3) == slot
        flat_ref[:, cols] = jnp.where(mine, wide, 0.0).astype(BF)
    gates = [
        bank_ref[FIRST_GATES : FIRST_GATES + 64, :PADC], bank_ref[FIRST_GATES : FIRST_GATES + 64, PADC:],
        bank_ref[FIRST_GATES + 64 : FIRST_GATES + 128, :PADC],
    ]
    term_pairs(filled_zero_ref, grad_ref[...], lambda a: gates[a], flat_zero_ref)
    for half in range(2):
        rows = slice(16 * CHUNK * half, 16 * CHUNK * (half + 1))
        part = part_ref[rows] + dot_nt(pick_out_ref[...], flat_ref[:, 1152 * half : 1152 * (half + 1)])
        buffer_ref[16 * half : 16 * (half + 1), 0:CHUNK] = part.astype(BF).reshape(16, CHUNK, PADC)
    share = dot_nt(pick_first_ref[...], flat_zero_ref[...]).astype(BF)
    for place in range(ROWS):
        kind = place // 8
        buffer_ref[place, CHUNK : CHUNK + SHARE] = share[SHARE * kind : SHARE * (kind + 1)]
    keep.wait()


def last_kernel(
    mine_ref, grad_ref, bank_ref, state_ref, sea_ref,
    estimate_ref, dx_ref, up_ref, down_ref, local_ref,
    pad_ref, dx_all_ref, narrow_ref,
):
    for a in range(3):
        for b in range(3):
            at = FIRST_W + PADC * a + 32 * b
            block = jnp.concatenate([bank_ref[at : at + 32], jnp.zeros((PADC - 32, HID), BF)], 0)
            to = HID * (3 * b + a)
            narrow_ref[to : to + HID, :PADC] = dot_nt(eye(HID, HID), block).astype(BF)
            at = OUT_BACK + PADC * b + FIELDS * a
            block = jnp.concatenate([bank_ref[at : at + FIELDS], jnp.zeros((PADC - FIELDS, HID), BF)], 0)
            to = HID * (3 * a + b)
            narrow_ref[to : to + HID, PADC:] = dot_tn(block, eye(PADC, PADC)).astype(BF)
    comp = lax.axis_index("comp")
    col = lax.axis_index(("xh", "core"))
    width = mine_ref.shape[2]
    pad_ref[...] = jnp.zeros_like(pad_ref)
    fold_row(
        lambda col: pad_lines(grad_ref[CELLS * col : CELLS * (col + 1)], pad_ref),
        narrow_ref, 0, slice(0, PADC), dx_all_ref, down_ref, up_ref, local_ref,
    )
    dx_ref[...] = dx_all_ref[pl.ds(pl.multiple_of(col * CELLS, CELLS), CELLS)]
    total = None
    for a in range(3):
        weights = narrow_ref[width * a : width * (a + 1), PADC:]
        piece = dot(mine_ref[a : a + TS].reshape(CELLS, width), weights)
        total = piece if total is None else total + piece
    weight = jnp.where(comp == 1, sea_ref[...].astype(F32), 1.0)
    estimate_ref[...] = (state_ref[...].astype(F32) + weight * total.T[:FIELDS]).astype(BF)


def sum_kernel(spread_ref, share_ref, sum_ref):
    total = spread_ref[0].astype(F32)
    for place in range(1, ROWS):
        total = total + spread_ref[place].astype(F32)
    sum_ref[...] = total[:CHUNK]
    share = total[CHUNK:].astype(BF)
    for place in range(16):
        share_ref[place] = share


def finish_kernel(
    dx_ref, next_ref, prev_ref, local_ref, bank_ref, cot_ref, sum_ref,
    own_ref, send_ref, central_ref, closing_ref,
):
    give = bank_ref[GIVE_OWN : GIVE_OWN + CELLS]
    strips = jnp.concatenate([next_ref[...], prev_ref[...], local_ref[...]], 0)
    total = (dx_ref[...] + dot(give, strips)).T
    own_ref[...] = cot_ref[...].astype(F32) + total[:FIELDS]
    send_ref[...] = total[FIELDS : FIELDS + COUPLED]
    sums = sum_ref[...]
    repeat = repeat_four(HID // 4, HID)
    wide = dot(bank_ref[OWN_GATES : OWN_GATES + 32, :64], repeat)[:CHUNK]
    low, high = keep_of(wide, lax.broadcasted_iota(jnp.int32, (CHUNK, HID), 1) & 3)
    lows, highs = dot_exact_right(sums[:, :64], repeat), dot_exact_right(sums[:, 64:], repeat)
    central = jnp.where(low, lows, jnp.where(high, highs, 0.0))
    for line in range(18):
        central_ref[:, HID * line : HID * (line + 1)] = central[line : line + 1]
    place = lax.broadcasted_iota(jnp.int32, (CHUNK, CHUNK), 0)
    late = (place >= 9).astype(jnp.int32)
    spread = dot_exact(one_hot((CHUNK, CHUNK), 1, 18 + late), sums)
    place = lax.broadcasted_iota(jnp.int32, (CHUNK, PADC), 0)
    slot = place - 9 * (place >= 9).astype(jnp.int32)
    lane = lax.broadcasted_iota(jnp.int32, (CHUNK, PADC), 1)
    spread = jnp.where((lane >> 3) == slot, spread, 0.0)
    flat = 3 * PADC
    from_lane = lax.broadcasted_iota(jnp.int32, (PADC, flat), 0) & 7
    group = (lax.broadcasted_iota(jnp.int32, (PADC, flat), 1) & 15) >> 2
    lows = dot_exact_right(spread, (from_lane == group).astype(F32).astype(BF))
    highs = dot_exact_right(spread, (from_lane == group + 4).astype(F32).astype(BF))
    group = (lax.broadcasted_iota(jnp.int32, (PADC, flat), 1) & 15) >> 2
    wide = dot(bank_ref[OWN_GATES : OWN_GATES + 32, PADC:], one_hot((PADC, flat), 0, group))[:CHUNK]
    lane = lax.broadcasted_iota(jnp.int32, (CHUNK, flat), 1)
    low, high = keep_of(wide, lane & 3)
    closing = jnp.where(low, lows, jnp.where(high, highs, 0.0))
    here = lax.broadcasted_iota(jnp.int32, (CHUNK, flat), 0) == (lane >> 4)
    closing_ref[...] = jnp.sum(jnp.where(here, closing, 0.0), 0, keepdims=True)[:, : 18 * FIELDS]


def opening_kernel(share_ref, bank_ref, out_ref):
    count = 9 * (FIELDS + COUPLED)
    wanted = lax.broadcasted_iota(jnp.int32, (count, 16 * SHARE), 0)
    block = (wanted * 4682) >> 16
    pick = one_hot((count, 16 * SHARE), 1, SHARE * block + wanted - 14 * block)
    pairs = dot(pick, share_ref[...]).astype(BF)
    repeat = repeat_four(HID // 4, HID)
    low, high = keep_of(bank_ref[FIRST_WIDE : FIRST_WIDE + count].astype(F32), lax.broadcasted_iota(jnp.int32, (count, HID), 1) & 3)
    out_ref[...] = jnp.where(low, dot(pairs[:, :64], repeat), jnp.where(high, dot(pairs[:, 64:], repeat), 0.0))


VMEM = pl.BlockSpec(memory_space=pltpu.VMEM)
SMEM = pl.BlockSpec(memory_space=pltpu.SMEM)
HBM = pl.BlockSpec(memory_space=pltpu.HBM)


def call(body, out, args, scratch=(), scalars=(), far=(), far_out=(), flops=0, limit=10):
    args = [pltpu.with_memory_space_constraint(arg, pltpu.HBM) if place in far else arg for place, arg in enumerate(args)]
    specs = [SMEM if place in scalars else HBM if place in far else VMEM for place in range(len(args))]
    size = sum(int(np.prod(item.shape)) * item.dtype.itemsize for item in list(args) + list(out))
    return pl.pallas_call(
        body,
        out_shape=[jax.ShapeDtypeStruct(item.shape, item.dtype) for item in out],
        in_specs=specs,
        out_specs=[HBM if place in far_out else VMEM for place in range(len(out))],
        scratch_shapes=list(scratch),
        compiler_params=pltpu.CompilerParams(vmem_limit_bytes=limit * 1024 * 1024),
        cost_estimate=pl.CostEstimate(flops=flops, bytes_accessed=size, transcendentals=0),
    )(*args)


def sds(shape, kind):
    return jax.ShapeDtypeStruct(shape, kind)


def row_shift(value, step):
    pairs = [(face, (face + ROW * step) % TILES) for face in range(TILES)]
    return lax.ppermute(value, FACE, pairs)


def body(
    state, cotangent, land_sea, turn_table, first_kernel, mid_kernel, out_kernel, first_gates, mid_gates, out_gates
):
    sea = land_sea.reshape(1, CELLS)

    packed = call(pack_kernel, [sds((8, 2 * FIELDS, CELLS), BF)], [state[0], cotangent[0], sea],
        scratch=[
            pltpu.VMEM((FIELDS, CELLS), BF), pltpu.VMEM((FIELDS, CELLS), BF), pltpu.VMEM((1, CELLS), jnp.int32),
            pltpu.SemaphoreType.DMA((3,)),
        ],
        far=(0, 1, 2),
    )[0]
    line = lax.all_to_all(packed, LINE_AXES, 0, 0).reshape(2, ROW, 2 * FIELDS, CELLS)

    turns, out_turned = turn_table.T, out_gates[0].T
    first_turned, mid_turned = first_gates[0].T, mid_gates[0].T
    early, middle = call(
        prepare_early_kernel, [sds((BANK_ONE, HID), BF), sds((BANK_MID, HID), BF)],
        [turns, first_turned, out_turned, first_kernel[0], out_kernel[0].T, mid_turned, mid_kernel[0]],
        scratch=[
            pltpu.SMEM((4, TILES), jnp.int32), pltpu.VMEM((64, 9 * DEPTH), jnp.int32),
            pltpu.VMEM((4, 9 * HID), jnp.int32), pltpu.VMEM((9 * DEPTH, HID), BF),
            pltpu.VMEM((FIELDS, 9 * HID), BF), pltpu.VMEM((64, 9 * HID), jnp.int32),
            pltpu.VMEM((9 * HID, HID), BF), pltpu.SemaphoreType.DMA((7,)),
        ],
        far=(0, 1, 2, 3, 4, 5, 6), flops=5 * 10**9,
    )

    field, grad_cells, strips_zero = call(
        start_kernel,
        [sds((LINE, PADC), BF), sds((LINE, PADC), BF), sds((256, PADC), BF)], [line, early],
    )
    prev_zero = row_shift(strips_zero[UP], 1)
    next_zero = row_shift(strips_zero[DOWN], -1)
    two = call(
        prepare_late_kernel, [sds((BANK_TWO, HID), BF)], [middle, first_turned, out_turned],
        scratch=[
            pltpu.VMEM((64, 9 * DEPTH), jnp.int32), pltpu.VMEM((4, 9 * HID), jnp.int32),
            pltpu.SemaphoreType.DMA((2,)),
        ],
        far=(1, 2), flops=10**9,
    )[0]
    exchange = [sds((192, HID), BF), sds((160, HID), BF), sds((160, HID), BF), sds((LINE, HID), F32)]
    filled_zero, act_one, hid_one, local_one, up_one, down_one, inner_two = call(
        layer_one_kernel,
        [sds((ROW, TS + 2, TS, PADC), BF), sds((LINE, HID), F32), sds((LINE, HID), BF)] + exchange,
        [field, strips_zero, prev_zero, next_zero, grad_cells, early],
    )
    prev_one = row_shift(up_one, 1)
    next_one = row_shift(down_one, -1)

    three, slope_one = call(
        prepare_last_kernel, [sds((BANK_THREE, HID), BF), sds((LINE, HID), F32)],
        [early, middle, first_turned, out_turned, act_one], flops=10**9,
    )

    filled_one, grad_two, hid_two, local_two, up_two, down_two, inner_one = call(
        layer_two_kernel,
        [sds((ROW, TS + 2, TS, 3 * HID), BF), sds((LINE, HID), BF), sds((LINE, HID), BF)] + exchange,
        [hid_one, local_one, prev_one, next_one, inner_two, early, middle, two],
        scratch=[pltpu.VMEM((TS + 2, TS, 3 * HID), BF)],
    )
    prev_two = row_shift(up_two, 1)
    next_two = row_shift(down_two, -1)

    part, pick_out, pick_first = call(
        mid_term_kernel,
        [sds((32 * CHUNK, PADC), F32), sds((16 * CHUNK, 1152), BF), sds((4 * SHARE, 3 * PADC), BF)],
        [filled_one, grad_two, middle],
        scratch=[pltpu.VMEM((PADC, 9 * HID), BF)], flops=2 * 10**9,
    )

    buffer, mine_two, grad_one = call(
        terms_kernel,
        [sds((ROWS, CHUNK + SHARE, PADC), BF), sds((TS + 2, TS, 3 * HID), BF), sds((LINE, HID), BF)],
        [hid_two, local_two, prev_two, next_two, inner_one, slope_one, filled_zero, grad_cells, early, two,
         part, pick_out, pick_first],
        scratch=[
            pltpu.VMEM((ROW, TS + 2, TS, 3 * HID), BF), pltpu.VMEM((PADC, 9 * HID), BF),
            pltpu.VMEM((PADC, 3 * PADC), BF), pltpu.SemaphoreType.DMA,
        ],
        far_out=(1,),
    )
    spread = lax.all_to_all(buffer, ROW_AXES, 0, 0)

    estimate, dx_own, up_three, down_three, local_three = call(
        last_kernel,
        [sds((FIELDS, CELLS), BF), sds((CELLS, PADC), F32), sds((80, PADC), BF), sds((80, PADC), BF),
         sds((96, PADC), BF)],
        [mine_two, grad_one, early, state[0], sea],
        scratch=[
            pltpu.VMEM((TS + 2, TS, 3 * HID), BF), pltpu.VMEM((LINE, PADC), F32),
            pltpu.VMEM((9 * HID, HID), BF),
        ],
        flops=2 * 10**9,
    )
    prev_three = row_shift(up_three, 1)
    next_three = row_shift(down_three, -1)

    shared, summed = call(sum_kernel, [sds((16, SHARE, PADC), BF), sds((CHUNK, PADC), F32)], [spread])
    opened = lax.all_to_all(shared, ("y", "xh", "core"), 0, 0).reshape(16 * SHARE, PADC)

    own, send, central, closing = call(
        finish_kernel,
        [sds((FIELDS, CELLS), F32), sds((COUPLED, CELLS), F32), sds((1, 18 * HID), F32), sds((1, 18 * FIELDS), F32)],
        [dx_own, next_three, prev_three, local_three, three, cotangent[0], summed],
    )
    returned = lax.ppermute(send, "comp", [(0, 1), (1, 0)])
    adjoint = own + jnp.pad(returned, ((0, FIELDS - COUPLED), (0, 0)))
    opening = call(opening_kernel, [sds((9 * DEPTH, HID), F32)], [opened, three])[0]
    return estimate[None], adjoint[None], opening[None], central, closing


def solution(mesh):
    fine = Mesh(mesh.devices.reshape(2, 4, 8, 2, 2), ("comp",) + FACE)
    whole = P("comp", None, None)
    in_specs = (P("comp", None, FACE), P("comp", None, FACE), P(FACE), P()) + (whole,) * 6
    out_specs = (P("comp", None, FACE), P("comp", None, FACE), whole, P("comp", FACE), P("comp", FACE))

    return jax.shard_map(body, mesh=fine, in_specs=in_specs, out_specs=out_specs, check_vma=False)
```

```python
import jax
import jax.numpy as jnp
import numpy as np
from jax import lax
from jax.experimental import pallas as pl
from jax.experimental.pallas import tpu as pltpu
from jax.sharding import Mesh, PartitionSpec as P


FIELDS = 16
COUPLED = 8
TS = 16
CELLS = TS * TS
ROW = 4
ROWS = 32
TILES = ROW * ROWS
LINE = ROW * CELLS
HID = 256
PADC = 128
CHUNK = 24
SHARE = 16
DEPTH = FIELDS + COUPLED

GIVE = 0
TAKE = GIVE + LINE
FIRST_W = TAKE + LINE
OUT_BACK = FIRST_W + 3 * PADC
BANK_ONE = OUT_BACK + 3 * PADC
MID_BACK = 0
MID_GATES = MID_BACK + 9 * HID
BANK_MID = MID_GATES + 9 * 64
MID_W = 0
FIRST_GATES = MID_W + 9 * HID
OUT_GATES = FIRST_GATES + 2 * 64
BANK_TWO = OUT_GATES + 9 * 16
FIRST_WIDE = 0
GIVE_OWN = FIRST_WIDE + 224
OWN_GATES = GIVE_OWN + CELLS
BANK_THREE = OWN_GATES + 32
BF = jnp.bfloat16
F32 = jnp.float32

FACE = ("y", "z", "xh", "core")
ROW_AXES = ("y", "z")
LINE_AXES = ("comp", "xh", "core")

EDGE_MAP = (
    ((0, False), (2, True), (1, True), (3, False)),
    ((1, False), (3, True), (0, True), (2, False)),
    ((2, False), (1, False), (3, True), (0, True)),
    ((3, False), (0, False), (2, True), (1, True)),
)

STRIPS = (
    [(col, 2, 8 + col) for col in range(4)]
    + [(3, 0, 8)]
    + [(col, 3, col) for col in range(4)]
    + [(0, 1, 3)]
    + [(col - 1, 0, 4 + col) for col in (1, 2, 3)]
    + [(col + 1, 1, 4 + col) for col in (0, 1, 2)]
)


def edge_line(slot, flip):
    first, step = ((TS - 1, TS), (0, TS), ((TS - 1) * TS, 1), (0, 1))[slot]
    if flip:
        first, step = first + (TS - 1) * step, -step
    return first, step


def dot(left, right):
    return jnp.dot(left, right, preferred_element_type=F32)


def dot_nt(left, right):
    return lax.dot_general(left, right, (((1,), (1,)), ((), ())), preferred_element_type=F32)


def dot_tn(left, right):
    return lax.dot_general(left, right, (((0,), (0,)), ((), ())), preferred_element_type=F32)


def dot_exact(left, right):
    high = right.astype(BF)
    rest = right - high.astype(F32)
    mid = rest.astype(BF)
    low = (rest - mid.astype(F32)).astype(BF)
    return dot(left, high) + (dot(left, mid) + dot(left, low))


def dot_exact_right(left, right):
    high = left.astype(BF)
    rest = left - high.astype(F32)
    mid = rest.astype(BF)
    low = (rest - mid.astype(F32)).astype(BF)
    return dot(high, right) + (dot(mid, right) + dot(low, right))


def fetch(sources, buffers, sems):
    copies = [
        pltpu.make_async_copy(source, buffer, sems.at[place])
        for place, (source, buffer) in enumerate(zip(sources, buffers))
    ]
    for copy in copies:
        copy.start()
    return copies


def one_hot(shape, axis, index):
    return (lax.broadcasted_iota(jnp.int32, shape, axis) == index).astype(F32).astype(BF)


def shift_cells(value, step, axis):
    along = lax.broadcasted_iota(jnp.int32, value.shape, axis)
    moved = pltpu.roll(value, step % TS, axis)
    edge = 0 if step == 1 else TS - 1
    return jnp.where(along == edge, 0.0, moved)


def shift_lines(lines, step, strip):
    along = lax.broadcasted_iota(jnp.int32, lines.shape, 1)
    moved = pltpu.roll(lines, step % TS, 1)
    edge = 0 if step == 1 else TS - 1
    return jnp.where(along == edge, jnp.broadcast_to(strip.astype(F32)[:, None, :], lines.shape), moved)


def fill(out_ref, tiles, local, from_prev, from_next):
    depth = tiles.shape[1]
    for col in range(ROW):
        south = from_prev[TS * col : TS * (col + 1)]
        north = from_next[TS * col : TS * (col + 1)]
        west = from_prev[4 * TS : 5 * TS] if col == 0 else local[TS * (col - 1) : TS * col]
        east = from_next[4 * TS : 5 * TS] if col == 3 else local[TS * (3 + col) : TS * (4 + col)]
        own = tiles[CELLS * col : CELLS * (col + 1)]
        wide = own.astype(F32).reshape(TS, TS, depth)
        left = shift_lines(wide, 1, west)
        right = shift_lines(wide, -1, east)
        out_ref[col, 1 : TS + 1, :, 0:depth] = left.astype(BF)
        out_ref[col, 1 : TS + 1, :, depth : 2 * depth] = own.reshape(TS, TS, depth)
        out_ref[col, 1 : TS + 1, :, 2 * depth : 3 * depth] = right.astype(BF)
        for line, strip in ((0, south), (TS + 1, north)):
            wide = strip.astype(F32)
            out_ref[col, line, :, 0:depth] = shift_cells(wide, 1, 0).astype(BF)
            out_ref[col, line, :, depth : 2 * depth] = strip
            out_ref[col, line, :, 2 * depth : 3 * depth] = shift_cells(wide, -1, 0).astype(BF)


def fill_packed(out_ref, tiles, local, from_prev, from_next):
    def choose(left, own, right):
        lane = lax.broadcasted_iota(jnp.int32, own.shape, own.ndim - 1)
        return jnp.where(lane < 32, left, jnp.where(lane < 64, own, right)).astype(BF)

    for col in range(ROW):
        south = from_prev[TS * col : TS * (col + 1)]
        north = from_next[TS * col : TS * (col + 1)]
        west = from_prev[4 * TS : 5 * TS] if col == 0 else local[TS * (col - 1) : TS * col]
        east = from_next[4 * TS : 5 * TS] if col == 3 else local[TS * (3 + col) : TS * (4 + col)]
        wide = tiles[CELLS * col : CELLS * (col + 1)].astype(F32).reshape(TS, TS, PADC)
        left = shift_lines(wide, 1, west)
        right = shift_lines(wide, -1, east)
        out_ref[col, 1 : TS + 1] = choose(left, wide, right)
        for line, strip in ((0, south), (TS + 1, north)):
            wide = strip.astype(F32)
            out_ref[col, line] = choose(shift_cells(wide, 1, 0), wide, shift_cells(wide, -1, 0))


def take_strips(bank_ref, cells_ref):
    total = None
    for col in range(ROW):
        block = slice(TAKE + CELLS * col, TAKE + CELLS * (col + 1))
        piece = dot(bank_ref[block], cells_ref[CELLS * col : CELLS * (col + 1)])
        total = piece if total is None else total + piece
    return total.astype(BF)


def conv_tile(filled_ref, bank_ref, base, col, lanes=slice(None)):
    width = filled_ref.shape[3]
    total = None
    for a in range(3):
        weights = bank_ref[base + width * a : base + width * (a + 1), lanes]
        piece = dot(filled_ref[col, a : a + TS].reshape(CELLS, width), weights)
        total = piece if total is None else total + piece
    return total


def pad_lines(grad, pad_ref):
    deep = grad.shape[1]
    lines = grad.reshape(TS, TS, deep)
    for a in range(3):
        pad_ref[a : a + TS, :, deep * a : deep * (a + 1)] = lines
    return pad_ref[...].reshape((TS + 2) * TS, 3 * deep)


def pad_lines_packed(grad):
    lines = grad.astype(F32).reshape(TS, TS, PADC)
    blank = jnp.zeros((1, TS, PADC), F32)
    lane = lax.broadcasted_iota(jnp.int32, (TS + 2, TS, PADC), 2)
    one, two, three = (
        jnp.concatenate([blank] * a + [lines] + [blank] * (2 - a), 0) for a in range(3)
    )
    padded = jnp.where(lane < 16, one, jnp.where(lane < 32, two, three))
    return padded.reshape((TS + 2) * TS, PADC).astype(BF)


def fold_tile(padded, bank_ref, base, lanes):
    deep = padded.shape[1]
    left, mid, right = (
        dot(padded, bank_ref[base + deep * b : base + deep * (b + 1), lanes]) for b in range(3)
    )
    depth = mid.shape[1]
    left, mid, right = (part.reshape(TS + 2, TS, depth) for part in (left, mid, right))
    merged = mid + shift_cells(left, -1, 1) + shift_cells(right, 1, 1)
    inner = merged[1 : TS + 1].reshape(CELLS, depth)
    south = merged[0].astype(BF)
    north = merged[TS + 1].astype(BF)
    west = left[1 : TS + 1, 0, :].astype(BF)
    east = right[1 : TS + 1, TS - 1, :].astype(BF)
    return inner, south, north, west, east


def fold_row(padded_of, bank_ref, base, lanes, inner_ref, prev_ref, next_ref, local_ref):
    for col in range(ROW):
        inner, south, north, west, east = fold_tile(padded_of(col), bank_ref, base, lanes)
        inner_ref[CELLS * col : CELLS * (col + 1)] = inner
        prev_ref[TS * col : TS * (col + 1)] = south
        next_ref[TS * col : TS * (col + 1)] = north
        if col == 0:
            prev_ref[4 * TS : 5 * TS] = west
        else:
            local_ref[TS * (col - 1) : TS * col] = west
        if col == 3:
            next_ref[4 * TS : 5 * TS] = east
        else:
            local_ref[TS * (3 + col) : TS * (4 + col)] = east


def sigmoid(values):
    return 1.0 / (1.0 + jnp.exp(-values))


def slope(values):
    sig = sigmoid(values)
    return sig * (1.0 + values * (1.0 - sig))


UP = slice(0, 80)
DOWN = slice(80, 160)
LOCAL = slice(160, 256)


def keep_of(wide, lane):
    low = jnp.where(wide >= 4.5, 2, jnp.where(wide >= 2.5, 1, 0))
    high = jnp.where(wide < 0.5, 1, jnp.where((wide < 1.5) | ((wide > 2.5) & (wide < 3.5)), 2, 3))
    return lane == low, lane == high


def kept_pair(planes, gates):
    one, two, three, four = planes
    low = jnp.where(gates >= 4.5, three, jnp.where(gates >= 2.5, two, one))
    high = jnp.where(gates < 0.5, two, jnp.where((gates < 1.5) | ((gates > 2.5) & (gates < 3.5)), three, four))
    return low, high


def eye(rows, cols):
    return one_hot((rows, cols), 1, lax.broadcasted_iota(jnp.int32, (rows, cols), 0))


def repeat_four(groups, width):
    rows = lax.broadcasted_iota(jnp.int32, (groups, width), 0)
    cols = lax.broadcasted_iota(jnp.int32, (groups, width), 1)
    return ((cols >> 2) == rows).astype(F32).astype(BF)


def plane_order():
    rows = lax.broadcasted_iota(jnp.int32, (HID, HID), 0)
    return one_hot((HID, HID), 1, 4 * (rows & 63) + (rows >> 6))


def pack_kernel(state_hbm, cot_hbm, sea_hbm, out_ref, state_ref, cot_ref, sea_ref, sems):
    copies = fetch((state_hbm, cot_hbm, sea_hbm), (state_ref, cot_ref, sea_ref), sems)
    for copy in copies:
        copy.wait()
    comp = lax.axis_index("comp")
    weight = jnp.where(comp == 1, sea_ref[...].astype(F32), 1.0)
    grad = (weight * cot_ref[...].astype(F32)).astype(BF)
    for place in range(8):
        out_ref[place, 0:FIELDS] = state_ref[...]
        out_ref[place, FIELDS : 2 * FIELDS] = grad


def kept_rows(gates, kernel):
    outputs = kernel.shape[0]
    rows = lax.broadcasted_iota(jnp.int32, (outputs, outputs // 4), 0) >> 2
    repeat = one_hot((outputs, outputs // 4), 1, rows)
    low = jnp.where(gates >= 4.5, 2.0, jnp.where(gates >= 2.5, 1.0, 0.0)).astype(BF)
    high = jnp.where(gates < 0.5, 1.0, jnp.where((gates < 1.5) | ((gates > 2.5) & (gates < 3.5)), 2.0, 3.0)).astype(BF)
    lane = (lax.broadcasted_iota(jnp.int32, kernel.shape, 0) & 3).astype(F32)
    return jnp.where((dot(repeat, low) == lane) | (dot(repeat, high) == lane), kernel, 0.0)


def prepare_early_kernel(
    turn_hbm, first_gates_hbm, out_gates_hbm, first_hbm, out_hbm, mid_gates_hbm, mid_hbm, bank_ref, middle_ref,
    turn_ref, first_gates_ref, out_gates_ref, first_ref, out_ref, mid_gates_ref, mid_ref, sems,
):
    copies = fetch(
        (turn_hbm, first_gates_hbm, out_gates_hbm, first_hbm, out_hbm, mid_gates_hbm, mid_hbm),
        (turn_ref, first_gates_ref, out_gates_ref, first_ref, out_ref, mid_gates_ref, mid_ref), sems,
    )
    copies[0].wait()
    row = lax.axis_index(ROW_AXES)
    strip_of = lax.broadcasted_iota(jnp.int32, (8, 256), 1) >> 4
    along = lax.broadcasted_iota(jnp.int32, (8, 256), 1) & 15
    cells = jnp.zeros((8, 256), jnp.int32)
    for number, (source, side, reader) in enumerate(STRIPS):
        turn = turn_ref[side, lax.rem(ROW * row + reader - ROW + TILES, TILES)]
        first, step = edge_line(*EDGE_MAP[side][3])
        for turns in range(3):
            one, two = edge_line(*EDGE_MAP[side][turns])
            first, step = jnp.where(turn == turns, one, first), jnp.where(turn == turns, two, step)
        first = first + source * CELLS
        cells = jnp.where(strip_of == number, first + step * along, cells)
        place = lax.broadcasted_iota(jnp.int32, (TS, LINE), 1)
        wanted = first + step * lax.broadcasted_iota(jnp.int32, (TS, LINE), 0)
        hit = (place == wanted).astype(F32).astype(BF)
        for col in range(ROW):
            at = TAKE + CELLS * col + TS * number
            bank_ref[at : at + TS] = hit[:, CELLS * col : CELLS * (col + 1)]
    bank_ref[GIVE : GIVE + LINE] = one_hot((LINE, 256), 0, cells[0:1])
    for copy in copies[1:]:
        copy.wait()
    count = 9 * DEPTH
    wide = dot_tn(first_gates_ref[...].astype(F32).astype(BF), repeat_four(HID // 4, HID))
    low, high = keep_of(wide, lax.broadcasted_iota(jnp.int32, (count, HID), 1) & 3)
    kernel = jnp.where(low | high, first_ref[...].astype(F32), 0.0)
    blank = jnp.zeros((32 - DEPTH, HID), F32)
    kernel_out = kept_rows(out_gates_ref[...].astype(F32), out_ref[...].astype(F32)).astype(BF)
    for a in range(3):
        pieces = []
        for b in range(3):
            tap = 3 * a + b
            pieces += [kernel[DEPTH * tap : DEPTH * (tap + 1)], blank]
            at = OUT_BACK + PADC * b + FIELDS * a
            bank_ref[at : at + FIELDS] = kernel_out[:, HID * tap : HID * (tap + 1)]
        pieces.append(jnp.zeros((32, HID), F32))
        bank_ref[FIRST_W + PADC * a : FIRST_W + PADC * (a + 1)] = jnp.concatenate(pieces, 0).astype(BF)
        bank_ref[OUT_BACK + PADC * a + 48 : OUT_BACK + PADC * (a + 1)] = jnp.zeros((PADC - 48, HID), BF)
    for tap in range(9):
        cols = slice(HID * tap, HID * (tap + 1))
        gates = mid_gates_ref[:, cols].astype(F32)
        middle_ref[MID_GATES + 64 * tap : MID_GATES + 64 * (tap + 1)] = gates.astype(BF)
        at = MID_BACK + HID * (3 * (tap % 3) + tap // 3)
        middle_ref[at : at + HID] = kept_rows(gates, dot_nt(eye(HID, HID), mid_ref[cols])).astype(BF)


def prepare_late_kernel(middle_ref, first_gates_hbm, out_gates_hbm, two_ref, first_gates_ref, out_gates_ref, sems):
    copies = fetch((first_gates_hbm, out_gates_hbm), (first_gates_ref, out_gates_ref), sems)
    for a in range(3):
        for b in range(3):
            at = MID_BACK + HID * (3 * b + a)
            to = MID_W + HID * (3 * a + b)
            two_ref[to : to + HID] = dot_tn(middle_ref[at : at + HID], eye(HID, HID)).astype(BF)
    for copy in copies:
        copy.wait()
    count = 9 * DEPTH
    place = lax.broadcasted_iota(jnp.int32, (count, 3 * PADC), 0)
    tap = (place * 2731) >> 16
    third = (tap * 11) >> 5
    target = PADC * third + 32 * (tap - 3 * third) + place - DEPTH * tap
    gates = first_gates_ref[...].astype(F32).astype(BF)
    spread = dot(gates, one_hot((count, 3 * PADC), 1, target)).astype(BF)
    two_ref[FIRST_GATES : FIRST_GATES + 64] = spread[:, :HID]
    two_ref[FIRST_GATES + 64 : FIRST_GATES + 128, :PADC] = spread[:, HID:]
    gates = dot(eye(16, 4), out_gates_ref[...].astype(F32).astype(BF)).astype(BF)
    for tap in range(9):
        two_ref[OUT_GATES + 16 * tap : OUT_GATES + 16 * (tap + 1)] = gates[:, HID * tap : HID * (tap + 1)]


def prepare_last_kernel(early_ref, middle_ref, first_gates_ref, out_gates_ref, act_ref,
    three_ref, slope_ref, pick_ref, pick_out_ref, pick_first_ref):
    slope_ref[...] = slope(act_ref[...])
    col = lax.axis_index(("xh", "core"))
    tile = lax.axis_index(FACE)
    shape = (16 * CHUNK, 1152)
    place = lax.broadcasted_iota(jnp.int32, shape, 0)
    block = (place * 2731) >> 16
    inside = place - CHUNK * block
    ahead = lax.broadcasted_iota(jnp.int32, shape, 1) - (72 * block + 18 * col)
    pick_ref[...] = ((ahead == inside) & (inside < 18)).astype(F32).astype(BF)
    late = ahead - 9 * (inside - 18)
    pick_out_ref[...] = ((late >= 0) & (late < 9) & (inside >= 18) & (inside < 20)).astype(F32).astype(BF)
    shape = (4 * SHARE, 3 * PADC)
    place = lax.broadcasted_iota(jnp.int32, shape, 0)
    inside = place & 15
    wanted = 14 * (4 * (place >> 4) + col) + inside
    tap = (wanted * 2731) >> 16
    third = (tap * 11) >> 5
    target = PADC * third + 32 * (tap - 3 * third) + wanted - DEPTH * tap
    real = (inside < 14) & (wanted < 9 * DEPTH)
    pick_first_ref[...] = ((lax.broadcasted_iota(jnp.int32, shape, 1) == target) & real).astype(F32).astype(BF)
    three_ref[GIVE_OWN : GIVE_OWN + CELLS] = early_ref[pl.ds(pl.multiple_of(GIVE + CELLS * col, CELLS), CELLS)]
    count = 9 * DEPTH
    gates = first_gates_ref[...].astype(F32).astype(BF)
    three_ref[FIRST_WIDE : FIRST_WIDE + count] = dot_tn(gates, repeat_four(HID // 4, HID)).astype(BF)
    place = lax.broadcasted_iota(jnp.int32, (32, 9 * HID), 0)
    mine = one_hot((32, 9 * HID), 1, jnp.where(place < 18, 18 * tile + place, -1))
    gates = bank_gates(middle_ref, MID_GATES, 64, range(9))
    three_ref[OWN_GATES : OWN_GATES + 32, :64] = dot_nt(mine, gates).astype(BF)
    gates = dot(eye(PADC, 4), out_gates_ref[...].astype(F32).astype(BF)).astype(BF)
    three_ref[OWN_GATES : OWN_GATES + 32, PADC:] = dot_nt(mine, gates).astype(BF)


def bank_gates(bank_ref, base, rows, blocks):
    step = max(rows, 16)
    return jnp.concatenate(
        [bank_ref[base + step * b : base + step * (b + 1)][:rows] for b in blocks], 1
    )


def start_kernel(line_ref, bank_ref, field_ref, grad_ref, strips_ref):
    comp = lax.axis_index("comp")
    for col in range(ROW):
        own = line_ref[comp, col].astype(F32)
        other = line_ref[1 - comp, col][:FIELDS].astype(F32)[:COUPLED]
        blank = jnp.zeros((32 - DEPTH, CELLS), F32)
        field = jnp.concatenate([own[:FIELDS], other, blank] * 3 + [jnp.zeros((32, CELLS), F32)], 0)
        field_ref[CELLS * col : CELLS * (col + 1)] = field.T.astype(BF)
        grad = jnp.concatenate([own[FIELDS:]] * 3 + [jnp.zeros((PADC - 3 * FIELDS, CELLS), F32)], 0)
        grad_ref[CELLS * col : CELLS * (col + 1)] = grad.T.astype(BF)
    strips_ref[...] = take_strips(bank_ref, field_ref)


def send_strips(strips, up_ref, down_ref, local_ref):
    up_ref[0:80] = strips[UP]
    down_ref[0:80] = strips[DOWN]
    local_ref[0:96] = strips[LOCAL]


def back_strips(prev_ref, next_ref, local_ref):
    return jnp.concatenate([next_ref[80:160], prev_ref[80:160], local_ref[96:192]], 0)


def layer_one_kernel(
    field_ref, strips_ref, prev_ref, next_ref, grad_ref, bank_ref,
    filled_ref, act_ref, hid_ref, local_ref, up_ref, down_ref, inner_ref,
):
    fill_packed(filled_ref, field_ref[...], strips_ref[LOCAL], prev_ref[...], next_ref[...])
    for col in range(ROW):
        act = conv_tile(filled_ref, bank_ref, FIRST_W, col)
        act_ref[CELLS * col : CELLS * (col + 1)] = act
        hid_ref[CELLS * col : CELLS * (col + 1)] = (act * sigmoid(act)).astype(BF)
    send_strips(take_strips(bank_ref, hid_ref), up_ref, down_ref, local_ref)
    fold_row(
        lambda col: pad_lines_packed(grad_ref[CELLS * col : CELLS * (col + 1)]),
        bank_ref, OUT_BACK, slice(None), inner_ref, down_ref.at[80:160], up_ref.at[80:160], local_ref.at[96:192],
    )


def layer_two_kernel(
    hid_ref, local_in_ref, prev_ref, next_ref, inner_two_ref, early_ref, middle_ref, bank_ref,
    filled_ref, grad_ref, hid_two_ref, local_ref, up_ref, down_ref, inner_ref,
    pad_ref,
):
    fill(filled_ref, hid_ref[...], local_in_ref[0:96], prev_ref[0:80], next_ref[0:80])
    strips = back_strips(prev_ref, next_ref, local_in_ref)
    for col in range(ROW):
        rows = slice(CELLS * col, CELLS * (col + 1))
        grad_hid = inner_two_ref[rows] + dot(early_ref[rows], strips)
        act = conv_tile(filled_ref, bank_ref, MID_W, col)
        sig = sigmoid(act)
        hid_two_ref[rows] = (act * sig).astype(BF)
        grad_ref[rows] = (grad_hid * (sig * (1.0 + act * (1.0 - sig)))).astype(BF)
    send_strips(take_strips(early_ref, hid_two_ref), up_ref, down_ref, local_ref)
    pad_ref[...] = jnp.zeros_like(pad_ref)
    fold_row(
        lambda col: pad_lines(grad_ref[CELLS * col : CELLS * (col + 1)], pad_ref),
        middle_ref, MID_BACK, slice(None), inner_ref, down_ref.at[80:160], up_ref.at[80:160], local_ref.at[96:192],
    )


def gather_rows(filled_ref, a):
    return jnp.concatenate(
        [filled_ref[col, a : a + TS].reshape(CELLS, filled_ref.shape[3]) for col in range(ROW)], 0
    )


def term_pairs(filled_ref, grad, gates_of, flat_ref):
    turned = dot_nt(plane_order(), grad).astype(BF)
    width = filled_ref.shape[3]
    for a in range(3):
        cols = slice(width * a, width * (a + 1))
        term = dot(turned, gather_rows(filled_ref, a))
        low, high = kept_pair([term[64 * m : 64 * (m + 1)] for m in range(4)], gates_of(a).astype(F32))
        flat_ref[0:64, cols] = low.astype(BF)
        flat_ref[64:128, cols] = high.astype(BF)


def mid_term_kernel(filled_ref, grad_ref, middle_ref, pick_ref, part_ref, flat_ref):
    term_pairs(
        filled_ref, grad_ref[...], lambda a: bank_gates(middle_ref, MID_GATES, 64, range(3 * a, 3 * a + 3)), flat_ref
    )
    for half in range(2):
        part_ref[16 * CHUNK * half : 16 * CHUNK * (half + 1)] = dot_nt(
            pick_ref[...], flat_ref[:, 1152 * half : 1152 * (half + 1)]
        )


def terms_kernel(
    hid_two_ref, local_ref, prev_ref, next_ref, inner_ref, slope_ref, filled_zero_ref, grad_three_ref, early_ref, bank_ref,
    part_ref, pick_out_ref, pick_first_ref,
    buffer_ref, mine_hbm, grad_ref,
    filled_ref, flat_ref, flat_zero_ref, sem,
):
    fill(filled_ref, hid_two_ref[...], local_ref[0:96], prev_ref[0:80], next_ref[0:80])
    keep = pltpu.make_async_copy(filled_ref.at[lax.axis_index(("xh", "core"))], mine_hbm, sem)
    keep.start()
    strips = back_strips(prev_ref, next_ref, local_ref)
    for col in range(ROW):
        rows = slice(CELLS * col, CELLS * (col + 1))
        grad_hid = inner_ref[rows] + dot(early_ref[rows], strips)
        grad_ref[rows] = (grad_hid * slope_ref[rows]).astype(BF)
    place = lax.broadcasted_iota(jnp.int32, (32, PADC), 0)
    group = place & 7
    wanted = jnp.where(group < 4, 4 * group + (place >> 3), -1)
    turned = dot_nt(one_hot((32, PADC), 1, wanted), grad_three_ref[...]).astype(BF)
    width = filled_ref.shape[3]
    for a in range(3):
        cols = slice(width * a, width * (a + 1))
        term = dot(turned, gather_rows(filled_ref, a))
        gates = bank_gates(bank_ref, OUT_GATES, 16, range(3 * a, 3 * a + 3)).astype(F32)[:8]
        low, high = kept_pair([term[8 * m : 8 * (m + 1)] for m in range(4)], gates)
        pair = low + pltpu.roll(high, 4, 0)
        wide = jnp.broadcast_to(pair[None], (16, 8, width)).reshape(128, width)
        kernel_row = lax.broadcasted_iota(jnp.int32, (8, width), 1) + width * a
        slot = kernel_row - 9 * ((kernel_row * 7282) >> 16)
        slot = jnp.broadcast_to(slot[None], (16, 8, width)).reshape(128, width)
        mine = (lax.broadcasted_iota(jnp.int32, (128, width), 0) >> 3) == slot
        flat_ref[:, cols] = jnp.where(mine, wide, 0.0).astype(BF)
    gates = [
        bank_ref[FIRST_GATES : FIRST_GATES + 64, :PADC], bank_ref[FIRST_GATES : FIRST_GATES + 64, PADC:],
        bank_ref[FIRST_GATES + 64 : FIRST_GATES + 128, :PADC],
    ]
    term_pairs(filled_zero_ref, grad_ref[...], lambda a: gates[a], flat_zero_ref)
    for half in range(2):
        rows = slice(16 * CHUNK * half, 16 * CHUNK * (half + 1))
        part = part_ref[rows] + dot_nt(pick_out_ref[...], flat_ref[:, 1152 * half : 1152 * (half + 1)])
        buffer_ref[16 * half : 16 * (half + 1), 0:CHUNK] = part.astype(BF).reshape(16, CHUNK, PADC)
    share = dot_nt(pick_first_ref[...], flat_zero_ref[...]).astype(BF)
    for place in range(ROWS):
        kind = place // 8
        buffer_ref[place, CHUNK : CHUNK + SHARE] = share[SHARE * kind : SHARE * (kind + 1)]
    keep.wait()


def last_kernel(
    mine_ref, grad_ref, bank_ref, state_ref, sea_ref,
    estimate_ref, dx_ref, up_ref, down_ref, local_ref,
    pad_ref, dx_all_ref, narrow_ref,
):
    for a in range(3):
        for b in range(3):
            at = FIRST_W + PADC * a + 32 * b
            block = jnp.concatenate([bank_ref[at : at + 32], jnp.zeros((PADC - 32, HID), BF)], 0)
            to = HID * (3 * b + a)
            narrow_ref[to : to + HID, :PADC] = dot_nt(eye(HID, HID), block).astype(BF)
            at = OUT_BACK + PADC * b + FIELDS * a
            block = jnp.concatenate([bank_ref[at : at + FIELDS], jnp.zeros((PADC - FIELDS, HID), BF)], 0)
            to = HID * (3 * a + b)
            narrow_ref[to : to + HID, PADC:] = dot_tn(block, eye(PADC, PADC)).astype(BF)
    comp = lax.axis_index("comp")
    col = lax.axis_index(("xh", "core"))
    width = mine_ref.shape[2]
    pad_ref[...] = jnp.zeros_like(pad_ref)
    fold_row(
        lambda col: pad_lines(grad_ref[CELLS * col : CELLS * (col + 1)], pad_ref),
        narrow_ref, 0, slice(0, PADC), dx_all_ref, down_ref, up_ref, local_ref,
    )
    dx_ref[...] = dx_all_ref[pl.ds(pl.multiple_of(col * CELLS, CELLS), CELLS)]
    total = None
    for a in range(3):
        weights = narrow_ref[width * a : width * (a + 1), PADC:]
        piece = dot(mine_ref[a : a + TS].reshape(CELLS, width), weights)
        total = piece if total is None else total + piece
    weight = jnp.where(comp == 1, sea_ref[...].astype(F32), 1.0)
    estimate_ref[...] = (state_ref[...].astype(F32) + weight * total.T[:FIELDS]).astype(BF)


def sum_kernel(spread_ref, share_ref, sum_ref):
    total = spread_ref[0].astype(F32)
    for place in range(1, ROWS):
        total = total + spread_ref[place].astype(F32)
    sum_ref[...] = total[:CHUNK]
    share = total[CHUNK:].astype(BF)
    for place in range(16):
        share_ref[place] = share


def finish_kernel(
    dx_ref, next_ref, prev_ref, local_ref, bank_ref, cot_ref, sum_ref,
    own_ref, send_ref, central_ref, closing_ref,
):
    give = bank_ref[GIVE_OWN : GIVE_OWN + CELLS]
    strips = jnp.concatenate([next_ref[...], prev_ref[...], local_ref[...]], 0)
    total = (dx_ref[...] + dot(give, strips)).T
    own_ref[...] = cot_ref[...].astype(F32) + total[:FIELDS]
    send_ref[...] = total[FIELDS : FIELDS + COUPLED]
    sums = sum_ref[...]
    repeat = repeat_four(HID // 4, HID)
    wide = dot(bank_ref[OWN_GATES : OWN_GATES + 32, :64], repeat)[:CHUNK]
    low, high = keep_of(wide, lax.broadcasted_iota(jnp.int32, (CHUNK, HID), 1) & 3)
    lows, highs = dot_exact_right(sums[:, :64], repeat), dot_exact_right(sums[:, 64:], repeat)
    central = jnp.where(low, lows, jnp.where(high, highs, 0.0))
    for line in range(18):
        central_ref[:, HID * line : HID * (line + 1)] = central[line : line + 1]
    place = lax.broadcasted_iota(jnp.int32, (CHUNK, CHUNK), 0)
    late = (place >= 9).astype(jnp.int32)
    spread = dot_exact(one_hot((CHUNK, CHUNK), 1, 18 + late), sums)
    place = lax.broadcasted_iota(jnp.int32, (CHUNK, PADC), 0)
    slot = place - 9 * (place >= 9).astype(jnp.int32)
    lane = lax.broadcasted_iota(jnp.int32, (CHUNK, PADC), 1)
    spread = jnp.where((lane >> 3) == slot, spread, 0.0)
    flat = 3 * PADC
    from_lane = lax.broadcasted_iota(jnp.int32, (PADC, flat), 0) & 7
    group = (lax.broadcasted_iota(jnp.int32, (PADC, flat), 1) & 15) >> 2
    lows = dot_exact_right(spread, (from_lane == group).astype(F32).astype(BF))
    highs = dot_exact_right(spread, (from_lane == group + 4).astype(F32).astype(BF))
    group = (lax.broadcasted_iota(jnp.int32, (PADC, flat), 1) & 15) >> 2
    wide = dot(bank_ref[OWN_GATES : OWN_GATES + 32, PADC:], one_hot((PADC, flat), 0, group))[:CHUNK]
    lane = lax.broadcasted_iota(jnp.int32, (CHUNK, flat), 1)
    low, high = keep_of(wide, lane & 3)
    closing = jnp.where(low, lows, jnp.where(high, highs, 0.0))
    here = lax.broadcasted_iota(jnp.int32, (CHUNK, flat), 0) == (lane >> 4)
    closing_ref[...] = jnp.sum(jnp.where(here, closing, 0.0), 0, keepdims=True)[:, : 18 * FIELDS]


def opening_kernel(share_ref, bank_ref, out_ref):
    count = 9 * (FIELDS + COUPLED)
    wanted = lax.broadcasted_iota(jnp.int32, (count, 16 * SHARE), 0)
    block = (wanted * 4682) >> 16
    pick = one_hot((count, 16 * SHARE), 1, SHARE * block + wanted - 14 * block)
    pairs = dot(pick, share_ref[...]).astype(BF)
    repeat = repeat_four(HID // 4, HID)
    low, high = keep_of(bank_ref[FIRST_WIDE : FIRST_WIDE + count].astype(F32), lax.broadcasted_iota(jnp.int32, (count, HID), 1) & 3)
    out_ref[...] = jnp.where(low, dot(pairs[:, :64], repeat), jnp.where(high, dot(pairs[:, 64:], repeat), 0.0))


VMEM = pl.BlockSpec(memory_space=pltpu.VMEM)
SMEM = pl.BlockSpec(memory_space=pltpu.SMEM)
HBM = pl.BlockSpec(memory_space=pltpu.HBM)


def call(body, out, args, scratch=(), scalars=(), far=(), far_out=(), flops=0, limit=10):
    args = [pltpu.with_memory_space_constraint(arg, pltpu.HBM) if place in far else arg for place, arg in enumerate(args)]
    specs = [SMEM if place in scalars else HBM if place in far else VMEM for place in range(len(args))]
    size = sum(int(np.prod(item.shape)) * item.dtype.itemsize for item in list(args) + list(out))
    return pl.pallas_call(
        body,
        out_shape=[jax.ShapeDtypeStruct(item.shape, item.dtype) for item in out],
        in_specs=specs,
        out_specs=[HBM if place in far_out else VMEM for place in range(len(out))],
        scratch_shapes=list(scratch),
        compiler_params=pltpu.CompilerParams(vmem_limit_bytes=limit * 1024 * 1024),
        cost_estimate=pl.CostEstimate(flops=flops, bytes_accessed=size, transcendentals=0),
    )(*args)


def sds(shape, kind):
    return jax.ShapeDtypeStruct(shape, kind)


def row_shift(value, step):
    pairs = [(face, (face + ROW * step) % TILES) for face in range(TILES)]
    return lax.ppermute(value, FACE, pairs)


def body(
    state, cotangent, land_sea, turn_table, first_kernel, mid_kernel, out_kernel, first_gates, mid_gates, out_gates
):
    sea = land_sea.reshape(1, CELLS)

    packed = call(pack_kernel, [sds((8, 2 * FIELDS, CELLS), BF)], [state[0], cotangent[0], sea],
        scratch=[
            pltpu.VMEM((FIELDS, CELLS), BF), pltpu.VMEM((FIELDS, CELLS), BF), pltpu.VMEM((1, CELLS), jnp.int32),
            pltpu.SemaphoreType.DMA((3,)),
        ],
        far=(0, 1, 2),
    )[0]
    line = lax.all_to_all(packed, LINE_AXES, 0, 0).reshape(2, ROW, 2 * FIELDS, CELLS)

    turns, out_turned = turn_table.T, out_gates[0].T
    first_turned, mid_turned = first_gates[0].T, mid_gates[0].T
    early, middle = call(
        prepare_early_kernel, [sds((BANK_ONE, HID), BF), sds((BANK_MID, HID), BF)],
        [turns, first_turned, out_turned, first_kernel[0], out_kernel[0].T, mid_turned, mid_kernel[0]],
        scratch=[
            pltpu.SMEM((4, TILES), jnp.int32), pltpu.VMEM((64, 9 * DEPTH), jnp.int32),
            pltpu.VMEM((4, 9 * HID), jnp.int32), pltpu.VMEM((9 * DEPTH, HID), BF),
            pltpu.VMEM((FIELDS, 9 * HID), BF), pltpu.VMEM((64, 9 * HID), jnp.int32),
            pltpu.VMEM((9 * HID, HID), BF), pltpu.SemaphoreType.DMA((7,)),
        ],
        far=(0, 1, 2, 3, 4, 5, 6), flops=5 * 10**9,
    )

    field, grad_cells, strips_zero = call(
        start_kernel,
        [sds((LINE, PADC), BF), sds((LINE, PADC), BF), sds((256, PADC), BF)], [line, early],
    )
    prev_zero = row_shift(strips_zero[UP], 1)
    next_zero = row_shift(strips_zero[DOWN], -1)
    two = call(
        prepare_late_kernel, [sds((BANK_TWO, HID), BF)], [middle, first_turned, out_turned],
        scratch=[
            pltpu.VMEM((64, 9 * DEPTH), jnp.int32), pltpu.VMEM((4, 9 * HID), jnp.int32),
            pltpu.SemaphoreType.DMA((2,)),
        ],
        far=(1, 2), flops=10**9,
    )[0]
    exchange = [sds((192, HID), BF), sds((160, HID), BF), sds((160, HID), BF), sds((LINE, HID), F32)]
    filled_zero, act_one, hid_one, local_one, up_one, down_one, inner_two = call(
        layer_one_kernel,
        [sds((ROW, TS + 2, TS, PADC), BF), sds((LINE, HID), F32), sds((LINE, HID), BF)] + exchange,
        [field, strips_zero, prev_zero, next_zero, grad_cells, early],
    )
    prev_one = row_shift(up_one, 1)
    next_one = row_shift(down_one, -1)

    three, slope_one, pick_mid, pick_out, pick_first = call(
        prepare_last_kernel, [sds((BANK_THREE, HID), BF), sds((LINE, HID), F32), sds((16 * CHUNK, 1152), BF), sds((16 * CHUNK, 1152), BF),
         sds((4 * SHARE, 3 * PADC), BF)],
        [early, middle, first_turned, out_turned, act_one], flops=10**9,
    )

    filled_one, grad_two, hid_two, local_two, up_two, down_two, inner_one = call(
        layer_two_kernel,
        [sds((ROW, TS + 2, TS, 3 * HID), BF), sds((LINE, HID), BF), sds((LINE, HID), BF)] + exchange,
        [hid_one, local_one, prev_one, next_one, inner_two, early, middle, two],
        scratch=[pltpu.VMEM((TS + 2, TS, 3 * HID), BF)],
    )
    prev_two = row_shift(up_two, 1)
    next_two = row_shift(down_two, -1)

    part = call(
        mid_term_kernel,
        [sds((32 * CHUNK, PADC), F32)],
        [filled_one, grad_two, middle, pick_mid],
        scratch=[pltpu.VMEM((PADC, 9 * HID), BF)], flops=2 * 10**9,
    )[0]

    buffer, mine_two, grad_one = call(
        terms_kernel,
        [sds((ROWS, CHUNK + SHARE, PADC), BF), sds((TS + 2, TS, 3 * HID), BF), sds((LINE, HID), BF)],
        [hid_two, local_two, prev_two, next_two, inner_one, slope_one, filled_zero, grad_cells, early, two,
         part, pick_out, pick_first],
        scratch=[
            pltpu.VMEM((ROW, TS + 2, TS, 3 * HID), BF), pltpu.VMEM((PADC, 9 * HID), BF),
            pltpu.VMEM((PADC, 3 * PADC), BF), pltpu.SemaphoreType.DMA,
        ],
        far_out=(1,),
    )
    spread = lax.all_to_all(buffer, ROW_AXES, 0, 0)

    estimate, dx_own, up_three, down_three, local_three = call(
        last_kernel,
        [sds((FIELDS, CELLS), BF), sds((CELLS, PADC), F32), sds((80, PADC), BF), sds((80, PADC), BF),
         sds((96, PADC), BF)],
        [mine_two, grad_one, early, state[0], sea],
        scratch=[
            pltpu.VMEM((TS + 2, TS, 3 * HID), BF), pltpu.VMEM((LINE, PADC), F32),
            pltpu.VMEM((9 * HID, HID), BF),
        ],
        flops=2 * 10**9,
    )
    prev_three = row_shift(up_three, 1)
    next_three = row_shift(down_three, -1)

    shared, summed = call(sum_kernel, [sds((16, SHARE, PADC), BF), sds((CHUNK, PADC), F32)], [spread])
    opened = lax.all_to_all(shared, ("y", "xh", "core"), 0, 0).reshape(16 * SHARE, PADC)

    own, send, central, closing = call(
        finish_kernel,
        [sds((FIELDS, CELLS), F32), sds((COUPLED, CELLS), F32), sds((1, 18 * HID), F32), sds((1, 18 * FIELDS), F32)],
        [dx_own, next_three, prev_three, local_three, three, cotangent[0], summed],
    )
    returned = lax.ppermute(send, "comp", [(0, 1), (1, 0)])
    adjoint = own + jnp.pad(returned, ((0, FIELDS - COUPLED), (0, 0)))
    opening = call(opening_kernel, [sds((9 * DEPTH, HID), F32)], [opened, three])[0]
    return estimate[None], adjoint[None], opening[None], central, closing


def solution(mesh):
    fine = Mesh(mesh.devices.reshape(2, 4, 8, 2, 2), ("comp",) + FACE)
    whole = P("comp", None, None)
    in_specs = (P("comp", None, FACE), P("comp", None, FACE), P(FACE), P()) + (whole,) * 6
    out_specs = (P("comp", None, FACE), P("comp", None, FACE), whole, P("comp", FACE), P("comp", FACE))

    return jax.shard_map(body, mesh=fine, in_specs=in_specs, out_specs=out_specs, check_vma=False)
```

```python
import jax
import jax.numpy as jnp
import numpy as np
from jax import lax
from jax.experimental import pallas as pl
from jax.experimental.pallas import tpu as pltpu
from jax.sharding import Mesh, PartitionSpec as P


FIELDS = 16
COUPLED = 8
TS = 16
CELLS = TS * TS
ROW = 4
ROWS = 32
TILES = ROW * ROWS
LINE = ROW * CELLS
HID = 256
PADC = 128
CHUNK = 24
SHARE = 16
DEPTH = FIELDS + COUPLED

GIVE = 0
TAKE = GIVE + LINE
FIRST_W = TAKE + LINE
OUT_BACK = FIRST_W + 3 * PADC
BANK_ONE = OUT_BACK + 3 * PADC
MID_BACK = 0
MID_GATES = MID_BACK + 9 * HID
BANK_MID = MID_GATES + 9 * 64
MID_W = 0
FIRST_GATES = MID_W + 9 * HID
OUT_GATES = FIRST_GATES + 2 * 64
BANK_TWO = OUT_GATES + 9 * 16
FIRST_WIDE = 0
GIVE_OWN = FIRST_WIDE + 224
OWN_GATES = GIVE_OWN + CELLS
BANK_THREE = OWN_GATES + 32
BF = jnp.bfloat16
F32 = jnp.float32

FACE = ("y", "z", "xh", "core")
ROW_AXES = ("y", "z")
LINE_AXES = ("comp", "xh", "core")

EDGE_MAP = (
    ((0, False), (2, True), (1, True), (3, False)),
    ((1, False), (3, True), (0, True), (2, False)),
    ((2, False), (1, False), (3, True), (0, True)),
    ((3, False), (0, False), (2, True), (1, True)),
)

STRIPS = (
    [(col, 2, 8 + col) for col in range(4)]
    + [(3, 0, 8)]
    + [(col, 3, col) for col in range(4)]
    + [(0, 1, 3)]
    + [(col - 1, 0, 4 + col) for col in (1, 2, 3)]
    + [(col + 1, 1, 4 + col) for col in (0, 1, 2)]
)


def edge_line(slot, flip):
    first, step = ((TS - 1, TS), (0, TS), ((TS - 1) * TS, 1), (0, 1))[slot]
    if flip:
        first, step = first + (TS - 1) * step, -step
    return first, step


def dot(left, right):
    return jnp.dot(left, right, preferred_element_type=F32)


def dot_nt(left, right):
    return lax.dot_general(left, right, (((1,), (1,)), ((), ())), preferred_element_type=F32)


def dot_tn(left, right):
    return lax.dot_general(left, right, (((0,), (0,)), ((), ())), preferred_element_type=F32)


def dot_exact(left, right):
    high = right.astype(BF)
    rest = right - high.astype(F32)
    mid = rest.astype(BF)
    low = (rest - mid.astype(F32)).astype(BF)
    return dot(left, high) + (dot(left, mid) + dot(left, low))


def dot_exact_right(left, right):
    high = left.astype(BF)
    rest = left - high.astype(F32)
    mid = rest.astype(BF)
    low = (rest - mid.astype(F32)).astype(BF)
    return dot(high, right) + (dot(mid, right) + dot(low, right))


def fetch(sources, buffers, sems):
    copies = [
        pltpu.make_async_copy(source, buffer, sems.at[place])
        for place, (source, buffer) in enumerate(zip(sources, buffers))
    ]
    for copy in copies:
        copy.start()
    return copies


def one_hot(shape, axis, index):
    return (lax.broadcasted_iota(jnp.int32, shape, axis) == index).astype(F32).astype(BF)


def shift_cells(value, step, axis):
    along = lax.broadcasted_iota(jnp.int32, value.shape, axis)
    moved = pltpu.roll(value, step % TS, axis)
    edge = 0 if step == 1 else TS - 1
    return jnp.where(along == edge, 0.0, moved)


def shift_lines(lines, step, strip):
    along = lax.broadcasted_iota(jnp.int32, lines.shape, 1)
    moved = pltpu.roll(lines, step % TS, 1)
    edge = 0 if step == 1 else TS - 1
    return jnp.where(along == edge, jnp.broadcast_to(strip.astype(F32)[:, None, :], lines.shape), moved)


def fill(out_ref, tiles, local, from_prev, from_next):
    depth = tiles.shape[1]
    for col in range(ROW):
        south = from_prev[TS * col : TS * (col + 1)]
        north = from_next[TS * col : TS * (col + 1)]
        west = from_prev[4 * TS : 5 * TS] if col == 0 else local[TS * (col - 1) : TS * col]
        east = from_next[4 * TS : 5 * TS] if col == 3 else local[TS * (3 + col) : TS * (4 + col)]
        own = tiles[CELLS * col : CELLS * (col + 1)]
        wide = own.astype(F32).reshape(TS, TS, depth)
        left = shift_lines(wide, 1, west)
        right = shift_lines(wide, -1, east)
        out_ref[col, 1 : TS + 1, :, 0:depth] = left.astype(BF)
        out_ref[col, 1 : TS + 1, :, depth : 2 * depth] = own.reshape(TS, TS, depth)
        out_ref[col, 1 : TS + 1, :, 2 * depth : 3 * depth] = right.astype(BF)
        for line, strip in ((0, south), (TS + 1, north)):
            wide = strip.astype(F32)
            out_ref[col, line, :, 0:depth] = shift_cells(wide, 1, 0).astype(BF)
            out_ref[col, line, :, depth : 2 * depth] = strip
            out_ref[col, line, :, 2 * depth : 3 * depth] = shift_cells(wide, -1, 0).astype(BF)


def fill_packed(out_ref, tiles, local, from_prev, from_next):
    def choose(left, own, right):
        lane = lax.broadcasted_iota(jnp.int32, own.shape, own.ndim - 1)
        return jnp.where(lane < 32, left, jnp.where(lane < 64, own, right)).astype(BF)

    for col in range(ROW):
        south = from_prev[TS * col : TS * (col + 1)]
        north = from_next[TS * col : TS * (col + 1)]
        west = from_prev[4 * TS : 5 * TS] if col == 0 else local[TS * (col - 1) : TS * col]
        east = from_next[4 * TS : 5 * TS] if col == 3 else local[TS * (3 + col) : TS * (4 + col)]
        wide = tiles[CELLS * col : CELLS * (col + 1)].astype(F32).reshape(TS, TS, PADC)
        left = shift_lines(wide, 1, west)
        right = shift_lines(wide, -1, east)
        out_ref[col, 1 : TS + 1] = choose(left, wide, right)
        for line, strip in ((0, south), (TS + 1, north)):
            wide = strip.astype(F32)
            out_ref[col, line] = choose(shift_cells(wide, 1, 0), wide, shift_cells(wide, -1, 0))


def take_strips(bank_ref, cells_ref):
    total = None
    for col in range(ROW):
        block = slice(TAKE + CELLS * col, TAKE + CELLS * (col + 1))
        piece = dot(bank_ref[block], cells_ref[CELLS * col : CELLS * (col + 1)])
        total = piece if total is None else total + piece
    return total.astype(BF)


def conv_tile(filled_ref, bank_ref, base, col, lanes=slice(None)):
    width = filled_ref.shape[3]
    total = None
    for a in range(3):
        weights = bank_ref[base + width * a : base + width * (a + 1), lanes]
        piece = dot(filled_ref[col, a : a + TS].reshape(CELLS, width), weights)
        total = piece if total is None else total + piece
    return total


def pad_lines(grad, pad_ref):
    deep = grad.shape[1]
    lines = grad.reshape(TS, TS, deep)
    for a in range(3):
        pad_ref[a : a + TS, :, deep * a : deep * (a + 1)] = lines
    return pad_ref[...].reshape((TS + 2) * TS, 3 * deep)


def pad_lines_packed(grad):
    lines = grad.astype(F32).reshape(TS, TS, PADC)
    blank = jnp.zeros((1, TS, PADC), F32)
    lane = lax.broadcasted_iota(jnp.int32, (TS + 2, TS, PADC), 2)
    one, two, three = (
        jnp.concatenate([blank] * a + [lines] + [blank] * (2 - a), 0) for a in range(3)
    )
    padded = jnp.where(lane < 16, one, jnp.where(lane < 32, two, three))
    return padded.reshape((TS + 2) * TS, PADC).astype(BF)


def fold_tile(padded, bank_ref, base, lanes):
    deep = padded.shape[1]
    left, mid, right = (
        dot(padded, bank_ref[base + deep * b : base + deep * (b + 1), lanes]) for b in range(3)
    )
    depth = mid.shape[1]
    left, mid, right = (part.reshape(TS + 2, TS, depth) for part in (left, mid, right))
    merged = mid + shift_cells(left, -1, 1) + shift_cells(right, 1, 1)
    inner = merged[1 : TS + 1].reshape(CELLS, depth)
    south = merged[0].astype(BF)
    north = merged[TS + 1].astype(BF)
    west = left[1 : TS + 1, 0, :].astype(BF)
    east = right[1 : TS + 1, TS - 1, :].astype(BF)
    return inner, south, north, west, east


def fold_row(padded_of, bank_ref, base, lanes, inner_ref, prev_ref, next_ref, local_ref):
    for col in range(ROW):
        inner, south, north, west, east = fold_tile(padded_of(col), bank_ref, base, lanes)
        inner_ref[CELLS * col : CELLS * (col + 1)] = inner
        prev_ref[TS * col : TS * (col + 1)] = south
        next_ref[TS * col : TS * (col + 1)] = north
        if col == 0:
            prev_ref[4 * TS : 5 * TS] = west
        else:
            local_ref[TS * (col - 1) : TS * col] = west
        if col == 3:
            next_ref[4 * TS : 5 * TS] = east
        else:
            local_ref[TS * (3 + col) : TS * (4 + col)] = east


def sigmoid(values):
    return 1.0 / (1.0 + jnp.exp(-values))


def slope(values):
    sig = sigmoid(values)
    return sig * (1.0 + values * (1.0 - sig))


UP = slice(0, 80)
DOWN = slice(80, 160)
LOCAL = slice(160, 256)


def keep_of(wide, lane):
    low = jnp.where(wide >= 4.5, 2, jnp.where(wide >= 2.5, 1, 0))
    high = jnp.where(wide < 0.5, 1, jnp.where((wide < 1.5) | ((wide > 2.5) & (wide < 3.5)), 2, 3))
    return lane == low, lane == high


def kept_pair(planes, gates):
    one, two, three, four = planes
    low = jnp.where(gates >= 4.5, three, jnp.where(gates >= 2.5, two, one))
    high = jnp.where(gates < 0.5, two, jnp.where((gates < 1.5) | ((gates > 2.5) & (gates < 3.5)), three, four))
    return low, high


def eye(rows, cols):
    return one_hot((rows, cols), 1, lax.broadcasted_iota(jnp.int32, (rows, cols), 0))


def repeat_four(groups, width):
    rows = lax.broadcasted_iota(jnp.int32, (groups, width), 0)
    cols = lax.broadcasted_iota(jnp.int32, (groups, width), 1)
    return ((cols >> 2) == rows).astype(F32).astype(BF)


def plane_order():
    rows = lax.broadcasted_iota(jnp.int32, (HID, HID), 0)
    return one_hot((HID, HID), 1, 4 * (rows & 63) + (rows >> 6))


def pack_kernel(state_hbm, cot_hbm, sea_hbm, out_ref, state_ref, cot_ref, sea_ref, sems):
    copies = fetch((state_hbm, cot_hbm, sea_hbm), (state_ref, cot_ref, sea_ref), sems)
    for copy in copies:
        copy.wait()
    comp = lax.axis_index("comp")
    weight = jnp.where(comp == 1, sea_ref[...].astype(F32), 1.0)
    grad = (weight * cot_ref[...].astype(F32)).astype(BF)
    for place in range(8):
        out_ref[place, 0:FIELDS] = state_ref[...]
        out_ref[place, FIELDS : 2 * FIELDS] = grad


def kept_rows(gates, kernel):
    outputs = kernel.shape[0]
    rows = lax.broadcasted_iota(jnp.int32, (outputs, outputs // 4), 0) >> 2
    repeat = one_hot((outputs, outputs // 4), 1, rows)
    low = jnp.where(gates >= 4.5, 2.0, jnp.where(gates >= 2.5, 1.0, 0.0)).astype(BF)
    high = jnp.where(gates < 0.5, 1.0, jnp.where((gates < 1.5) | ((gates > 2.5) & (gates < 3.5)), 2.0, 3.0)).astype(BF)
    lane = (lax.broadcasted_iota(jnp.int32, kernel.shape, 0) & 3).astype(F32)
    return jnp.where((dot(repeat, low) == lane) | (dot(repeat, high) == lane), kernel, 0.0)


def prepare_early_kernel(
    turn_hbm, first_gates_hbm, out_gates_hbm, first_hbm, out_hbm, mid_gates_hbm, mid_hbm, bank_ref, middle_ref,
    turn_ref, first_gates_ref, out_gates_ref, first_ref, out_ref, mid_gates_ref, mid_ref, sems,
):
    copies = fetch(
        (turn_hbm, first_gates_hbm, out_gates_hbm, first_hbm, out_hbm, mid_gates_hbm, mid_hbm),
        (turn_ref, first_gates_ref, out_gates_ref, first_ref, out_ref, mid_gates_ref, mid_ref), sems,
    )
    copies[0].wait()
    row = lax.axis_index(ROW_AXES)
    strip_of = lax.broadcasted_iota(jnp.int32, (8, 256), 1) >> 4
    along = lax.broadcasted_iota(jnp.int32, (8, 256), 1) & 15
    cells = jnp.zeros((8, 256), jnp.int32)
    for number, (source, side, reader) in enumerate(STRIPS):
        turn = turn_ref[side, lax.rem(ROW * row + reader - ROW + TILES, TILES)]
        first, step = edge_line(*EDGE_MAP[side][3])
        for turns in range(3):
            one, two = edge_line(*EDGE_MAP[side][turns])
            first, step = jnp.where(turn == turns, one, first), jnp.where(turn == turns, two, step)
        first = first + source * CELLS
        cells = jnp.where(strip_of == number, first + step * along, cells)
        place = lax.broadcasted_iota(jnp.int32, (TS, LINE), 1)
        wanted = first + step * lax.broadcasted_iota(jnp.int32, (TS, LINE), 0)
        hit = (place == wanted).astype(F32).astype(BF)
        for col in range(ROW):
            at = TAKE + CELLS * col + TS * number
            bank_ref[at : at + TS] = hit[:, CELLS * col : CELLS * (col + 1)]
    bank_ref[GIVE : GIVE + LINE] = one_hot((LINE, 256), 0, cells[0:1])
    for copy in copies[1:]:
        copy.wait()
    count = 9 * DEPTH
    wide = dot_tn(first_gates_ref[...].astype(F32).astype(BF), repeat_four(HID // 4, HID))
    low, high = keep_of(wide, lax.broadcasted_iota(jnp.int32, (count, HID), 1) & 3)
    kernel = jnp.where(low | high, first_ref[...].astype(F32), 0.0)
    blank = jnp.zeros((32 - DEPTH, HID), F32)
    kernel_out = kept_rows(out_gates_ref[...].astype(F32), out_ref[...].astype(F32)).astype(BF)
    for a in range(3):
        pieces = []
        for b in range(3):
            tap = 3 * a + b
            pieces += [kernel[DEPTH * tap : DEPTH * (tap + 1)], blank]
            at = OUT_BACK + PADC * b + FIELDS * a
            bank_ref[at : at + FIELDS] = kernel_out[:, HID * tap : HID * (tap + 1)]
        pieces.append(jnp.zeros((32, HID), F32))
        bank_ref[FIRST_W + PADC * a : FIRST_W + PADC * (a + 1)] = jnp.concatenate(pieces, 0).astype(BF)
        bank_ref[OUT_BACK + PADC * a + 48 : OUT_BACK + PADC * (a + 1)] = jnp.zeros((PADC - 48, HID), BF)
    for tap in range(9):
        cols = slice(HID * tap, HID * (tap + 1))
        gates = mid_gates_ref[:, cols].astype(F32)
        middle_ref[MID_GATES + 64 * tap : MID_GATES + 64 * (tap + 1)] = gates.astype(BF)
        at = MID_BACK + HID * (3 * (tap % 3) + tap // 3)
        middle_ref[at : at + HID] = kept_rows(gates, dot_nt(eye(HID, HID), mid_ref[cols])).astype(BF)


def prepare_late_kernel(middle_ref, first_gates_hbm, out_gates_hbm, two_ref, first_gates_ref, out_gates_ref, sems):
    copies = fetch((first_gates_hbm, out_gates_hbm), (first_gates_ref, out_gates_ref), sems)
    for a in range(3):
        for b in range(3):
            at = MID_BACK + HID * (3 * b + a)
            to = MID_W + HID * (3 * a + b)
            two_ref[to : to + HID] = dot_tn(middle_ref[at : at + HID], eye(HID, HID)).astype(BF)
    for copy in copies:
        copy.wait()
    count = 9 * DEPTH
    place = lax.broadcasted_iota(jnp.int32, (count, 3 * PADC), 0)
    tap = (place * 2731) >> 16
    third = (tap * 11) >> 5
    target = PADC * third + 32 * (tap - 3 * third) + place - DEPTH * tap
    gates = first_gates_ref[...].astype(F32).astype(BF)
    spread = dot(gates, one_hot((count, 3 * PADC), 1, target)).astype(BF)
    two_ref[FIRST_GATES : FIRST_GATES + 64] = spread[:, :HID]
    two_ref[FIRST_GATES + 64 : FIRST_GATES + 128, :PADC] = spread[:, HID:]
    gates = dot(eye(16, 4), out_gates_ref[...].astype(F32).astype(BF)).astype(BF)
    for tap in range(9):
        two_ref[OUT_GATES + 16 * tap : OUT_GATES + 16 * (tap + 1)] = gates[:, HID * tap : HID * (tap + 1)]


def prepare_last_kernel(early_ref, middle_ref, first_gates_ref, out_gates_ref, act_ref,
    three_ref, slope_ref, pick_ref, pick_out_ref, pick_first_ref):
    slope_ref[...] = slope(act_ref[...])
    col = lax.axis_index(("xh", "core"))
    tile = lax.axis_index(FACE)
    shape = (16 * CHUNK, 1152)
    place = lax.broadcasted_iota(jnp.int32, shape, 0)
    block = (place * 2731) >> 16
    inside = place - CHUNK * block
    ahead = lax.broadcasted_iota(jnp.int32, shape, 1) - (72 * block + 18 * col)
    pick_ref[...] = ((ahead == inside) & (inside < 18)).astype(F32).astype(BF)
    late = ahead - 9 * (inside - 18)
    pick_out_ref[...] = ((late >= 0) & (late < 9) & (inside >= 18) & (inside < 20)).astype(F32).astype(BF)
    shape = (4 * SHARE, 3 * PADC)
    place = lax.broadcasted_iota(jnp.int32, shape, 0)
    inside = place & 15
    wanted = 14 * (4 * (place >> 4) + col) + inside
    tap = (wanted * 2731) >> 16
    third = (tap * 11) >> 5
    target = PADC * third + 32 * (tap - 3 * third) + wanted - DEPTH * tap
    real = (inside < 14) & (wanted < 9 * DEPTH)
    pick_first_ref[...] = ((lax.broadcasted_iota(jnp.int32, shape, 1) == target) & real).astype(F32).astype(BF)
    three_ref[GIVE_OWN : GIVE_OWN + CELLS] = early_ref[pl.ds(pl.multiple_of(GIVE + CELLS * col, CELLS), CELLS)]
    count = 9 * DEPTH
    gates = first_gates_ref[...].astype(F32).astype(BF)
    three_ref[FIRST_WIDE : FIRST_WIDE + count] = dot_tn(gates, repeat_four(HID // 4, HID)).astype(BF)
    place = lax.broadcasted_iota(jnp.int32, (32, 9 * HID), 0)
    mine = one_hot((32, 9 * HID), 1, jnp.where(place < 18, 18 * tile + place, -1))
    gates = bank_gates(middle_ref, MID_GATES, 64, range(9))
    three_ref[OWN_GATES : OWN_GATES + 32, :64] = dot_nt(mine, gates).astype(BF)
    gates = dot(eye(PADC, 4), out_gates_ref[...].astype(F32).astype(BF)).astype(BF)
    three_ref[OWN_GATES : OWN_GATES + 32, PADC:] = dot_nt(mine, gates).astype(BF)


def bank_gates(bank_ref, base, rows, blocks):
    step = max(rows, 16)
    return jnp.concatenate(
        [bank_ref[base + step * b : base + step * (b + 1)][:rows] for b in blocks], 1
    )


def start_kernel(line_ref, bank_ref, field_ref, grad_ref, strips_ref):
    comp = lax.axis_index("comp")
    for col in range(ROW):
        own = line_ref[comp, col].astype(F32)
        other = line_ref[1 - comp, col][:FIELDS].astype(F32)[:COUPLED]
        blank = jnp.zeros((32 - DEPTH, CELLS), F32)
        field = jnp.concatenate([own[:FIELDS], other, blank] * 3 + [jnp.zeros((32, CELLS), F32)], 0)
        field_ref[CELLS * col : CELLS * (col + 1)] = field.T.astype(BF)
        grad = jnp.concatenate([own[FIELDS:]] * 3 + [jnp.zeros((PADC - 3 * FIELDS, CELLS), F32)], 0)
        grad_ref[CELLS * col : CELLS * (col + 1)] = grad.T.astype(BF)
    strips_ref[...] = take_strips(bank_ref, field_ref)


def send_strips(strips, up_ref, down_ref, local_ref):
    up_ref[0:80] = strips[UP]
    down_ref[0:80] = strips[DOWN]
    local_ref[0:96] = strips[LOCAL]


def back_strips(prev_ref, next_ref, local_ref):
    return jnp.concatenate([next_ref[80:160], prev_ref[80:160], local_ref[96:192]], 0)


def layer_one_kernel(
    field_ref, strips_ref, prev_ref, next_ref, grad_ref, bank_ref,
    filled_ref, act_ref, hid_ref, local_ref, up_ref, down_ref, inner_ref,
):
    fill_packed(filled_ref, field_ref[...], strips_ref[LOCAL], prev_ref[...], next_ref[...])
    for col in range(ROW):
        act = conv_tile(filled_ref, bank_ref, FIRST_W, col)
        act_ref[CELLS * col : CELLS * (col + 1)] = act
        hid_ref[CELLS * col : CELLS * (col + 1)] = (act * sigmoid(act)).astype(BF)
    send_strips(take_strips(bank_ref, hid_ref), up_ref, down_ref, local_ref)
    fold_row(
        lambda col: pad_lines_packed(grad_ref[CELLS * col : CELLS * (col + 1)]),
        bank_ref, OUT_BACK, slice(None), inner_ref, down_ref.at[80:160], up_ref.at[80:160], local_ref.at[96:192],
    )


def layer_two_kernel(
    hid_ref, local_in_ref, prev_ref, next_ref, inner_two_ref, early_ref, middle_ref, bank_ref,
    filled_ref, grad_ref, hid_two_ref, local_ref, up_ref, down_ref, inner_ref,
    pad_ref,
):
    fill(filled_ref, hid_ref[...], local_in_ref[0:96], prev_ref[0:80], next_ref[0:80])
    strips = back_strips(prev_ref, next_ref, local_in_ref)
    for col in range(ROW):
        rows = slice(CELLS * col, CELLS * (col + 1))
        grad_hid = inner_two_ref[rows] + dot(early_ref[rows], strips)
        act = conv_tile(filled_ref, bank_ref, MID_W, col)
        sig = sigmoid(act)
        hid_two_ref[rows] = (act * sig).astype(BF)
        grad_ref[rows] = (grad_hid * (sig * (1.0 + act * (1.0 - sig)))).astype(BF)
    send_strips(take_strips(early_ref, hid_two_ref), up_ref, down_ref, local_ref)
    pad_ref[...] = jnp.zeros_like(pad_ref)
    fold_row(
        lambda col: pad_lines(grad_ref[CELLS * col : CELLS * (col + 1)], pad_ref),
        middle_ref, MID_BACK, slice(None), inner_ref, down_ref.at[80:160], up_ref.at[80:160], local_ref.at[96:192],
    )


def gather_rows(filled_ref, a):
    return jnp.concatenate(
        [filled_ref[col, a : a + TS].reshape(CELLS, filled_ref.shape[3]) for col in range(ROW)], 0
    )


def term_by_tile(turned, filled_ref, a):
    total = None
    for col in range(ROW):
        tile = filled_ref[col, a : a + TS].reshape(CELLS, filled_ref.shape[3])
        piece = dot(turned[:, CELLS * col : CELLS * (col + 1)], tile)
        total = piece if total is None else total + piece
    return total


def term_pairs(filled_ref, grad, gates_of, flat_ref):
    turned = dot_nt(plane_order(), grad).astype(BF)
    width = filled_ref.shape[3]
    for a in range(3):
        cols = slice(width * a, width * (a + 1))
        term = dot(turned, gather_rows(filled_ref, a))
        low, high = kept_pair([term[64 * m : 64 * (m + 1)] for m in range(4)], gates_of(a).astype(F32))
        flat_ref[0:64, cols] = low.astype(BF)
        flat_ref[64:128, cols] = high.astype(BF)


def mid_term_kernel(filled_ref, grad_ref, middle_ref, pick_ref, part_ref, flat_ref):
    term_pairs(
        filled_ref, grad_ref[...], lambda a: bank_gates(middle_ref, MID_GATES, 64, range(3 * a, 3 * a + 3)), flat_ref
    )
    for half in range(2):
        part_ref[16 * CHUNK * half : 16 * CHUNK * (half + 1)] = dot_nt(
            pick_ref[...], flat_ref[:, 1152 * half : 1152 * (half + 1)]
        )


def terms_kernel(
    hid_two_ref, local_ref, prev_ref, next_ref, inner_ref, slope_ref, filled_zero_ref, grad_three_ref, early_ref, bank_ref,
    part_ref, pick_out_ref, pick_first_ref,
    buffer_ref, mine_hbm, grad_ref,
    filled_ref, flat_ref, flat_zero_ref, sem,
):
    fill(filled_ref, hid_two_ref[...], local_ref[0:96], prev_ref[0:80], next_ref[0:80])
    keep = pltpu.make_async_copy(filled_ref.at[lax.axis_index(("xh", "core"))], mine_hbm, sem)
    keep.start()
    strips = back_strips(prev_ref, next_ref, local_ref)
    for col in range(ROW):
        rows = slice(CELLS * col, CELLS * (col + 1))
        grad_hid = inner_ref[rows] + dot(early_ref[rows], strips)
        grad_ref[rows] = (grad_hid * slope_ref[rows]).astype(BF)
    place = lax.broadcasted_iota(jnp.int32, (32, PADC), 0)
    group = place & 7
    wanted = jnp.where(group < 4, 4 * group + (place >> 3), -1)
    turned = dot_nt(one_hot((32, PADC), 1, wanted), grad_three_ref[...]).astype(BF)
    width = filled_ref.shape[3]
    for a in range(3):
        cols = slice(width * a, width * (a + 1))
        term = term_by_tile(turned, filled_ref, a)
        gates = bank_gates(bank_ref, OUT_GATES, 16, range(3 * a, 3 * a + 3)).astype(F32)[:8]
        low, high = kept_pair([term[8 * m : 8 * (m + 1)] for m in range(4)], gates)
        pair = low + pltpu.roll(high, 4, 0)
        wide = jnp.broadcast_to(pair[None], (16, 8, width)).reshape(128, width)
        kernel_row = lax.broadcasted_iota(jnp.int32, (8, width), 1) + width * a
        slot = kernel_row - 9 * ((kernel_row * 7282) >> 16)
        slot = jnp.broadcast_to(slot[None], (16, 8, width)).reshape(128, width)
        mine = (lax.broadcasted_iota(jnp.int32, (128, width), 0) >> 3) == slot
        flat_ref[:, cols] = jnp.where(mine, wide, 0.0).astype(BF)
    gates = [
        bank_ref[FIRST_GATES : FIRST_GATES + 64, :PADC], bank_ref[FIRST_GATES : FIRST_GATES + 64, PADC:],
        bank_ref[FIRST_GATES + 64 : FIRST_GATES + 128, :PADC],
    ]
    term_pairs(filled_zero_ref, grad_ref[...], lambda a: gates[a], flat_zero_ref)
    for half in range(2):
        rows = slice(16 * CHUNK * half, 16 * CHUNK * (half + 1))
        part = part_ref[rows] + dot_nt(pick_out_ref[...], flat_ref[:, 1152 * half : 1152 * (half + 1)])
        buffer_ref[16 * half : 16 * (half + 1), 0:CHUNK] = part.astype(BF).reshape(16, CHUNK, PADC)
    share = dot_nt(pick_first_ref[...], flat_zero_ref[...]).astype(BF)
    for place in range(ROWS):
        kind = place // 8
        buffer_ref[place, CHUNK : CHUNK + SHARE] = share[SHARE * kind : SHARE * (kind + 1)]
    keep.wait()


def last_kernel(
    mine_ref, grad_ref, bank_ref, state_ref, sea_ref,
    estimate_ref, dx_ref, up_ref, down_ref, local_ref,
    pad_ref, dx_all_ref, narrow_ref,
):
    for a in range(3):
        for b in range(3):
            at = FIRST_W + PADC * a + 32 * b
            block = jnp.concatenate([bank_ref[at : at + 32], jnp.zeros((PADC - 32, HID), BF)], 0)
            to = HID * (3 * b + a)
            narrow_ref[to : to + HID, :PADC] = dot_nt(eye(HID, HID), block).astype(BF)
            at = OUT_BACK + PADC * b + FIELDS * a
            block = jnp.concatenate([bank_ref[at : at + FIELDS], jnp.zeros((PADC - FIELDS, HID), BF)], 0)
            to = HID * (3 * a + b)
            narrow_ref[to : to + HID, PADC:] = dot_tn(block, eye(PADC, PADC)).astype(BF)
    comp = lax.axis_index("comp")
    col = lax.axis_index(("xh", "core"))
    width = mine_ref.shape[2]
    pad_ref[...] = jnp.zeros_like(pad_ref)
    fold_row(
        lambda col: pad_lines(grad_ref[CELLS * col : CELLS * (col + 1)], pad_ref),
        narrow_ref, 0, slice(0, PADC), dx_all_ref, down_ref, up_ref, local_ref,
    )
    dx_ref[...] = dx_all_ref[pl.ds(pl.multiple_of(col * CELLS, CELLS), CELLS)]
    total = None
    for a in range(3):
        weights = narrow_ref[width * a : width * (a + 1), PADC:]
        piece = dot(mine_ref[a : a + TS].reshape(CELLS, width), weights)
        total = piece if total is None else total + piece
    weight = jnp.where(comp == 1, sea_ref[...].astype(F32), 1.0)
    estimate_ref[...] = (state_ref[...].astype(F32) + weight * total.T[:FIELDS]).astype(BF)


def sum_kernel(spread_ref, share_ref, sum_ref):
    total = spread_ref[0].astype(F32)
    for place in range(1, ROWS):
        total = total + spread_ref[place].astype(F32)
    sum_ref[...] = total[:CHUNK]
    share = total[CHUNK:].astype(BF)
    for place in range(16):
        share_ref[place] = share


def finish_kernel(
    dx_ref, next_ref, prev_ref, local_ref, bank_ref, cot_ref, sum_ref,
    own_ref, send_ref, central_ref, closing_ref,
):
    give = bank_ref[GIVE_OWN : GIVE_OWN + CELLS]
    strips = jnp.concatenate([next_ref[...], prev_ref[...], local_ref[...]], 0)
    total = (dx_ref[...] + dot(give, strips)).T
    own_ref[...] = cot_ref[...].astype(F32) + total[:FIELDS]
    send_ref[...] = total[FIELDS : FIELDS + COUPLED]
    sums = sum_ref[...]
    repeat = repeat_four(HID // 4, HID)
    wide = dot(bank_ref[OWN_GATES : OWN_GATES + 32, :64], repeat)[:CHUNK]
    low, high = keep_of(wide, lax.broadcasted_iota(jnp.int32, (CHUNK, HID), 1) & 3)
    lows, highs = dot_exact_right(sums[:, :64], repeat), dot_exact_right(sums[:, 64:], repeat)
    central = jnp.where(low, lows, jnp.where(high, highs, 0.0))
    for line in range(18):
        central_ref[:, HID * line : HID * (line + 1)] = central[line : line + 1]
    place = lax.broadcasted_iota(jnp.int32, (CHUNK, CHUNK), 0)
    late = (place >= 9).astype(jnp.int32)
    spread = dot_exact(one_hot((CHUNK, CHUNK), 1, 18 + late), sums)
    place = lax.broadcasted_iota(jnp.int32, (CHUNK, PADC), 0)
    slot = place - 9 * (place >= 9).astype(jnp.int32)
    lane = lax.broadcasted_iota(jnp.int32, (CHUNK, PADC), 1)
    spread = jnp.where((lane >> 3) == slot, spread, 0.0)
    flat = 3 * PADC
    from_lane = lax.broadcasted_iota(jnp.int32, (PADC, flat), 0) & 7
    group = (lax.broadcasted_iota(jnp.int32, (PADC, flat), 1) & 15) >> 2
    lows = dot_exact_right(spread, (from_lane == group).astype(F32).astype(BF))
    highs = dot_exact_right(spread, (from_lane == group + 4).astype(F32).astype(BF))
    group = (lax.broadcasted_iota(jnp.int32, (PADC, flat), 1) & 15) >> 2
    wide = dot(bank_ref[OWN_GATES : OWN_GATES + 32, PADC:], one_hot((PADC, flat), 0, group))[:CHUNK]
    lane = lax.broadcasted_iota(jnp.int32, (CHUNK, flat), 1)
    low, high = keep_of(wide, lane & 3)
    closing = jnp.where(low, lows, jnp.where(high, highs, 0.0))
    here = lax.broadcasted_iota(jnp.int32, (CHUNK, flat), 0) == (lane >> 4)
    closing_ref[...] = jnp.sum(jnp.where(here, closing, 0.0), 0, keepdims=True)[:, : 18 * FIELDS]


def opening_kernel(share_ref, bank_ref, out_ref):
    count = 9 * (FIELDS + COUPLED)
    wanted = lax.broadcasted_iota(jnp.int32, (count, 16 * SHARE), 0)
    block = (wanted * 4682) >> 16
    pick = one_hot((count, 16 * SHARE), 1, SHARE * block + wanted - 14 * block)
    pairs = dot(pick, share_ref[...]).astype(BF)
    repeat = repeat_four(HID // 4, HID)
    low, high = keep_of(bank_ref[FIRST_WIDE : FIRST_WIDE + count].astype(F32), lax.broadcasted_iota(jnp.int32, (count, HID), 1) & 3)
    out_ref[...] = jnp.where(low, dot(pairs[:, :64], repeat), jnp.where(high, dot(pairs[:, 64:], repeat), 0.0))


VMEM = pl.BlockSpec(memory_space=pltpu.VMEM)
SMEM = pl.BlockSpec(memory_space=pltpu.SMEM)
HBM = pl.BlockSpec(memory_space=pltpu.HBM)


def call(body, out, args, scratch=(), scalars=(), far=(), far_out=(), flops=0, limit=10):
    args = [pltpu.with_memory_space_constraint(arg, pltpu.HBM) if place in far else arg for place, arg in enumerate(args)]
    specs = [SMEM if place in scalars else HBM if place in far else VMEM for place in range(len(args))]
    size = sum(int(np.prod(item.shape)) * item.dtype.itemsize for item in list(args) + list(out))
    return pl.pallas_call(
        body,
        out_shape=[jax.ShapeDtypeStruct(item.shape, item.dtype) for item in out],
        in_specs=specs,
        out_specs=[HBM if place in far_out else VMEM for place in range(len(out))],
        scratch_shapes=list(scratch),
        compiler_params=pltpu.CompilerParams(vmem_limit_bytes=limit * 1024 * 1024),
        cost_estimate=pl.CostEstimate(flops=flops, bytes_accessed=size, transcendentals=0),
    )(*args)


def sds(shape, kind):
    return jax.ShapeDtypeStruct(shape, kind)


def row_shift(value, step):
    pairs = [(face, (face + ROW * step) % TILES) for face in range(TILES)]
    return lax.ppermute(value, FACE, pairs)


def body(
    state, cotangent, land_sea, turn_table, first_kernel, mid_kernel, out_kernel, first_gates, mid_gates, out_gates
):
    sea = land_sea.reshape(1, CELLS)

    packed = call(pack_kernel, [sds((8, 2 * FIELDS, CELLS), BF)], [state[0], cotangent[0], sea],
        scratch=[
            pltpu.VMEM((FIELDS, CELLS), BF), pltpu.VMEM((FIELDS, CELLS), BF), pltpu.VMEM((1, CELLS), jnp.int32),
            pltpu.SemaphoreType.DMA((3,)),
        ],
        far=(0, 1, 2),
    )[0]
    line = lax.all_to_all(packed, LINE_AXES, 0, 0).reshape(2, ROW, 2 * FIELDS, CELLS)

    turns, out_turned = turn_table.T, out_gates[0].T
    first_turned, mid_turned = first_gates[0].T, mid_gates[0].T
    early, middle = call(
        prepare_early_kernel, [sds((BANK_ONE, HID), BF), sds((BANK_MID, HID), BF)],
        [turns, first_turned, out_turned, first_kernel[0], out_kernel[0].T, mid_turned, mid_kernel[0]],
        scratch=[
            pltpu.SMEM((4, TILES), jnp.int32), pltpu.VMEM((64, 9 * DEPTH), jnp.int32),
            pltpu.VMEM((4, 9 * HID), jnp.int32), pltpu.VMEM((9 * DEPTH, HID), BF),
            pltpu.VMEM((FIELDS, 9 * HID), BF), pltpu.VMEM((64, 9 * HID), jnp.int32),
            pltpu.VMEM((9 * HID, HID), BF), pltpu.SemaphoreType.DMA((7,)),
        ],
        far=(0, 1, 2, 3, 4, 5, 6), flops=5 * 10**9,
    )

    field, grad_cells, strips_zero = call(
        start_kernel,
        [sds((LINE, PADC), BF), sds((LINE, PADC), BF), sds((256, PADC), BF)], [line, early],
    )
    prev_zero = row_shift(strips_zero[UP], 1)
    next_zero = row_shift(strips_zero[DOWN], -1)
    two = call(
        prepare_late_kernel, [sds((BANK_TWO, HID), BF)], [middle, first_turned, out_turned],
        scratch=[
            pltpu.VMEM((64, 9 * DEPTH), jnp.int32), pltpu.VMEM((4, 9 * HID), jnp.int32),
            pltpu.SemaphoreType.DMA((2,)),
        ],
        far=(1, 2), flops=10**9,
    )[0]
    exchange = [sds((192, HID), BF), sds((160, HID), BF), sds((160, HID), BF), sds((LINE, HID), F32)]
    filled_zero, act_one, hid_one, local_one, up_one, down_one, inner_two = call(
        layer_one_kernel,
        [sds((ROW, TS + 2, TS, PADC), BF), sds((LINE, HID), F32), sds((LINE, HID), BF)] + exchange,
        [field, strips_zero, prev_zero, next_zero, grad_cells, early],
    )
    prev_one = row_shift(up_one, 1)
    next_one = row_shift(down_one, -1)

    three, slope_one, pick_mid, pick_out, pick_first = call(
        prepare_last_kernel, [sds((BANK_THREE, HID), BF), sds((LINE, HID), F32), sds((16 * CHUNK, 1152), BF), sds((16 * CHUNK, 1152), BF),
         sds((4 * SHARE, 3 * PADC), BF)],
        [early, middle, first_turned, out_turned, act_one], flops=10**9,
    )

    filled_one, grad_two, hid_two, local_two, up_two, down_two, inner_one = call(
        layer_two_kernel,
        [sds((ROW, TS + 2, TS, 3 * HID), BF), sds((LINE, HID), BF), sds((LINE, HID), BF)] + exchange,
        [hid_one, local_one, prev_one, next_one, inner_two, early, middle, two],
        scratch=[pltpu.VMEM((TS + 2, TS, 3 * HID), BF)],
    )
    prev_two = row_shift(up_two, 1)
    next_two = row_shift(down_two, -1)

    part = call(
        mid_term_kernel,
        [sds((32 * CHUNK, PADC), F32)],
        [filled_one, grad_two, middle, pick_mid],
        scratch=[pltpu.VMEM((PADC, 9 * HID), BF)], flops=2 * 10**9,
    )[0]

    buffer, mine_two, grad_one = call(
        terms_kernel,
        [sds((ROWS, CHUNK + SHARE, PADC), BF), sds((TS + 2, TS, 3 * HID), BF), sds((LINE, HID), BF)],
        [hid_two, local_two, prev_two, next_two, inner_one, slope_one, filled_zero, grad_cells, early, two,
         part, pick_out, pick_first],
        scratch=[
            pltpu.VMEM((ROW, TS + 2, TS, 3 * HID), BF), pltpu.VMEM((PADC, 9 * HID), BF),
            pltpu.VMEM((PADC, 3 * PADC), BF), pltpu.SemaphoreType.DMA,
        ],
        far_out=(1,),
    )
    spread = lax.all_to_all(buffer, ROW_AXES, 0, 0)

    estimate, dx_own, up_three, down_three, local_three = call(
        last_kernel,
        [sds((FIELDS, CELLS), BF), sds((CELLS, PADC), F32), sds((80, PADC), BF), sds((80, PADC), BF),
         sds((96, PADC), BF)],
        [mine_two, grad_one, early, state[0], sea],
        scratch=[
            pltpu.VMEM((TS + 2, TS, 3 * HID), BF), pltpu.VMEM((LINE, PADC), F32),
            pltpu.VMEM((9 * HID, HID), BF),
        ],
        flops=2 * 10**9,
    )
    prev_three = row_shift(up_three, 1)
    next_three = row_shift(down_three, -1)

    shared, summed = call(sum_kernel, [sds((16, SHARE, PADC), BF), sds((CHUNK, PADC), F32)], [spread])
    opened = lax.all_to_all(shared, ("y", "xh", "core"), 0, 0).reshape(16 * SHARE, PADC)

    own, send, central, closing = call(
        finish_kernel,
        [sds((FIELDS, CELLS), F32), sds((COUPLED, CELLS), F32), sds((1, 18 * HID), F32), sds((1, 18 * FIELDS), F32)],
        [dx_own, next_three, prev_three, local_three, three, cotangent[0], summed],
    )
    returned = lax.ppermute(send, "comp", [(0, 1), (1, 0)])
    adjoint = own + jnp.pad(returned, ((0, FIELDS - COUPLED), (0, 0)))
    opening = call(opening_kernel, [sds((9 * DEPTH, HID), F32)], [opened, three])[0]
    return estimate[None], adjoint[None], opening[None], central, closing


def solution(mesh):
    fine = Mesh(mesh.devices.reshape(2, 4, 8, 2, 2), ("comp",) + FACE)
    whole = P("comp", None, None)
    in_specs = (P("comp", None, FACE), P("comp", None, FACE), P(FACE), P()) + (whole,) * 6
    out_specs = (P("comp", None, FACE), P("comp", None, FACE), whole, P("comp", FACE), P("comp", FACE))

    return jax.shard_map(body, mesh=fine, in_specs=in_specs, out_specs=out_specs, check_vma=False)
```
